32 devices in a mesh: grp: 4 (over x, core), blk: 8 (over z, y).
Axes of the slice: x: 2, y: 2, z: 4, core: 2. Of those that a mesh axis runs over, the one named last changes fastest.
Arguments:
- masses: bfloat16 [8, 2, 256, 256], P('blk'), may hold values from -3 to 3
- spins: int32 [8, 256], P('blk'), may hold values from 0 to 1
- shift_table: int32 [32, 256], P('blk'), may hold values from 0 to 255, as said below
- flip_table: int32 [32, 256], P('blk'), may hold values from 0 to 255, as said below
- ph_in: float32 [2, 32, 256, 256], P(None, 'blk', 'grp'), may hold values from -6 to 6
- pp_in: float32 [2, 32, 256, 256], P(None, 'blk', 'grp'), may hold values from -6 to 6
Outputs:
- ph_out: float32 [2, 32, 256, 256], P(None, 'blk', 'grp')
- pp_out: float32 [2, 32, 256, 256], P(None, 'blk', 'grp')
The draws below stay inside these ranges and needn't reach their ends.
Inputs may be any that keep to these rules, and one draw needn't show every extreme that they name: Row t of shift_table maps w * 16 + k to ((w + n_t) mod 16) * 16 + (k + q_t) mod 16 for some integers n_t, q_t of the transfer; every row is a permutation. Row t of flip_table maps w * 16 + k to ((n_t - w - 1) mod 16) * 16 + (q_t - k) mod 16 with the same n_t, q_t as shift_table's row t.
All inputs are finite; a program needn't handle non-finite values.
Results may differ from the reference program's by a relative error of at most 0.0064.
Values may be sent and summed in bfloat16 or wider, within the bound.
A program may use at most 128 MiB of HBM per device.

```python
import math
import jax
import jax.numpy as jnp
from jax import lax

NW = 16
NK = 16
ORDER = 256
WALK_DEV = 1
TR_DEV = 4
WALKERS = 8
TRANS = 32
SHIFTS = 7
N_BLK = 8


def table_moves(key):
    momentum_move = jax.random.randint(jax.random.fold_in(key, 71), (TRANS,), 0, NK)
    frequency_move = jax.random.randint(jax.random.fold_in(key, 72), (TRANS,), 0, NW)
    return (momentum_move, frequency_move)


def draw_shift_table(key, part):
    momentum_move, frequency_move = table_moves(key)
    index = jnp.arange(NW * NK, dtype=jnp.int32)
    frequency = index // NK
    momentum = index % NK
    result = (frequency[None, :] + frequency_move[:, None]) % NW * NK + (momentum[None, :] + momentum_move[:, None]) % NK
    return result.astype(jnp.int32)


def draw_flip_table(key, part):
    momentum_move, frequency_move = table_moves(key)
    index = jnp.arange(NW * NK, dtype=jnp.int32)
    frequency = index // NK
    momentum = index % NK
    result = (frequency_move[:, None] - frequency[None, :] - 1) % NW * NK + (momentum_move[:, None] - momentum[None, :]) % NK
    return result.astype(jnp.int32)


def plant(values, own_key, smallest, top_value):
    extent = values.shape
    spot = [jax.random.randint(jax.random.fold_in(own_key, axis), (), 0, extent[axis]) for axis in range(len(extent))]
    values = values.at[tuple(spot)].set(smallest)
    longest = extent.index(max(extent))
    spot[longest] = (spot[longest] + 1) % extent[longest]
    return values.at[tuple(spot)].set(top_value)


def steps_of(key, shape, cuts, least, largest):
    level, own = 1.0, jax.random.fold_in(key, 6)
    for position, blocks in cuts:
        draws = jnp.exp(jax.random.uniform(jax.random.fold_in(own, position), (blocks,), jnp.float32, least / len(cuts), largest / len(cuts)))
        level = level * jnp.repeat(draws, shape[position] // blocks).reshape([-1 if axis == position else 1 for axis in range(len(shape))])
    return level


def noise(rng, extent, width, bound, cuts=(), kind=jnp.bfloat16):
    array = width * jax.random.normal(rng, extent, jnp.float32)
    if cuts:
        array = array * steps_of(rng, extent, cuts, -0.22, 0.18)
    return jnp.clip(array, -bound, bound).astype(kind)


def setup_inputs(seed: int = 0) -> dict:
    key_of = jax.random.split(jax.random.key(seed), 7)
    return {
        "masses": noise(key_of[0], (WALKERS, 2, ORDER, ORDER), 0.5, 3.0, ((0, 8),)),
        "spins": plant(jax.random.randint(key_of[1], (WALKERS, ORDER), 0, 2), jax.random.fold_in(key_of[1], 1), 0, 1).astype(jnp.int32),
        "shift_table": draw_shift_table(jax.random.fold_in(key_of[6], 71), 0),
        "flip_table": draw_flip_table(jax.random.fold_in(key_of[6], 71), 0),
        "ph_in": noise(key_of[4], (2, TRANS, ORDER, ORDER), 1.0, 6.0, ((1, 8), (2, 4)), jnp.float32),
        "pp_in": noise(key_of[5], (2, TRANS, ORDER, ORDER), 1.0, 6.0, ((1, 8), (2, 4)), jnp.float32),
    }


COUPLING = 0.5

def dft_tables():
    index = jnp.arange(NW * NK, dtype=jnp.int32)
    frequency = index // NK
    momentum = index % NK
    numerator = ((2 * frequency[:, None] + 1) * frequency[None, :] * NK - 2 * momentum[:, None] * momentum[None, :] * NW) % (2 * NW * NK)
    phase = numerator.astype(jnp.float32) * (math.pi / (NW * NK))
    norm_scale = 1.0 / math.sqrt(NW * NK)
    return ((jnp.cos(phase) * norm_scale).astype(jnp.bfloat16), (jnp.sin(phase) * norm_scale).astype(jnp.bfloat16))

def build(masses, spins, real_table, imag_table):
    signed = (2 * spins - 1).astype(jnp.float32)
    factors = jnp.stack([jnp.exp(COUPLING * signed), jnp.exp(-COUPLING * signed)], 1)
    scaled = (masses.astype(jnp.float32) * factors[:, :, None, :]).astype(jnp.bfloat16).astype(jnp.float32)
    first_real = jnp.einsum('ri,wsij->wsrj', real_table.astype(jnp.float32), scaled).astype(jnp.bfloat16)
    first_imag = jnp.einsum('ri,wsij->wsrj', imag_table.astype(jnp.float32), scaled).astype(jnp.bfloat16)
    joined = jnp.concatenate([first_real, first_imag], -1).astype(jnp.float32)
    big_table = jnp.concatenate([jnp.concatenate([real_table.T, -imag_table.T], 1), jnp.concatenate([imag_table.T, real_table.T], 1)], 0).astype(jnp.float32)
    second = jnp.einsum('wsri,ij->wsrj', joined, big_table)
    order = real_table.shape[1]
    return jnp.stack([second[..., :order], second[..., order:]], 2).astype(jnp.bfloat16)

def reference(masses, spins, shift_table, flip_table, ph_in, pp_in):
    real_table, imag_table = dft_tables()
    propagator = build(masses, spins, real_table, imag_table)

    def one_block(block, totals):
        ph_total, pp_total = totals
        homes = (block - jnp.arange(SHIFTS + 1, dtype=jnp.int32)) % N_BLK
        walker_ids = (homes[:, None] * WALK_DEV + jnp.arange(WALK_DEV, dtype=jnp.int32)[None, :]).reshape(-1)
        props = propagator[walker_ids].astype(jnp.float32)
        begin = (block * TR_DEV).astype(jnp.int32)
        shifts = lax.dynamic_slice_in_dim(shift_table, begin, TR_DEV, 0)
        flips = lax.dynamic_slice_in_dim(flip_table, begin, TR_DEV, 0)
        mirrored = jnp.swapaxes(props, 3, 4)[:, :, :, None]
        moved = props[:, :, :, shifts[:, :, None], shifts[:, None, :]]
        ph_real = lax.optimization_barrier(jnp.sum(mirrored[:, :, 0] * moved[:, :, 0] - mirrored[:, :, 1] * moved[:, :, 1], axis=(0, 1)))
        ph_imag = lax.optimization_barrier(jnp.sum(mirrored[:, :, 0] * moved[:, :, 1] + mirrored[:, :, 1] * moved[:, :, 0], axis=(0, 1)))
        upper = props[:, 0][:, :, None]
        lowered = props[:, 1][:, :, flips[:, :, None], flips[:, None, :]]
        pp_real = lax.optimization_barrier(jnp.sum(upper[:, 0] * lowered[:, 0] - upper[:, 1] * lowered[:, 1], axis=0))
        pp_imag = lax.optimization_barrier(jnp.sum(upper[:, 0] * lowered[:, 1] + upper[:, 1] * lowered[:, 0], axis=0))
        ph_old = lax.dynamic_slice_in_dim(ph_total, begin, TR_DEV, 1)
        pp_old = lax.dynamic_slice_in_dim(pp_total, begin, TR_DEV, 1)
        ph_total = lax.dynamic_update_slice_in_dim(ph_total, ph_old + jnp.stack([ph_real, ph_imag]), begin, 1)
        pp_total = lax.dynamic_update_slice_in_dim(pp_total, pp_old + jnp.stack([pp_real, pp_imag]), begin, 1)
        return (ph_total, pp_total)
    ph_out, pp_out = lax.fori_loop(0, N_BLK, one_block, (ph_in, pp_in))
    return (ph_out, pp_out)
```

```python
import functools
import math

import jax
import jax.numpy as jnp
from jax import lax
from jax.experimental import pallas as pl
from jax.experimental.pallas import tpu as pltpu
from jax.sharding import PartitionSpec as P

NW = 16
NK = 16
COUPLING = 0.5
MESH = pl.DeviceIdType.MESH
NT = (((1,), (1,)), ((), ()))


def angle(steps):
    return steps.astype(jnp.float32) * (math.pi / NW)


def base_steps(row, col):
    return ((2 * (row // NK) + 1) * (col // NK) - 2 * (row % NK) * (col % NK)) % (2 * NW)


def move_steps(freq, mom, col):
    return (2 * freq * (col // NK) - 2 * mom * (col % NK)) % (2 * NW)


def whole_gather(blocks, groups, reach):
    return blocks == 8 and groups == 4 and reach == 7


def send(src, dst, send_sem, recv_sem, target):
    return pltpu.make_async_remote_copy(
        src_ref=src,
        dst_ref=dst,
        send_sem=send_sem,
        recv_sem=recv_sem,
        device_id=target,
        device_id_type=MESH,
    )


def bulk(view, sem):
    return pltpu.make_async_copy(view, view, sem)


class Gather:
    TURNS = ("", "O0 O1 H0 I0", "H1 h0 F0", "F1 i0 I1", "h1 f0", "f1 i1", "", "")
    SLOTS = "SOHFIhfi"

    def __init__(self, group, block, order, walkers, masses, spins, held, held_spins, recv, sends):
        self.chip, self.core = group // 2, group % 2
        self.block, self.layer, self.side = block, block // 2, block % 2
        self.masses, self.spins = masses, spins
        self.held, self.held_spins = held, held_spins
        self.recv, self.sends = recv, sends
        self.quarter = order // 4
        self.walkers = walkers
        self.end = jnp.logical_or(self.layer == 0, self.layer == 3)
        other = self.chip * 2 + (1 - self.core)
        self.other = other
        self.partner = (other, block)
        self.across = ((1 - self.chip) * 2 + (1 - self.core), block)
        self.beside = (other, self.layer * 2 + (1 - self.side))
        same, mate = self.side, 1 - self.side
        first, second = self.by_layer(1, 3, 0, 2), self.by_layer(2, 2, 1, 1)
        full = self.by_layer(3, 0, 3, 0)
        self.slots = {
            "S": block,
            "O": self.layer * 2 + mate,
            "H": first * 2 + same,
            "I": second * 2 + same,
            "F": full * 2 + same,
            "h": first * 2 + mate,
            "i": second * 2 + mate,
            "f": full * 2 + mate,
        }

    def by_layer(self, *values):
        return sum(
            value * (self.layer == i).astype(jnp.int32) for i, value in enumerate(values)
        )

    def slot_at(self, k):
        return sum(
            self.slots[kind] * (k == i).astype(jnp.int32) for i, kind in enumerate(self.SLOTS)
        )

    def up(self, layer):
        return (self.other, layer * 2 + self.side)

    def others(self):
        return [(self.other, lax.rem(self.block + step, 8)) for step in range(1, 8)]

    def greet(self):
        self.barrier = pltpu.get_barrier_semaphore()
        targets = self.others() + [self.partner, self.across]
        for target in targets:
            pl.semaphore_signal(self.barrier, inc=1, device_id=target, device_id_type=MESH)

    def enter(self):
        pl.semaphore_wait(self.barrier, 9)

    def rows(self, ref, half, parity):
        first = pl.multiple_of((half * 2 + parity) * self.quarter, self.quarter)
        return ref.at[:, :, pl.ds(first, self.quarter)]

    def own(self, part, target):
        half = 1 - self.chip if part else self.chip
        dst = self.rows(self.held.at[self.block], half, 1 - self.core)
        src = self.rows(self.masses, half, 1 - self.core)
        send(src, dst, self.sends.at[0], self.recv.at[self.block, part], target).start()

    def note(self, target):
        return send(self.spins, self.held_spins.at[self.block], self.sends.at[3],
                    self.sends.at[4], target)

    def begin(self):
        for target in self.others():
            self.note(target).start()
        ends = self.by_layer(1, 0, 0, 2), self.by_layer(3, 0, 0, 0)
        inner = self.by_layer(2, 2, 1, 1)
        near_end, far_end = self.by_layer(0, 0, 3, 0), self.by_layer(0, 3, 0, 0)

        @pl.when(self.end)
        def _():
            self.own(0, self.beside)
            self.own(1, self.beside)
            self.own(0, self.up(inner))
            for layer in ends:
                self.own(0, self.up(layer))
                self.own(1, self.up(layer))

        @pl.when(jnp.logical_not(self.end))
        def _():
            self.own(0, self.up(near_end))
            self.own(0, self.up(far_end))
            self.own(0, self.beside)
            self.own(1, self.beside)
            self.own(0, self.up(inner))

    def parity(self, kind, part):
        moved = kind in "fi" if part == 0 else kind in "HIf"
        if kind == "h":
            moved = part == 0
        return 1 - self.core if moved else self.core

    def event(self, kind, part):
        slot = self.slots[kind]
        half = 1 - self.chip if part else self.chip
        view = self.rows(self.held.at[slot], half, self.parity(kind, part))

        def copy(sem, recv, target):
            return send(view, view, self.sends.at[sem], self.recv.at[slot, recv], target)

        copy(1, part, self.partner).wait_recv()
        if kind == "F" or (kind in "HI" and part == 0):
            copy(1, part, self.beside).start()
        if kind in "HIhi" and part == 0:
            copy(1, 1, self.across).start()
        copy(2, 2, self.partner).start()

    def some(self, count):
        return self.held.at[0:count, :, :, 0 : self.quarter]

    def turn(self, k):
        for i, turn in enumerate(self.TURNS):
            if turn:
                @pl.when(k == i)
                def _():
                    for name in turn.split():
                        self.event(name[0], int(name[1]))

        @pl.when(k == 1)
        def _():
            bulk(self.held_spins.at[0:7], self.sends.at[4]).wait()

        @pl.when(k >= 1)
        def _():
            half = self.held.at[0, :, :, 0 : 2 * self.quarter]
            bulk(half, self.recv.at[self.slot_at(k), 2]).wait()

    def drain(self):
        pl.when(self.end)(lambda: bulk(self.some(7), self.sends.at[0]).wait())
        pl.when(jnp.logical_not(self.end))(lambda: bulk(self.some(5), self.sends.at[0]).wait())
        bulk(self.some(8), self.sends.at[1]).wait()
        bulk(self.held.at[0:7, :, :, 0 : 2 * self.quarter], self.sends.at[2]).wait()
        bulk(self.held_spins.at[0:7], self.sends.at[3]).wait()


class Chain:
    def __init__(self, group, block, groups, blocks, reach, height, masses, spins, held,
                 held_spins, recv, sends):
        self.group, self.block = group, block
        self.blocks, self.reach, self.height = blocks, reach, height
        self.groups, self.chips = groups, groups // 2
        self.chip, self.core = group // 2, group % 2
        self.partner = self.chip * 2 + (1 - self.core)
        self.masses, self.spins = masses, spins
        self.held, self.held_spins = held, held_spins
        self.recv, self.sends = recv, sends

    def slot_at(self, k):
        return k

    def far(self, step):
        return lax.rem(self.chip + step, self.chips) * 2 + self.core

    def rows(self, ref, piece):
        first = pl.multiple_of(piece * self.height, self.height)
        return ref.at[:, :, pl.ds(first, self.height)]

    def greet(self):
        self.barrier = pltpu.get_barrier_semaphore()
        blocks = [
            lax.rem(self.block - offset + self.blocks, self.blocks)
            for offset in range(1, self.reach + 1)
        ]
        targets = [(self.group, block) for block in blocks] + [(self.partner, self.block)]
        targets += [(self.far(step), self.block) for step in range(1, self.chips)]
        for target in targets:
            pl.semaphore_signal(self.barrier, inc=1, device_id=target, device_id_type=MESH)

    def enter(self):
        pl.semaphore_wait(self.barrier, self.reach + self.chips)

    def direct(self, offset):
        target = (self.group, lax.rem(self.block + offset, self.blocks))
        return (
            send(
                self.rows(self.masses, self.group),
                self.rows(self.held.at[offset], self.group),
                self.sends.at[offset, 0], self.recv.at[offset, self.group], target,
            ),
            send(
                self.spins, self.held_spins.at[offset],
                self.sends.at[offset, 1], self.recv.at[offset, self.groups], target,
            ),
        )

    def passed(self, offset, piece, target, sem):
        view = self.rows(self.held.at[offset], piece)
        return send(view, view, self.sends.at[offset, sem], self.recv.at[offset, piece],
                    (target, self.block))

    def to_core(self, offset):
        return self.passed(offset, self.group, self.partner, 2)

    def to_far(self, offset, step):
        return self.passed(offset, self.group, self.far(step), 1 + 2 * step)

    def relay(self, offset, step):
        return self.passed(offset, self.far(step), self.partner, 2 + 2 * step)

    def arrival(self, offset, piece):
        return self.passed(offset, piece, self.partner, 2)

    def begin(self):
        for offset in range(1, self.reach + 1):
            for copy in self.direct(offset):
                copy.start()

    def take(self, k):
        self.arrival(k, self.group).wait_recv()
        for step in range(1, self.chips):
            self.to_far(k, step).start()
        self.to_core(k).start()

    def turn(self, k):
        pl.when(k == 0)(lambda: self.take(1))
        pl.when(jnp.logical_and(k >= 1, k < self.reach))(lambda: self.take(k + 1))

        @pl.when(k >= 1)
        def _():
            for step in range(1, self.chips):
                self.arrival(k, self.far(step)).wait_recv()
                self.relay(k, step).start()
            self.arrival(k, self.partner).wait_recv()
            for step in range(1, self.chips):
                piece = lax.rem(self.chip + step, self.chips) * 2 + (1 - self.core)
                self.arrival(k, piece).wait_recv()
            self.direct(k)[1].wait_recv()

    def drain(self):
        for offset in range(1, self.reach + 1):
            for copy in self.direct(offset):
                copy.wait_send()
            self.to_core(offset).wait_send()
            for step in range(1, self.chips):
                self.to_far(offset, step).wait_send()
                self.relay(offset, step).wait_send()

def kernel(
    blocks, groups, reach, shift_ref, masses_ref, spins_ref, ph_ref, pp_ref, ph_out, pp_out,
    held, held_spins, col_table, sh_cols, fl_cols, band, sh_rows, fl_rows,
    x_ph, x_pp, fixed, recv_sem, send_sem, local_sem,
):
    group = lax.axis_index("grp")
    block = lax.axis_index("blk")
    order = held.shape[-1]
    walkers = held.shape[1]
    trans = ph_out.shape[1]
    height = order // groups
    chips = groups // 2
    chip, core = group // 2, group % 2
    partner = chip * 2 + (1 - core)
    f32, bf16 = jnp.float32, jnp.bfloat16
    gather = whole_gather(blocks, groups, reach)
    home = block if gather else 0

    local = [
        pltpu.make_async_copy(masses_ref, held.at[home], local_sem.at[0]),
        pltpu.make_async_copy(spins_ref, held_spins.at[home], local_sem.at[1]),
        pltpu.make_async_copy(ph_ref, ph_out, local_sem.at[2]),
        pltpu.make_async_copy(pp_ref, pp_out, local_sem.at[3]),
    ]
    if gather:
        plan = Gather(
            group, block, order, walkers, masses_ref, spins_ref, held, held_spins,
            recv_sem, send_sem,
        )
    else:
        plan = Chain(
            group, block, groups, blocks, reach, height, masses_ref, spins_ref, held,
            held_spins, recv_sem, send_sem,
        )
    plan.greet()
    for copy in local:
        copy.start()
    plan.enter()
    plan.begin()

    norm = 1.0 / math.sqrt(NW * NK)
    index_col = lax.broadcasted_iota(jnp.int32, (order, 128), 0)
    lane = lax.broadcasted_iota(jnp.int32, (order, 128), 1)
    freq = jnp.zeros((order, 128), jnp.int32)
    mom = jnp.zeros((order, 128), jnp.int32)
    for t in range(trans):
        start = shift_ref[t, 0]
        freq = jnp.where(lane == t, start // NK, freq)
        mom = jnp.where(lane == t, start % NK, mom)
    move = angle(move_steps(freq, mom, index_col))
    move_cos, move_sin = jnp.cos(move), jnp.sin(move)

    def put_cols(ref, t, real, imag):
        where = (slice(None),) if t is None else (t, slice(None))
        real, imag = (real * norm).astype(bf16), (imag * norm).astype(bf16)
        ref[where[:-1] + (slice(0, order), slice(0, order))] = real
        ref[where[:-1] + (slice(0, order), slice(order, 2 * order))] = -imag
        ref[where[:-1] + (slice(order, 2 * order), slice(0, order))] = imag
        ref[where[:-1] + (slice(order, 2 * order), slice(order, 2 * order))] = real

    site = lax.broadcasted_iota(jnp.int32, (order, order), 0)
    momentum = lax.broadcasted_iota(jnp.int32, (order, order), 1)
    phase = angle(base_steps(momentum, site))
    cos, sin = jnp.cos(phase), jnp.sin(phase)
    put_cols(col_table, None, cos, sin)
    for t in range(trans):
        mc, ms = move_cos[:, t : t + 1], move_sin[:, t : t + 1]
        cc, ss, sc, cs = mc * cos, ms * sin, ms * cos, mc * sin
        put_cols(sh_cols, t, cc - ss, sc + cs)
        put_cols(fl_cols, t, cc + ss, sc - cs)

    row = lax.broadcasted_iota(jnp.int32, (height, order), 0) + group * height
    column = lax.broadcasted_iota(jnp.int32, (height, order), 1)
    phase = angle(base_steps(row, column))
    cos, sin = jnp.cos(phase), jnp.sin(phase)
    band[0:height, :] = (cos * norm).astype(bf16)
    band[height : 2 * height, :] = (sin * norm).astype(bf16)
    col8 = lax.broadcasted_iota(jnp.int32, (8, order), 1)
    for t in range(trans):
        start = shift_ref[t, 0]
        move = angle(move_steps(start // NK, start % NK, col8))
        mc, ms = jnp.cos(move)[0:1], jnp.sin(move)[0:1]
        cc, ss, sc, cs = mc * cos, ms * sin, ms * cos, mc * sin
        first = 2 * t * height
        sh_rows[first : first + height, :] = ((cc - ss) * norm).astype(bf16)
        sh_rows[first + height : first + 2 * height, :] = ((sc + cs) * norm).astype(bf16)
        fl_rows[first : first + height, :] = ((cc + ss) * norm).astype(bf16)
        fl_rows[first + height : first + 2 * height, :] = ((sc - cs) * norm).astype(bf16)

    def dot(a, b):
        return jnp.dot(a, b, preferred_element_type=f32)

    def absorb(slot):
        for w in range(walkers):
            place = pl.ds(pl.multiple_of((slot * walkers + w) * height, height), height)
            signed = (2 * held_spins[slot, w : w + 1, :] - 1).astype(f32)
            lefts = []
            for s in range(2):
                factor = jnp.exp((COUPLING if s == 0 else -COUPLING) * signed)
                scaled = (held[slot, w, s].astype(f32) * factor).astype(bf16)
                moved = dot(sh_rows[...], scaled).astype(bf16)
                for t in range(trans):
                    first = 2 * t * height
                    x_ph[t, s, place, 0:order] = moved[first : first + height]
                    x_ph[t, s, place, order:] = moved[first + height : first + 2 * height]
                if s == 1:
                    moved = dot(fl_rows[...], scaled).astype(bf16)
                    for t in range(trans):
                        first = 2 * t * height
                        x_pp[t, place, 0:order] = moved[first : first + height]
                        x_pp[t, place, order:] = moved[first + height : first + 2 * height]
                else:
                    upper = dot(band[...], scaled).astype(bf16)
                left = lax.dot_general(band[...], scaled, NT, preferred_element_type=f32)
                lefts.append(left.astype(bf16))
            lefts.append(upper)
            joined = jnp.concatenate(
                [jnp.concatenate([one[:height], one[height:]], 1) for one in lefts], 0
            )
            second = dot(joined, col_table[...])
            for part in range(3):
                fixed[part, place, :] = second[part * height : (part + 1) * height]

    @pl.loop(0, reach + 1)
    def _(k):
        @pl.when(k == 0)
        def _():
            local[0].wait()
            local[1].wait()

        plan.turn(k)
        absorb(plan.slot_at(k))

    local[2].wait()
    local[3].wait()
    length = (reach + 1) * walkers

    def product(left, right):
        for v in range(length):
            part = slice(v * height, (v + 1) * height)
            a, b = left[part, 0:order], left[part, order:]
            c, d = right[part, 0:order], right[part, order:]
            yield a, b, c, d

    @pl.loop(0, trans)
    def _(t):
        real, imag = ph_out[0, t], ph_out[1, t]
        for s in range(2):
            moved = dot(x_ph[t, s], sh_cols[t])
            for a, b, c, d in product(fixed[s], moved):
                real = real + (a * c + b * d)
                imag = imag + (a * d - b * c)
        ph_out[0, t] = real
        ph_out[1, t] = imag
        real, imag = pp_out[0, t], pp_out[1, t]
        lowered = dot(x_pp[t], fl_cols[t])
        for a, b, c, d in product(fixed[2], lowered):
            real = real + (a * c - b * d)
            imag = imag + (a * d + b * c)
        pp_out[0, t] = real
        pp_out[1, t] = imag

    plan.drain()


def on_device(masses, spins, shift_table, flip_table, ph_in, pp_in):
    groups = lax.axis_size("grp")
    blocks = lax.axis_size("blk")
    reach = min(8, blocks - 1)
    visits = reach + 1
    walkers, _, order, _ = masses.shape
    trans = shift_table.shape[0]
    height = order // groups
    chips = groups // 2
    f32, bf16 = jnp.float32, jnp.bfloat16
    dma = pltpu.SemaphoreType.DMA
    anywhere = pl.BlockSpec(memory_space=pl.ANY)
    if whole_gather(blocks, groups, reach):
        recv_shape, send_shape = (visits, 3), (5,)
    else:
        recv_shape, send_shape = (visits, groups + 1), (visits, 3 + 2 * (chips - 1))
    return pl.pallas_call(
        functools.partial(kernel, blocks, groups, reach),
        out_shape=(
            jax.ShapeDtypeStruct(ph_in.shape, f32),
            jax.ShapeDtypeStruct(pp_in.shape, f32),
        ),
        in_specs=[pl.BlockSpec(memory_space=pltpu.SMEM)] + [anywhere] * 4,
        out_specs=(pl.BlockSpec(memory_space=pltpu.VMEM),) * 2,
        scratch_shapes=[
            pltpu.VMEM((visits, walkers, 2, order, order), bf16),
            pltpu.VMEM((visits, walkers, order), jnp.int32),
            pltpu.VMEM((2 * order, 2 * order), bf16),
            pltpu.VMEM((trans, 2 * order, 2 * order), bf16),
            pltpu.VMEM((trans, 2 * order, 2 * order), bf16),
            pltpu.VMEM((2 * height, order), bf16),
            pltpu.VMEM((trans * 2 * height, order), bf16),
            pltpu.VMEM((trans * 2 * height, order), bf16),
            pltpu.VMEM((trans, 2, visits * walkers * height, 2 * order), bf16),
            pltpu.VMEM((trans, visits * walkers * height, 2 * order), bf16),
            pltpu.VMEM((3, visits * walkers * height, 2 * order), f32),
            dma(recv_shape),
            dma(send_shape),
            dma((4,)),
        ],
        compiler_params=pltpu.CompilerParams(
            collective_id=0, has_side_effects=True, vmem_limit_bytes=56 * 1024 * 1024
        ),
    )(shift_table, masses, spins, ph_in, pp_in)


def solution(mesh):
    placed = (
        P("blk", None, None, None),
        P("blk", None),
        P("blk", None),
        P("blk", None),
        P(None, "blk", "grp", None),
        P(None, "blk", "grp", None),
    )
    return jax.shard_map(
        on_device,
        mesh=mesh,
        in_specs=placed,
        out_specs=(P(None, "blk", "grp", None), P(None, "blk", "grp", None)),
        check_vma=False,
    )
```

```python
import functools
import math

import jax
import jax.numpy as jnp
from jax import lax
from jax.experimental import pallas as pl
from jax.experimental.pallas import tpu as pltpu
from jax.sharding import PartitionSpec as P

NW = 16
NK = 16
COUPLING = 0.5
VMEM = 67043328
MESH = pl.DeviceIdType.MESH
NT = (((1,), (1,)), ((), ()))


def angle(steps):
    return steps.astype(jnp.float32) * (math.pi / NW)


def base_steps(row, col):
    return ((2 * (row // NK) + 1) * (col // NK) - 2 * (row % NK) * (col % NK)) % (2 * NW)


def move_steps(freq, mom, col):
    return (2 * freq * (col // NK) - 2 * mom * (col % NK)) % (2 * NW)


def whole_gather(blocks, groups, reach):
    return blocks == 8 and groups == 4 and reach == 7


def send(src, dst, send_sem, recv_sem, target):
    return pltpu.make_async_remote_copy(
        src_ref=src,
        dst_ref=dst,
        send_sem=send_sem,
        recv_sem=recv_sem,
        device_id=target,
        device_id_type=MESH,
    )


def bulk(view, sem):
    return pltpu.make_async_copy(view, view, sem)


class Gather:
    TURNS = ("", "O0 O1 H0 I0", "H1 h0 F0", "F1 i0 I1", "h1 f0", "f1 i1", "", "")
    SLOTS = "SOHFIhfi"

    def __init__(self, group, block, order, walkers, masses, spins, held, held_spins, recv, sends):
        self.chip, self.core = group // 2, group % 2
        self.block, self.layer, self.side = block, block // 2, block % 2
        self.masses, self.spins = masses, spins
        self.held, self.held_spins = held, held_spins
        self.recv, self.sends = recv, sends
        self.quarter = order // 4
        self.walkers = walkers
        self.end = jnp.logical_or(self.layer == 0, self.layer == 3)
        other = self.chip * 2 + (1 - self.core)
        self.other = other
        self.partner = (other, block)
        self.across = ((1 - self.chip) * 2 + (1 - self.core), block)
        self.beside = (other, self.layer * 2 + (1 - self.side))
        same, mate = self.side, 1 - self.side
        first, second = self.by_layer(1, 3, 0, 2), self.by_layer(2, 2, 1, 1)
        full = self.by_layer(3, 0, 3, 0)
        self.slots = {
            "S": block,
            "O": self.layer * 2 + mate,
            "H": first * 2 + same,
            "I": second * 2 + same,
            "F": full * 2 + same,
            "h": first * 2 + mate,
            "i": second * 2 + mate,
            "f": full * 2 + mate,
        }

    def by_layer(self, *values):
        return sum(
            value * (self.layer == i).astype(jnp.int32) for i, value in enumerate(values)
        )

    def slot_at(self, k):
        return sum(
            self.slots[kind] * (k == i).astype(jnp.int32) for i, kind in enumerate(self.SLOTS)
        )

    def up(self, layer):
        return (self.other, layer * 2 + self.side)

    def others(self):
        return [(self.other, lax.rem(self.block + step, 8)) for step in range(1, 8)]

    def greet(self):
        self.barrier = pltpu.get_barrier_semaphore()
        targets = self.others() + [self.partner, self.across]
        for target in targets:
            pl.semaphore_signal(self.barrier, inc=1, device_id=target, device_id_type=MESH)

    def enter(self):
        pl.semaphore_wait(self.barrier, 9)

    def rows(self, ref, half, parity):
        first = pl.multiple_of((half * 2 + parity) * self.quarter, self.quarter)
        return ref.at[:, :, pl.ds(first, self.quarter)]

    def own(self, part, target):
        half = 1 - self.chip if part else self.chip
        dst = self.rows(self.held.at[self.block], half, 1 - self.core)
        src = self.rows(self.masses, half, 1 - self.core)
        send(src, dst, self.sends.at[0], self.recv.at[self.block, part], target).start()

    def note(self, target):
        return send(self.spins, self.held_spins.at[self.block], self.sends.at[3],
                    self.sends.at[4], target)

    def begin(self):
        for target in self.others():
            self.note(target).start()
        ends = self.by_layer(1, 0, 0, 2), self.by_layer(3, 0, 0, 0)
        inner = self.by_layer(2, 2, 1, 1)
        near_end, far_end = self.by_layer(0, 0, 3, 0), self.by_layer(0, 3, 0, 0)

        @pl.when(self.end)
        def _():
            self.own(0, self.beside)
            self.own(1, self.beside)
            self.own(0, self.up(inner))
            for layer in ends:
                self.own(0, self.up(layer))
                self.own(1, self.up(layer))

        @pl.when(jnp.logical_not(self.end))
        def _():
            self.own(0, self.up(near_end))
            self.own(0, self.up(far_end))
            self.own(0, self.beside)
            self.own(1, self.beside)
            self.own(0, self.up(inner))

    def parity(self, kind, part):
        moved = kind in "fi" if part == 0 else kind in "HIf"
        if kind == "h":
            moved = part == 0
        return 1 - self.core if moved else self.core

    def event(self, kind, part):
        slot = self.slots[kind]
        half = 1 - self.chip if part else self.chip
        view = self.rows(self.held.at[slot], half, self.parity(kind, part))

        def copy(sem, recv, target):
            return send(view, view, self.sends.at[sem], self.recv.at[slot, recv], target)

        copy(1, part, self.partner).wait_recv()
        if kind == "F" or (kind in "HI" and part == 0):
            copy(1, part, self.beside).start()
        if kind in "HIhi" and part == 0:
            copy(1, 1, self.across).start()
        copy(2, 2, self.partner).start()

    def some(self, count):
        return self.held.at[0:count, :, :, 0 : self.quarter]

    def turn(self, k):
        for i, turn in enumerate(self.TURNS):
            if turn:
                @pl.when(k == i)
                def _():
                    for name in turn.split():
                        self.event(name[0], int(name[1]))

        @pl.when(k == 1)
        def _():
            bulk(self.held_spins.at[0:7], self.sends.at[4]).wait()

        @pl.when(k >= 1)
        def _():
            half = self.held.at[0, :, :, 0 : 2 * self.quarter]
            bulk(half, self.recv.at[self.slot_at(k), 2]).wait()

    def drain(self):
        pl.when(self.end)(lambda: bulk(self.some(7), self.sends.at[0]).wait())
        pl.when(jnp.logical_not(self.end))(lambda: bulk(self.some(5), self.sends.at[0]).wait())
        bulk(self.some(8), self.sends.at[1]).wait()
        bulk(self.held.at[0:7, :, :, 0 : 2 * self.quarter], self.sends.at[2]).wait()
        bulk(self.held_spins.at[0:7], self.sends.at[3]).wait()


class Chain:
    def __init__(self, group, block, groups, blocks, reach, height, masses, spins, held,
                 held_spins, recv, sends):
        self.group, self.block = group, block
        self.blocks, self.reach, self.height = blocks, reach, height
        self.groups, self.chips = groups, groups // 2
        self.chip, self.core = group // 2, group % 2
        self.partner = self.chip * 2 + (1 - self.core)
        self.masses, self.spins = masses, spins
        self.held, self.held_spins = held, held_spins
        self.recv, self.sends = recv, sends

    def slot_at(self, k):
        return k

    def far(self, step):
        return lax.rem(self.chip + step, self.chips) * 2 + self.core

    def rows(self, ref, piece):
        first = pl.multiple_of(piece * self.height, self.height)
        return ref.at[:, :, pl.ds(first, self.height)]

    def greet(self):
        self.barrier = pltpu.get_barrier_semaphore()
        blocks = [
            lax.rem(self.block - offset + self.blocks, self.blocks)
            for offset in range(1, self.reach + 1)
        ]
        targets = [(self.group, block) for block in blocks] + [(self.partner, self.block)]
        targets += [(self.far(step), self.block) for step in range(1, self.chips)]
        for target in targets:
            pl.semaphore_signal(self.barrier, inc=1, device_id=target, device_id_type=MESH)

    def enter(self):
        pl.semaphore_wait(self.barrier, self.reach + self.chips)

    def direct(self, offset):
        target = (self.group, lax.rem(self.block + offset, self.blocks))
        return (
            send(
                self.rows(self.masses, self.group),
                self.rows(self.held.at[offset], self.group),
                self.sends.at[offset, 0], self.recv.at[offset, self.group], target,
            ),
            send(
                self.spins, self.held_spins.at[offset],
                self.sends.at[offset, 1], self.recv.at[offset, self.groups], target,
            ),
        )

    def passed(self, offset, piece, target, sem):
        view = self.rows(self.held.at[offset], piece)
        return send(view, view, self.sends.at[offset, sem], self.recv.at[offset, piece],
                    (target, self.block))

    def to_core(self, offset):
        return self.passed(offset, self.group, self.partner, 2)

    def to_far(self, offset, step):
        return self.passed(offset, self.group, self.far(step), 1 + 2 * step)

    def relay(self, offset, step):
        return self.passed(offset, self.far(step), self.partner, 2 + 2 * step)

    def arrival(self, offset, piece):
        return self.passed(offset, piece, self.partner, 2)

    def begin(self):
        for offset in range(1, self.reach + 1):
            for copy in self.direct(offset):
                copy.start()

    def take(self, k):
        self.arrival(k, self.group).wait_recv()
        for step in range(1, self.chips):
            self.to_far(k, step).start()
        self.to_core(k).start()

    def turn(self, k):
        pl.when(k == 0)(lambda: self.take(1))
        pl.when(jnp.logical_and(k >= 1, k < self.reach))(lambda: self.take(k + 1))

        @pl.when(k >= 1)
        def _():
            for step in range(1, self.chips):
                self.arrival(k, self.far(step)).wait_recv()
                self.relay(k, step).start()
            self.arrival(k, self.partner).wait_recv()
            for step in range(1, self.chips):
                piece = lax.rem(self.chip + step, self.chips) * 2 + (1 - self.core)
                self.arrival(k, piece).wait_recv()
            self.direct(k)[1].wait_recv()

    def drain(self):
        for offset in range(1, self.reach + 1):
            for copy in self.direct(offset):
                copy.wait_send()
            self.to_core(offset).wait_send()
            for step in range(1, self.chips):
                self.to_far(offset, step).wait_send()
                self.relay(offset, step).wait_send()

def kernel(
    blocks, groups, reach, shift_ref, masses_ref, spins_ref, ph_ref, pp_ref, ph_out, pp_out,
    held, held_spins, col_table, sh_cols, fl_cols, band, sh_rows, fl_rows,
    x_ph, x_pp, fixed, recv_sem, send_sem, local_sem,
):
    group = lax.axis_index("grp")
    block = lax.axis_index("blk")
    order = held.shape[-1]
    walkers = held.shape[1]
    trans = ph_out.shape[1]
    height = order // groups
    chips = groups // 2
    chip, core = group // 2, group % 2
    partner = chip * 2 + (1 - core)
    f32, bf16 = jnp.float32, jnp.bfloat16
    gather = whole_gather(blocks, groups, reach)
    home = block if gather else 0

    local = [
        pltpu.make_async_copy(masses_ref, held.at[home], local_sem.at[0]),
        pltpu.make_async_copy(spins_ref, held_spins.at[home], local_sem.at[1]),
        pltpu.make_async_copy(ph_ref, ph_out, local_sem.at[2]),
        pltpu.make_async_copy(pp_ref, pp_out, local_sem.at[3]),
    ]
    if gather:
        plan = Gather(
            group, block, order, walkers, masses_ref, spins_ref, held, held_spins,
            recv_sem, send_sem,
        )
    else:
        plan = Chain(
            group, block, groups, blocks, reach, height, masses_ref, spins_ref, held,
            held_spins, recv_sem, send_sem,
        )
    plan.greet()
    for copy in local:
        copy.start()
    plan.enter()
    plan.begin()

    norm = 1.0 / math.sqrt(NW * NK)
    index_col = lax.broadcasted_iota(jnp.int32, (order, 128), 0)
    lane = lax.broadcasted_iota(jnp.int32, (order, 128), 1)
    freq = jnp.zeros((order, 128), jnp.int32)
    mom = jnp.zeros((order, 128), jnp.int32)
    for t in range(trans):
        start = shift_ref[t, 0]
        freq = jnp.where(lane == t, start // NK, freq)
        mom = jnp.where(lane == t, start % NK, mom)
    move = angle(move_steps(freq, mom, index_col))
    move_cos, move_sin = jnp.cos(move), jnp.sin(move)

    def put_cols(ref, t, real, imag):
        where = (slice(None),) if t is None else (t, slice(None))
        real, imag = (real * norm).astype(bf16), (imag * norm).astype(bf16)
        ref[where[:-1] + (slice(0, order), slice(0, order))] = real
        ref[where[:-1] + (slice(0, order), slice(order, 2 * order))] = -imag
        ref[where[:-1] + (slice(order, 2 * order), slice(0, order))] = imag
        ref[where[:-1] + (slice(order, 2 * order), slice(order, 2 * order))] = real

    site = lax.broadcasted_iota(jnp.int32, (order, order), 0)
    momentum = lax.broadcasted_iota(jnp.int32, (order, order), 1)
    phase = angle(base_steps(momentum, site))
    cos, sin = jnp.cos(phase), jnp.sin(phase)
    put_cols(col_table, None, cos, sin)
    for t in range(trans):
        mc, ms = move_cos[:, t : t + 1], move_sin[:, t : t + 1]
        cc, ss, sc, cs = mc * cos, ms * sin, ms * cos, mc * sin
        put_cols(sh_cols, t, cc - ss, sc + cs)
        put_cols(fl_cols, t, cc + ss, sc - cs)

    row = lax.broadcasted_iota(jnp.int32, (height, order), 0) + group * height
    column = lax.broadcasted_iota(jnp.int32, (height, order), 1)
    phase = angle(base_steps(row, column))
    cos, sin = jnp.cos(phase), jnp.sin(phase)
    band[0:height, :] = (cos * norm).astype(bf16)
    band[height : 2 * height, :] = (sin * norm).astype(bf16)
    col8 = lax.broadcasted_iota(jnp.int32, (8, order), 1)
    for t in range(trans):
        start = shift_ref[t, 0]
        move = angle(move_steps(start // NK, start % NK, col8))
        mc, ms = jnp.cos(move)[0:1], jnp.sin(move)[0:1]
        cc, ss, sc, cs = mc * cos, ms * sin, ms * cos, mc * sin
        first = 2 * t * height
        sh_rows[first : first + height, :] = ((cc - ss) * norm).astype(bf16)
        sh_rows[first + height : first + 2 * height, :] = ((sc + cs) * norm).astype(bf16)
        fl_rows[first : first + height, :] = ((cc + ss) * norm).astype(bf16)
        fl_rows[first + height : first + 2 * height, :] = ((sc - cs) * norm).astype(bf16)

    def dot(a, b):
        return jnp.dot(a, b, preferred_element_type=f32)

    def absorb(slot):
        for w in range(walkers):
            place = pl.ds(pl.multiple_of((slot * walkers + w) * height, height), height)
            signed = (2 * held_spins[slot, w : w + 1, :] - 1).astype(f32)
            lefts = []
            for s in range(2):
                factor = jnp.exp((COUPLING if s == 0 else -COUPLING) * signed)
                scaled = (held[slot, w, s].astype(f32) * factor).astype(bf16)
                moved = dot(sh_rows[...], scaled).astype(bf16)
                for t in range(trans):
                    first = 2 * t * height
                    x_ph[t, s, place, 0:order] = moved[first : first + height]
                    x_ph[t, s, place, order:] = moved[first + height : first + 2 * height]
                if s == 1:
                    moved = dot(fl_rows[...], scaled).astype(bf16)
                    for t in range(trans):
                        first = 2 * t * height
                        x_pp[t, place, 0:order] = moved[first : first + height]
                        x_pp[t, place, order:] = moved[first + height : first + 2 * height]
                else:
                    upper = dot(band[...], scaled).astype(bf16)
                left = lax.dot_general(band[...], scaled, NT, preferred_element_type=f32)
                lefts.append(left.astype(bf16))
            lefts.append(upper)
            joined = jnp.concatenate(
                [jnp.concatenate([one[:height], one[height:]], 1) for one in lefts], 0
            )
            second = dot(joined, col_table[...])
            for part in range(3):
                fixed[part, place, :] = second[part * height : (part + 1) * height]

    @pl.loop(0, reach + 1)
    def _(k):
        @pl.when(k == 0)
        def _():
            local[0].wait()
            local[1].wait()

        plan.turn(k)
        absorb(plan.slot_at(k))

    local[2].wait()
    local[3].wait()
    length = (reach + 1) * walkers

    def product(left, right):
        for v in range(length):
            part = slice(v * height, (v + 1) * height)
            a, b = left[part, 0:order], left[part, order:]
            c, d = right[part, 0:order], right[part, order:]
            yield a, b, c, d

    @pl.loop(0, trans)
    def _(t):
        real, imag = ph_out[0, t], ph_out[1, t]
        for s in range(2):
            moved = dot(x_ph[t, s], sh_cols[t])
            for a, b, c, d in product(fixed[s], moved):
                real = real + (a * c + b * d)
                imag = imag + (a * d - b * c)
        ph_out[0, t] = real
        ph_out[1, t] = imag
        real, imag = pp_out[0, t], pp_out[1, t]
        lowered = dot(x_pp[t], fl_cols[t])
        for a, b, c, d in product(fixed[2], lowered):
            real = real + (a * c - b * d)
            imag = imag + (a * d + b * c)
        pp_out[0, t] = real
        pp_out[1, t] = imag

    plan.drain()


def leave(ph_sum, pp_sum, ph_out, pp_out, sem):
    copies = [
        pltpu.make_async_copy(ph_sum, ph_out, sem.at[0]),
        pltpu.make_async_copy(pp_sum, pp_out, sem.at[1]),
    ]
    for copy in copies:
        copy.start()
    for copy in copies:
        copy.wait()


def on_device(masses, spins, shift_table, flip_table, ph_in, pp_in):
    groups = lax.axis_size("grp")
    blocks = lax.axis_size("blk")
    reach = min(8, blocks - 1)
    visits = reach + 1
    walkers, _, order, _ = masses.shape
    trans = shift_table.shape[0]
    height = order // groups
    chips = groups // 2
    f32, bf16 = jnp.float32, jnp.bfloat16
    dma = pltpu.SemaphoreType.DMA
    anywhere = pl.BlockSpec(memory_space=pl.ANY)
    if whole_gather(blocks, groups, reach):
        recv_shape, send_shape = (visits, 3), (5,)
    else:
        recv_shape, send_shape = (visits, groups + 1), (visits, 3 + 2 * (chips - 1))
    sums = pl.pallas_call(
        functools.partial(kernel, blocks, groups, reach),
        out_shape=(pltpu.VMEM(ph_in.shape, f32), pltpu.VMEM(pp_in.shape, f32)),
        in_specs=[pl.BlockSpec(memory_space=pltpu.SMEM)]
        + [pl.BlockSpec(memory_space=pltpu.HBM)] * 4,
        out_specs=(pl.BlockSpec(memory_space=pltpu.VMEM),) * 2,
        scratch_shapes=[
            pltpu.VMEM((visits, walkers, 2, order, order), bf16),
            pltpu.VMEM((visits, walkers, order), jnp.int32),
            pltpu.VMEM((2 * order, 2 * order), bf16),
            pltpu.VMEM((trans, 2 * order, 2 * order), bf16),
            pltpu.VMEM((trans, 2 * order, 2 * order), bf16),
            pltpu.VMEM((2 * height, order), bf16),
            pltpu.VMEM((trans * 2 * height, order), bf16),
            pltpu.VMEM((trans * 2 * height, order), bf16),
            pltpu.VMEM((trans, 2, visits * walkers * height, 2 * order), bf16),
            pltpu.VMEM((trans, visits * walkers * height, 2 * order), bf16),
            pltpu.VMEM((3, visits * walkers * height, 2 * order), f32),
            dma(recv_shape),
            dma(send_shape),
            dma((4,)),
        ],
        compiler_params=pltpu.CompilerParams(
            collective_id=0, has_side_effects=True, vmem_limit_bytes=VMEM - 4 * (ph_in.size + pp_in.size) - 65536
        ),
    )(shift_table, masses, spins, ph_in, pp_in)
    return pl.pallas_call(
        leave,
        out_shape=(
            jax.ShapeDtypeStruct(ph_in.shape, f32),
            jax.ShapeDtypeStruct(pp_in.shape, f32),
        ),
        in_specs=[pl.BlockSpec(memory_space=pltpu.VMEM)] * 2,
        out_specs=(anywhere,) * 2,
        scratch_shapes=[dma((2,))],
    )(*[pltpu.with_memory_space_constraint(one, pltpu.VMEM) for one in sums])


def solution(mesh):
    placed = (
        P("blk", None, None, None),
        P("blk", None),
        P("blk", None),
        P("blk", None),
        P(None, "blk", "grp", None),
        P(None, "blk", "grp", None),
    )
    return jax.shard_map(
        on_device,
        mesh=mesh,
        in_specs=placed,
        out_specs=(P(None, "blk", "grp", None), P(None, "blk", "grp", None)),
        check_vma=False,
    )
```

```python
import functools
import math

import jax
import jax.numpy as jnp
from jax import lax
from jax.experimental import pallas as pl
from jax.experimental.pallas import tpu as pltpu
from jax.sharding import PartitionSpec as P

NW = 16
NK = 16
COUPLING = 0.5
VMEM = 67043328
LANES = 128
MESH = pl.DeviceIdType.MESH
NT = (((1,), (1,)), ((), ()))


def angle(steps):
    return steps.astype(jnp.float32) * (math.pi / NW)


def base_steps(row, col):
    return ((2 * (row // NK) + 1) * (col // NK) - 2 * (row % NK) * (col % NK)) % (2 * NW)


def whole_gather(blocks, groups, reach):
    return blocks == 8 and groups == 4 and reach == 7


def send(src, dst, send_sem, recv_sem, target):
    return pltpu.make_async_remote_copy(
        src_ref=src,
        dst_ref=dst,
        send_sem=send_sem,
        recv_sem=recv_sem,
        device_id=target,
        device_id_type=MESH,
    )


def bulk(view, sem):
    return pltpu.make_async_copy(view, view, sem)


class Gather:
    TURNS = ("", "O0 O1 H0 I0", "H1 h0 F0", "F1 i0 I1", "h1 f0", "f1 i1", "", "")
    SLOTS = "SOHFIhfi"

    def __init__(self, group, block, order, walkers, masses, spins, held, held_spins, recv, sends):
        self.chip, self.core = group // 2, group % 2
        self.block, self.layer, self.side = block, block // 2, block % 2
        self.masses, self.spins = masses, spins
        self.held, self.held_spins = held, held_spins
        self.recv, self.sends = recv, sends
        self.quarter = order // 4
        self.walkers = walkers
        self.end = jnp.logical_or(self.layer == 0, self.layer == 3)
        other = self.chip * 2 + (1 - self.core)
        self.other = other
        self.partner = (other, block)
        self.across = ((1 - self.chip) * 2 + (1 - self.core), block)
        self.beside = (other, self.layer * 2 + (1 - self.side))
        same, mate = self.side, 1 - self.side
        first, second = self.by_layer(1, 3, 0, 2), self.by_layer(2, 2, 1, 1)
        full = self.by_layer(3, 0, 3, 0)
        self.slots = {
            "S": block,
            "O": self.layer * 2 + mate,
            "H": first * 2 + same,
            "I": second * 2 + same,
            "F": full * 2 + same,
            "h": first * 2 + mate,
            "i": second * 2 + mate,
            "f": full * 2 + mate,
        }

    def by_layer(self, *values):
        return sum(
            value * (self.layer == i).astype(jnp.int32) for i, value in enumerate(values)
        )

    def slot_at(self, k):
        return sum(
            self.slots[kind] * (k == i).astype(jnp.int32) for i, kind in enumerate(self.SLOTS)
        )

    def up(self, layer):
        return (self.other, layer * 2 + self.side)

    def others(self):
        return [(self.other, lax.rem(self.block + step, 8)) for step in range(1, 8)]

    def greet(self):
        self.barrier = pltpu.get_barrier_semaphore()
        targets = self.others() + [self.partner, self.across]
        for target in targets:
            pl.semaphore_signal(self.barrier, inc=1, device_id=target, device_id_type=MESH)

    def enter(self):
        pl.semaphore_wait(self.barrier, 9)

    def rows(self, ref, half, parity):
        first = pl.multiple_of((half * 2 + parity) * self.quarter, self.quarter)
        return ref.at[:, :, pl.ds(first, self.quarter)]

    def own(self, part, target):
        half = 1 - self.chip if part else self.chip
        dst = self.rows(self.held.at[self.block], half, 1 - self.core)
        src = self.rows(self.masses, half, 1 - self.core)
        send(src, dst, self.sends.at[0], self.recv.at[self.block, part], target).start()

    def note(self, target):
        return send(self.spins, self.held_spins.at[self.block], self.sends.at[3],
                    self.sends.at[4], target)

    def begin(self):
        for target in self.others():
            self.note(target).start()
        ends = self.by_layer(1, 0, 0, 2), self.by_layer(3, 0, 0, 0)
        inner = self.by_layer(2, 2, 1, 1)
        near_end, far_end = self.by_layer(0, 0, 3, 0), self.by_layer(0, 3, 0, 0)

        @pl.when(self.end)
        def _():
            self.own(0, self.beside)
            self.own(1, self.beside)
            self.own(0, self.up(inner))
            for layer in ends:
                self.own(0, self.up(layer))
                self.own(1, self.up(layer))

        @pl.when(jnp.logical_not(self.end))
        def _():
            self.own(0, self.up(near_end))
            self.own(0, self.up(far_end))
            self.own(0, self.beside)
            self.own(1, self.beside)
            self.own(0, self.up(inner))

    def parity(self, kind, part):
        moved = kind in "fi" if part == 0 else kind in "HIf"
        if kind == "h":
            moved = part == 0
        return 1 - self.core if moved else self.core

    def event(self, kind, part):
        slot = self.slots[kind]
        half = 1 - self.chip if part else self.chip
        view = self.rows(self.held.at[slot], half, self.parity(kind, part))

        def copy(sem, recv, target):
            return send(view, view, self.sends.at[sem], self.recv.at[slot, recv], target)

        copy(1, part, self.partner).wait_recv()
        if kind == "F" or (kind in "HI" and part == 0):
            copy(1, part, self.beside).start()
        if kind in "HIhi" and part == 0:
            copy(1, 1, self.across).start()
        copy(2, 2, self.partner).start()

    def some(self, count):
        return self.held.at[0:count, :, :, 0 : self.quarter]

    def turn(self, k):
        for i, turn in enumerate(self.TURNS):
            if turn:
                @pl.when(k == i)
                def _():
                    for name in turn.split():
                        self.event(name[0], int(name[1]))

        @pl.when(k == 1)
        def _():
            bulk(self.held_spins.at[0:7], self.sends.at[4]).wait()

        @pl.when(k >= 1)
        def _():
            half = self.held.at[0, :, :, 0 : 2 * self.quarter]
            bulk(half, self.recv.at[self.slot_at(k), 2]).wait()

    def drain(self):
        pl.when(self.end)(lambda: bulk(self.some(7), self.sends.at[0]).wait())
        pl.when(jnp.logical_not(self.end))(lambda: bulk(self.some(5), self.sends.at[0]).wait())
        bulk(self.some(8), self.sends.at[1]).wait()
        bulk(self.held.at[0:7, :, :, 0 : 2 * self.quarter], self.sends.at[2]).wait()
        bulk(self.held_spins.at[0:7], self.sends.at[3]).wait()


class Chain:
    def __init__(self, group, block, groups, blocks, reach, height, masses, spins, held,
                 held_spins, recv, sends):
        self.group, self.block = group, block
        self.blocks, self.reach, self.height = blocks, reach, height
        self.groups, self.chips = groups, groups // 2
        self.chip, self.core = group // 2, group % 2
        self.partner = self.chip * 2 + (1 - self.core)
        self.masses, self.spins = masses, spins
        self.held, self.held_spins = held, held_spins
        self.recv, self.sends = recv, sends

    def slot_at(self, k):
        return k

    def far(self, step):
        return lax.rem(self.chip + step, self.chips) * 2 + self.core

    def rows(self, ref, piece):
        first = pl.multiple_of(piece * self.height, self.height)
        return ref.at[:, :, pl.ds(first, self.height)]

    def greet(self):
        self.barrier = pltpu.get_barrier_semaphore()
        blocks = [
            lax.rem(self.block - offset + self.blocks, self.blocks)
            for offset in range(1, self.reach + 1)
        ]
        targets = [(self.group, block) for block in blocks] + [(self.partner, self.block)]
        targets += [(self.far(step), self.block) for step in range(1, self.chips)]
        for target in targets:
            pl.semaphore_signal(self.barrier, inc=1, device_id=target, device_id_type=MESH)

    def enter(self):
        pl.semaphore_wait(self.barrier, self.reach + self.chips)

    def direct(self, offset):
        target = (self.group, lax.rem(self.block + offset, self.blocks))
        return (
            send(
                self.rows(self.masses, self.group),
                self.rows(self.held.at[offset], self.group),
                self.sends.at[offset, 0], self.recv.at[offset, self.group], target,
            ),
            send(
                self.spins, self.held_spins.at[offset],
                self.sends.at[offset, 1], self.recv.at[offset, self.groups], target,
            ),
        )

    def passed(self, offset, piece, target, sem):
        view = self.rows(self.held.at[offset], piece)
        return send(view, view, self.sends.at[offset, sem], self.recv.at[offset, piece],
                    (target, self.block))

    def to_core(self, offset):
        return self.passed(offset, self.group, self.partner, 2)

    def to_far(self, offset, step):
        return self.passed(offset, self.group, self.far(step), 1 + 2 * step)

    def relay(self, offset, step):
        return self.passed(offset, self.far(step), self.partner, 2 + 2 * step)

    def arrival(self, offset, piece):
        return self.passed(offset, piece, self.partner, 2)

    def begin(self):
        for offset in range(1, self.reach + 1):
            for copy in self.direct(offset):
                copy.start()

    def take(self, k):
        self.arrival(k, self.group).wait_recv()
        for step in range(1, self.chips):
            self.to_far(k, step).start()
        self.to_core(k).start()

    def turn(self, k):
        pl.when(k == 0)(lambda: self.take(1))
        pl.when(jnp.logical_and(k >= 1, k < self.reach))(lambda: self.take(k + 1))

        @pl.when(k >= 1)
        def _():
            for step in range(1, self.chips):
                self.arrival(k, self.far(step)).wait_recv()
                self.relay(k, step).start()
            self.arrival(k, self.partner).wait_recv()
            for step in range(1, self.chips):
                piece = lax.rem(self.chip + step, self.chips) * 2 + (1 - self.core)
                self.arrival(k, piece).wait_recv()
            self.direct(k)[1].wait_recv()

    def drain(self):
        for offset in range(1, self.reach + 1):
            for copy in self.direct(offset):
                copy.wait_send()
            self.to_core(offset).wait_send()
            for step in range(1, self.chips):
                self.to_far(offset, step).wait_send()
                self.relay(offset, step).wait_send()

def kernel(
    blocks, groups, reach, shift_ref, masses_ref, spins_ref, ph_ref, pp_ref,
    sums, ph_keep, pp_keep, held, held_spins, steps, band, unit, skew, props, fixed,
    recv_sem, send_sem, local_sem,
):
    group = lax.axis_index("grp")
    block = lax.axis_index("blk")
    order = held.shape[-1]
    walkers = held.shape[1]
    trans = sums.shape[0]
    height = order // groups
    lanes = sums.shape[-1]
    f32, bf16 = jnp.float32, jnp.bfloat16
    gather = whole_gather(blocks, groups, reach)
    home = block if gather else 0

    local = [
        pltpu.make_async_copy(masses_ref, held.at[home], local_sem.at[0]),
        pltpu.make_async_copy(spins_ref, held_spins.at[home], local_sem.at[1]),
        pltpu.make_async_copy(ph_ref, ph_keep, local_sem.at[2]),
        pltpu.make_async_copy(pp_ref, pp_keep, local_sem.at[3]),
    ]
    if gather:
        plan = Gather(
            group, block, order, walkers, masses_ref, spins_ref, held, held_spins,
            recv_sem, send_sem,
        )
    else:
        plan = Chain(
            group, block, groups, blocks, reach, height, masses_ref, spins_ref, held,
            held_spins, recv_sem, send_sem,
        )
    plan.greet()
    for copy in local:
        copy.start()
    plan.enter()
    plan.begin()

    norm = 1.0 / math.sqrt(NW * NK)
    row = lax.broadcasted_iota(jnp.int32, (order, order), 0)
    column = lax.broadcasted_iota(jnp.int32, (order, order), 1)
    phase = angle(base_steps(row, column))
    cos, sin = jnp.cos(phase), jnp.sin(phase)
    unit[0], unit[1] = cos, sin
    steps[0:order] = (cos * norm).astype(bf16)
    steps[order:] = (sin * norm).astype(bf16)
    mine = pl.ds(pl.multiple_of(group * height, height), height)
    band[0:height] = (unit[0, mine] * norm).astype(bf16)
    band[height:] = (unit[1, mine] * norm).astype(bf16)
    start = angle(lax.broadcasted_iota(jnp.int32, (8, order), 1) // NK)
    start_cos, start_sin = jnp.cos(start)[0:1], jnp.sin(start)[0:1]
    even = ((cos * start_cos + sin * start_sin) * norm).astype(bf16)
    odd = ((sin * start_cos - cos * start_sin) * norm).astype(bf16)
    skew[0:order, 0:order] = even
    skew[0:order, order:] = -odd
    skew[order:, 0:order] = odd
    skew[order:, order:] = even
    sums[...] = jnp.zeros(sums.shape, f32)

    def dot(a, b):
        return jnp.dot(a, b, preferred_element_type=f32)

    def absorb(slot, w):
        signed = (2 * held_spins[slot, w : w + 1, :] - 1).astype(f32)
        for s in range(2):
            factor = jnp.exp((COUPLING if s == 0 else -COUPLING) * signed)
            scaled = (held[slot, w, s].astype(f32) * factor).astype(bf16)
            first = dot(steps[...], scaled)
            real, imag = first[:order], first[order:]
            turned = jnp.concatenate(
                [real * unit[0] + imag * unit[1], imag * unit[0] - real * unit[1]], 1
            ).astype(bf16)
            left = lax.dot_general(band[...], scaled, NT, preferred_element_type=f32)
            real, imag = left[:height], left[height:]
            mine_cos, mine_sin = unit[0, mine], unit[1, mine]
            back = jnp.concatenate(
                [mine_cos * real + mine_sin * imag, mine_cos * imag - mine_sin * real], 1
            ).astype(bf16)
            moving = dot(turned, skew[...])
            kept = dot(back, skew[...])
            for part in range(2):
                for half in range(order // lanes):
                    here = slice(part * order + half * lanes, part * order + (half + 1) * lanes)
                    fixed[s, part, half] = kept[:, here]
                    tile = moving[:, here].reshape(NW, NK, lanes)
                    props[s, part, half, :, 0:NK] = tile
                    props[s, part, half, :, NK:] = tile

        @pl.loop(0, trans)
        def _(t):
            freq, mom = shift_ref[t, 0] // NK, shift_ref[t, 0] % NK
            ahead, behind = pl.ds(mom, NK), pl.ds(lax.rem(NK - mom, NK), NK)
            for i in range(height // NK):
                place = slice(i * NK, (i + 1) * NK)
                at = group * (height // NK) + i
                up, down = lax.rem(at + freq, NW), lax.rem(at - freq + NW, NW)
                for half in range(order // lanes):
                    real, imag = sums[t, 0, half, place], sums[t, 1, half, place]
                    for s in range(2):
                        a, b = fixed[s, 0, half, place], fixed[s, 1, half, place]
                        c, d = props[s, 0, half, up, ahead], props[s, 1, half, up, ahead]
                        real = real + (a * c + b * d)
                        imag = imag + (a * d - b * c)
                    sums[t, 0, half, place] = real
                    sums[t, 1, half, place] = imag
                    a, b = props[0, 0, half, at, 0:NK], props[0, 1, half, at, 0:NK]
                    c, d = props[1, 0, half, down, behind], props[1, 1, half, down, behind]
                    sums[t, 2, half, place] += a * c + b * d
                    sums[t, 3, half, place] += b * c - a * d

    @pl.loop(0, reach + 1)
    def _(k):
        @pl.when(k == 0)
        def _():
            local[0].wait()
            local[1].wait()

        plan.turn(k)
        for w in range(walkers):
            absorb(plan.slot_at(k), w)

    local[2].wait()
    local[3].wait()
    plan.drain()


def leave(groups, sums, ph_keep, pp_keep, ph_out, pp_out, ph_new, pp_new, sem):
    trans, _, _, height, lanes = sums.shape
    group = lax.axis_index("grp")
    row = lax.broadcasted_iota(jnp.int32, (height, lanes), 0)
    lane = lax.broadcasted_iota(jnp.int32, (height, lanes), 1)
    freq = (lane // NK - group * (height // NK) - row // NK + 2 * NW) % NW
    mom = (lane % NK - row % NK + NK) % NK
    source = freq * NK + mom
    index, upper = source % lanes, source >= lanes
    copies = []
    for t in range(trans):
        for keep, new, first in ((ph_keep, ph_new, 0), (pp_keep, pp_new, 2)):
            for part in range(2):
                low, high = [
                    jnp.take_along_axis(sums[t, first + part, half], index, 1) for half in range(2)
                ]
                new[part, t, :, 0:lanes] = keep[part, t, :, 0:lanes] + jnp.where(upper, high, low)
                new[part, t, :, lanes:] = keep[part, t, :, lanes:] + jnp.where(upper, low, high)
        for i, (new, out) in enumerate(((ph_new, ph_out), (pp_new, pp_out))):
            copies.append(pltpu.make_async_copy(new.at[:, t], out.at[:, t], sem.at[t, i]))
            copies[-1].start()
    for copy in copies:
        copy.wait()


def on_device(masses, spins, shift_table, flip_table, ph_in, pp_in):
    groups = lax.axis_size("grp")
    blocks = lax.axis_size("blk")
    reach = min(8, blocks - 1)
    visits = reach + 1
    walkers, _, order, _ = masses.shape
    trans = shift_table.shape[0]
    height = order // groups
    chips = groups // 2
    f32, bf16 = jnp.float32, jnp.bfloat16
    sums_shape = (trans, 4, order // LANES, height, LANES)
    dma = pltpu.SemaphoreType.DMA
    anywhere = pl.BlockSpec(memory_space=pl.ANY)
    if whole_gather(blocks, groups, reach):
        recv_shape, send_shape = (visits, 3), (5,)
    else:
        recv_shape, send_shape = (visits, groups + 1), (visits, 3 + 2 * (chips - 1))
    sums = pl.pallas_call(
        functools.partial(kernel, blocks, groups, reach),
        out_shape=(
            pltpu.VMEM(sums_shape, f32),
            pltpu.VMEM(ph_in.shape, f32),
            pltpu.VMEM(pp_in.shape, f32),
        ),
        in_specs=[pl.BlockSpec(memory_space=pltpu.SMEM)]
        + [pl.BlockSpec(memory_space=pltpu.HBM)] * 4,
        out_specs=(pl.BlockSpec(memory_space=pltpu.VMEM),) * 3,
        scratch_shapes=[
            pltpu.VMEM((visits, walkers, 2, order, order), bf16),
            pltpu.VMEM((visits, walkers, order), jnp.int32),
            pltpu.VMEM((2 * order, order), bf16),
            pltpu.VMEM((2 * height, order), bf16),
            pltpu.VMEM((2, order, order), f32),
            pltpu.VMEM((2 * order, 2 * order), bf16),
            pltpu.VMEM((2, 2, order // LANES, NW, 2 * NK, LANES), f32),
            pltpu.VMEM((2, 2, order // LANES, height, LANES), f32),
            dma(recv_shape),
            dma(send_shape),
            dma((4,)),
        ],
        compiler_params=pltpu.CompilerParams(
            collective_id=0, has_side_effects=True, vmem_limit_bytes=VMEM - 8 * (ph_in.size + pp_in.size) - 65536
        ),
    )(shift_table, masses, spins, ph_in, pp_in)
    return pl.pallas_call(
        functools.partial(leave, groups),
        out_shape=(
            jax.ShapeDtypeStruct(ph_in.shape, f32),
            jax.ShapeDtypeStruct(pp_in.shape, f32),
        ),
        in_specs=[pl.BlockSpec(memory_space=pltpu.VMEM)] * 3,
        out_specs=(anywhere,) * 2,
        scratch_shapes=[
            pltpu.VMEM(ph_in.shape, f32),
            pltpu.VMEM(pp_in.shape, f32),
            dma((trans, 2)),
        ],
        compiler_params=pltpu.CompilerParams(vmem_limit_bytes=16 * 1024 * 1024),
    )(*[pltpu.with_memory_space_constraint(one, pltpu.VMEM) for one in sums])


def solution(mesh):
    placed = (
        P("blk", None, None, None),
        P("blk", None),
        P("blk", None),
        P("blk", None),
        P(None, "blk", "grp", None),
        P(None, "blk", "grp", None),
    )
    return jax.shard_map(
        on_device,
        mesh=mesh,
        in_specs=placed,
        out_specs=(P(None, "blk", "grp", None), P(None, "blk", "grp", None)),
        check_vma=False,
    )
```

```python
import functools
import math

import jax
import jax.numpy as jnp
from jax import lax
from jax.experimental import pallas as pl
from jax.experimental.pallas import tpu as pltpu
from jax.sharding import PartitionSpec as P

NW = 16
NK = 16
COUPLING = 0.5
VMEM = 67043328
LANES = 128
ROWS = 8
MESH = pl.DeviceIdType.MESH
NT = (((1,), (1,)), ((), ()))


def angle(steps):
    return steps.astype(jnp.float32) * (math.pi / NW)


def whole_gather(blocks, groups, reach):
    return blocks == 8 and groups == 4 and reach == 7


def send(src, dst, send_sem, recv_sem, target):
    return pltpu.make_async_remote_copy(
        src_ref=src,
        dst_ref=dst,
        send_sem=send_sem,
        recv_sem=recv_sem,
        device_id=target,
        device_id_type=MESH,
    )


def bulk(view, sem):
    return pltpu.make_async_copy(view, view, sem)


class Gather:
    TURNS = ("", "O0 O1 H0 I0", "H1 h0 F0", "F1 i0 I1", "", "h1 f0 f1 i1", "", "")
    SLOTS = "SOHFIhfi"

    def __init__(self, group, block, order, walkers, masses, spins, held, held_spins, recv, sends):
        self.chip, self.core = group // 2, group % 2
        self.block, self.layer, self.side = block, block // 2, block % 2
        self.masses, self.spins = masses, spins
        self.held, self.held_spins = held, held_spins
        self.recv, self.sends = recv, sends
        self.quarter = order // 4
        self.walkers = walkers
        self.end = jnp.logical_or(self.layer == 0, self.layer == 3)
        other = self.chip * 2 + (1 - self.core)
        self.other = other
        self.partner = (other, block)
        self.across = ((1 - self.chip) * 2 + (1 - self.core), block)
        self.beside = (other, self.layer * 2 + (1 - self.side))
        same, mate = self.side, 1 - self.side
        first, second = self.by_layer(1, 3, 0, 2), self.by_layer(2, 2, 1, 1)
        full = self.by_layer(3, 0, 3, 0)
        self.slots = {
            "S": block,
            "O": self.layer * 2 + mate,
            "H": first * 2 + same,
            "I": second * 2 + same,
            "F": full * 2 + same,
            "h": first * 2 + mate,
            "i": second * 2 + mate,
            "f": full * 2 + mate,
        }

    def by_layer(self, *values):
        return sum(
            value * (self.layer == i).astype(jnp.int32) for i, value in enumerate(values)
        )

    def slot_at(self, k):
        return sum(
            self.slots[kind] * (k == i).astype(jnp.int32) for i, kind in enumerate(self.SLOTS)
        )

    def up(self, layer):
        return (self.other, layer * 2 + self.side)

    def others(self):
        return [(self.other, lax.rem(self.block + step, 8)) for step in range(1, 8)]

    def greet(self):
        self.barrier = pltpu.get_barrier_semaphore()
        targets = self.others() + [self.partner, self.across]
        for target in targets:
            pl.semaphore_signal(self.barrier, inc=1, device_id=target, device_id_type=MESH)

    def enter(self):
        pl.semaphore_wait(self.barrier, 9)

    def rows(self, ref, half, parity):
        first = pl.multiple_of((half * 2 + parity) * self.quarter, self.quarter)
        return ref.at[:, :, pl.ds(first, self.quarter)]

    def own(self, part, target):
        half = 1 - self.chip if part else self.chip
        dst = self.rows(self.held.at[self.block], half, 1 - self.core)
        src = self.rows(self.masses, half, 1 - self.core)
        send(src, dst, self.sends.at[0], self.recv.at[self.block, part], target).start()

    def note(self, target):
        return send(self.spins, self.held_spins.at[self.block], self.sends.at[3],
                    self.sends.at[4], target)

    def begin(self):
        for target in self.others():
            self.note(target).start()
        ends = self.by_layer(1, 0, 0, 2), self.by_layer(3, 0, 0, 0)
        inner = self.by_layer(2, 2, 1, 1)
        near_end, far_end = self.by_layer(0, 0, 3, 0), self.by_layer(0, 3, 0, 0)

        @pl.when(self.end)
        def _():
            self.own(0, self.beside)
            self.own(1, self.beside)
            self.own(0, self.up(inner))
            for layer in ends:
                self.own(0, self.up(layer))
                self.own(1, self.up(layer))

        @pl.when(jnp.logical_not(self.end))
        def _():
            self.own(0, self.up(near_end))
            self.own(0, self.up(far_end))
            self.own(0, self.beside)
            self.own(1, self.beside)
            self.own(0, self.up(inner))

    def parity(self, kind, part):
        moved = kind in "fi" if part == 0 else kind in "HIf"
        if kind == "h":
            moved = part == 0
        return 1 - self.core if moved else self.core

    def event(self, kind, part):
        slot = self.slots[kind]
        half = 1 - self.chip if part else self.chip
        view = self.rows(self.held.at[slot], half, self.parity(kind, part))

        def copy(sem, recv, target):
            return send(view, view, self.sends.at[sem], self.recv.at[slot, recv], target)

        copy(1, part, self.partner).wait_recv()
        if kind == "F" or (kind in "HI" and part == 0):
            copy(1, part, self.beside).start()
        if kind in "HIhi" and part == 0:
            copy(1, 1, self.across).start()
        copy(2, 2, self.partner).start()

    def some(self, count):
        return self.held.at[0:count, :, :, 0 : self.quarter]

    def turn(self, k):
        for i, turn in enumerate(self.TURNS):
            if turn:
                @pl.when(k == i)
                def _():
                    for name in turn.split():
                        self.event(name[0], int(name[1]))

        @pl.when(k == 1)
        def _():
            bulk(self.held_spins.at[0:7], self.sends.at[4]).wait()

        @pl.when(k >= 1)
        def _():
            half = self.held.at[0, :, :, 0 : 2 * self.quarter]
            bulk(half, self.recv.at[self.slot_at(k), 2]).wait()

    def drain(self):
        pl.when(self.end)(lambda: bulk(self.some(7), self.sends.at[0]).wait())
        pl.when(jnp.logical_not(self.end))(lambda: bulk(self.some(5), self.sends.at[0]).wait())
        bulk(self.some(8), self.sends.at[1]).wait()
        bulk(self.held.at[0:7, :, :, 0 : 2 * self.quarter], self.sends.at[2]).wait()
        bulk(self.held_spins.at[0:7], self.sends.at[3]).wait()


class Chain:
    def __init__(self, group, block, groups, blocks, reach, height, masses, spins, held,
                 held_spins, recv, sends):
        self.group, self.block = group, block
        self.blocks, self.reach, self.height = blocks, reach, height
        self.groups, self.chips = groups, groups // 2
        self.chip, self.core = group // 2, group % 2
        self.partner = self.chip * 2 + (1 - self.core)
        self.masses, self.spins = masses, spins
        self.held, self.held_spins = held, held_spins
        self.recv, self.sends = recv, sends

    def slot_at(self, k):
        return k

    def far(self, step):
        return lax.rem(self.chip + step, self.chips) * 2 + self.core

    def rows(self, ref, piece):
        first = pl.multiple_of(piece * self.height, self.height)
        return ref.at[:, :, pl.ds(first, self.height)]

    def greet(self):
        self.barrier = pltpu.get_barrier_semaphore()
        blocks = [
            lax.rem(self.block - offset + self.blocks, self.blocks)
            for offset in range(1, self.reach + 1)
        ]
        targets = [(self.group, block) for block in blocks] + [(self.partner, self.block)]
        targets += [(self.far(step), self.block) for step in range(1, self.chips)]
        for target in targets:
            pl.semaphore_signal(self.barrier, inc=1, device_id=target, device_id_type=MESH)

    def enter(self):
        pl.semaphore_wait(self.barrier, self.reach + self.chips)

    def direct(self, offset):
        target = (self.group, lax.rem(self.block + offset, self.blocks))
        return (
            send(
                self.rows(self.masses, self.group),
                self.rows(self.held.at[offset], self.group),
                self.sends.at[offset, 0], self.recv.at[offset, self.group], target,
            ),
            send(
                self.spins, self.held_spins.at[offset],
                self.sends.at[offset, 1], self.recv.at[offset, self.groups], target,
            ),
        )

    def passed(self, offset, piece, target, sem):
        view = self.rows(self.held.at[offset], piece)
        return send(view, view, self.sends.at[offset, sem], self.recv.at[offset, piece],
                    (target, self.block))

    def to_core(self, offset):
        return self.passed(offset, self.group, self.partner, 2)

    def to_far(self, offset, step):
        return self.passed(offset, self.group, self.far(step), 1 + 2 * step)

    def relay(self, offset, step):
        return self.passed(offset, self.far(step), self.partner, 2 + 2 * step)

    def arrival(self, offset, piece):
        return self.passed(offset, piece, self.partner, 2)

    def begin(self):
        for offset in range(1, self.reach + 1):
            for copy in self.direct(offset):
                copy.start()

    def take(self, k):
        self.arrival(k, self.group).wait_recv()
        for step in range(1, self.chips):
            self.to_far(k, step).start()
        self.to_core(k).start()

    def turn(self, k):
        pl.when(k == 0)(lambda: self.take(1))
        pl.when(jnp.logical_and(k >= 1, k < self.reach))(lambda: self.take(k + 1))

        @pl.when(k >= 1)
        def _():
            for step in range(1, self.chips):
                self.arrival(k, self.far(step)).wait_recv()
                self.relay(k, step).start()
            self.arrival(k, self.partner).wait_recv()
            for step in range(1, self.chips):
                piece = lax.rem(self.chip + step, self.chips) * 2 + (1 - self.core)
                self.arrival(k, piece).wait_recv()
            self.direct(k)[1].wait_recv()

    def drain(self):
        for offset in range(1, self.reach + 1):
            for copy in self.direct(offset):
                copy.wait_send()
            self.to_core(offset).wait_send()
            for step in range(1, self.chips):
                self.to_far(offset, step).wait_send()
                self.relay(offset, step).wait_send()

def kernel(
    blocks, groups, reach, shift_ref, masses_ref, spins_ref, ph_ref, pp_ref,
    sums, ph_keep, pp_keep, held, held_spins, steps, band, unit, skew, props, fixed,
    recv_sem, send_sem, local_sem,
):
    group = lax.axis_index("grp")
    block = lax.axis_index("blk")
    order = held.shape[-1]
    walkers = held.shape[1]
    trans = sums.shape[0]
    height = order // groups
    lanes = sums.shape[-1]
    f32, bf16 = jnp.float32, jnp.bfloat16
    gather = whole_gather(blocks, groups, reach)
    home = block if gather else 0

    local = [
        pltpu.make_async_copy(masses_ref, held.at[home], local_sem.at[0]),
        pltpu.make_async_copy(spins_ref, held_spins.at[home], local_sem.at[1]),
        pltpu.make_async_copy(ph_ref, ph_keep, local_sem.at[2]),
        pltpu.make_async_copy(pp_ref, pp_keep, local_sem.at[3]),
    ]
    if gather:
        plan = Gather(
            group, block, order, walkers, masses_ref, spins_ref, held, held_spins,
            recv_sem, send_sem,
        )
    else:
        plan = Chain(
            group, block, groups, blocks, reach, height, masses_ref, spins_ref, held,
            held_spins, recv_sem, send_sem,
        )
    plan.greet()
    for copy in local:
        copy.start()
    plan.enter()
    plan.begin()

    norm = 1.0 / math.sqrt(NW * NK)
    row = lax.broadcasted_iota(jnp.int32, (NW, order), 0)
    column = lax.broadcasted_iota(jnp.int32, (NW, order), 1)
    slices, sites = column // NK, column % NK

    def circle(numerator):
        turn = angle(numerator % (2 * NW))
        return jnp.cos(turn), jnp.sin(turn)

    site_cos, site_sin = circle(2 * NW * NK - 2 * row * sites)
    odd_cos, odd_sin = circle((2 * row + 1) * slices)
    even_cos, even_sin = circle(2 * row * slices)
    for i in range(NW):
        here = slice(i * NK, (i + 1) * NK)
        c, d = odd_cos[i : i + 1], odd_sin[i : i + 1]
        cos, sin = c * site_cos - d * site_sin, d * site_cos + c * site_sin
        unit[0, here], unit[1, here] = cos, sin
        if i < NW // 2:
            steps[here] = (cos * norm).astype(bf16)
            steps[order // 2 + i * NK : order // 2 + (i + 1) * NK] = (sin * norm).astype(bf16)
        c, d = even_cos[i : i + 1], even_sin[i : i + 1]
        skew[here, 0:order] = ((c * site_cos - d * site_sin) * norm).astype(bf16)
        skew[here, order:] = ((d * site_cos + c * site_sin) * norm).astype(bf16)
    mine = pl.ds(pl.multiple_of(group * height, height), height)
    band[0:height] = (unit[0, mine] * norm).astype(bf16)
    band[height:] = (unit[1, mine] * norm).astype(bf16)
    sums[...] = jnp.zeros(sums.shape, f32)

    def dot(a, b):
        return jnp.dot(a, b, preferred_element_type=f32)

    middle = order // 2
    flip = ROWS - 1 - lax.broadcasted_iota(jnp.int32, (ROWS, lanes), 0)

    def put(s, part, half, lower, upper):
        for i in range(NW // 2):
            tiles = [lower[i * NK + r : i * NK + r + ROWS] for r in range(0, NK, ROWS)]
            for r, tile in enumerate(tiles + tiles[:1]):
                props[s, part, half, i, r * ROWS : (r + 1) * ROWS] = tile
            tiles = [upper[i * NK + r : i * NK + r + ROWS] for r in range(0, NK, ROWS)]
            tiles = [jnp.take_along_axis(tile, flip, 0) for tile in tiles[::-1]]
            for r, tile in enumerate(tiles + tiles[:1]):
                props[s, part, half, NW - 1 - i, r * ROWS : (r + 1) * ROWS] = tile

    def from_row(freq, mom):
        mirrored = (freq >= NW // 2).astype(jnp.int32)
        return pl.ds(lax.rem(mom - mirrored + NK, NK), ROWS)

    def absorb(slot, w):
        signed = (2 * held_spins[slot, w : w + 1, :] - 1).astype(f32)
        turned, back = [], []
        for s in range(2):
            factor = jnp.exp((COUPLING if s == 0 else -COUPLING) * signed)
            scaled = (held[slot, w, s].astype(f32) * factor).astype(bf16)
            left = lax.dot_general(band[...], scaled, NT, preferred_element_type=f32)
            real, imag = left[:height], left[height:]
            cos, sin = unit[0, mine], unit[1, mine]
            back += [
                (cos * real + sin * imag).astype(bf16),
                (sin * real - cos * imag).astype(bf16),
            ]
            first = dot(steps[...], scaled)
            real, imag = first[:middle], first[middle:]
            cos, sin = unit[0, 0:middle], unit[1, 0:middle]
            turned += [
                (real * cos + imag * sin).astype(bf16),
                (imag * cos - real * sin).astype(bf16),
            ]
        moving = dot(jnp.concatenate(turned + back, 0), skew[...])
        for s in range(2):
            for half in range(order // lanes):
                even = slice(half * lanes, (half + 1) * lanes)
                odd = slice(order + half * lanes, order + (half + 1) * lanes)
                real = moving[s * order : s * order + middle]
                imag = moving[s * order + middle : (s + 1) * order]
                put(s, 0, half, real[:, even] + imag[:, odd], real[:, even] - imag[:, odd])
                put(s, 1, half, imag[:, even] - real[:, odd], -imag[:, even] - real[:, odd])
                first = 2 * order + 2 * s * height
                real = moving[first : first + height]
                imag = moving[first + height : first + 2 * height]
                fixed[s, 0, half] = real[:, even] - imag[:, odd]
                fixed[s, 1, half] = -real[:, odd] - imag[:, even]

        @pl.loop(0, trans)
        def _(t):
            freq, mom = shift_ref[t, 0] // NK, shift_ref[t, 0] % NK
            for i in range(height // NK):
                at = group * (height // NK) + i
                up, down = lax.rem(at + freq, NW), lax.rem(at - freq + NW, NW)
                for piece in range(NK // ROWS):
                    rows = i * NK + piece * ROWS
                    place = slice(rows, rows + ROWS)
                    offset = piece * ROWS
                    ahead = from_row(up, mom + offset)
                    behind = from_row(down, NK - mom + offset)
                    own = from_row(at, offset)
                    for half in range(order // lanes):
                        real, imag = sums[t, 0, half, place], sums[t, 1, half, place]
                        for s in range(2):
                            a, b = fixed[s, 0, half, place], fixed[s, 1, half, place]
                            c, d = props[s, 0, half, up, ahead], props[s, 1, half, up, ahead]
                            real = real + (a * c + b * d)
                            imag = imag + (a * d - b * c)
                        sums[t, 0, half, place] = real
                        sums[t, 1, half, place] = imag
                        a, b = props[0, 0, half, at, own], props[0, 1, half, at, own]
                        c, d = props[1, 0, half, down, behind], props[1, 1, half, down, behind]
                        sums[t, 2, half, place] += a * c + b * d
                        sums[t, 3, half, place] += b * c - a * d

    @pl.loop(0, reach + 1)
    def _(k):
        @pl.when(k == 0)
        def _():
            local[0].wait()
            local[1].wait()

        plan.turn(k)
        for w in range(walkers):
            absorb(plan.slot_at(k), w)

    local[2].wait()
    local[3].wait()
    plan.drain()


def leave(groups, sums, ph_keep, pp_keep, ph_out, pp_out, ph_new, pp_new, sem):
    trans, _, _, height, lanes = sums.shape
    group = lax.axis_index("grp")
    row = lax.broadcasted_iota(jnp.int32, (height, lanes), 0)
    lane = lax.broadcasted_iota(jnp.int32, (height, lanes), 1)
    freq = (lane // NK - group * (height // NK) - row // NK + 2 * NW) % NW
    mom = (lane % NK - row % NK + NK) % NK
    source = freq * NK + mom
    index, upper = source % lanes, source >= lanes
    copies = []
    for t in range(trans):
        for keep, new, first in ((ph_keep, ph_new, 0), (pp_keep, pp_new, 2)):
            for part in range(2):
                low, high = [
                    jnp.take_along_axis(sums[t, first + part, half], index, 1) for half in range(2)
                ]
                new[part, t, :, 0:lanes] = keep[part, t, :, 0:lanes] + jnp.where(upper, high, low)
                new[part, t, :, lanes:] = keep[part, t, :, lanes:] + jnp.where(upper, low, high)
        for i, (new, out) in enumerate(((ph_new, ph_out), (pp_new, pp_out))):
            copies.append(pltpu.make_async_copy(new.at[:, t], out.at[:, t], sem.at[t, i]))
            copies[-1].start()
    for copy in copies:
        copy.wait()


def on_device(masses, spins, shift_table, flip_table, ph_in, pp_in):
    groups = lax.axis_size("grp")
    blocks = lax.axis_size("blk")
    reach = min(8, blocks - 1)
    visits = reach + 1
    walkers, _, order, _ = masses.shape
    trans = shift_table.shape[0]
    height = order // groups
    chips = groups // 2
    f32, bf16 = jnp.float32, jnp.bfloat16
    sums_shape = (trans, 4, order // LANES, height, LANES)
    dma = pltpu.SemaphoreType.DMA
    anywhere = pl.BlockSpec(memory_space=pl.ANY)
    if whole_gather(blocks, groups, reach):
        recv_shape, send_shape = (visits, 3), (5,)
    else:
        recv_shape, send_shape = (visits, groups + 1), (visits, 3 + 2 * (chips - 1))
    sums = pl.pallas_call(
        functools.partial(kernel, blocks, groups, reach),
        out_shape=(
            pltpu.VMEM(sums_shape, f32),
            pltpu.VMEM(ph_in.shape, f32),
            pltpu.VMEM(pp_in.shape, f32),
        ),
        in_specs=[pl.BlockSpec(memory_space=pltpu.SMEM)]
        + [pl.BlockSpec(memory_space=pltpu.HBM)] * 4,
        out_specs=(pl.BlockSpec(memory_space=pltpu.VMEM),) * 3,
        scratch_shapes=[
            pltpu.VMEM((visits, walkers, 2, order, order), bf16),
            pltpu.VMEM((visits, walkers, order), jnp.int32),
            pltpu.VMEM((order, order), bf16),
            pltpu.VMEM((2 * height, order), bf16),
            pltpu.VMEM((2, order, order), f32),
            pltpu.VMEM((order, 2 * order), bf16),
            pltpu.VMEM((2, 2, order // LANES, NW, NK + ROWS, LANES), f32),
            pltpu.VMEM((2, 2, order // LANES, height, LANES), f32),
            dma(recv_shape),
            dma(send_shape),
            dma((4,)),
        ],
        compiler_params=pltpu.CompilerParams(
            collective_id=0, has_side_effects=True, vmem_limit_bytes=VMEM - 8 * (ph_in.size + pp_in.size) - 65536
        ),
    )(shift_table, masses, spins, ph_in, pp_in)
    return pl.pallas_call(
        functools.partial(leave, groups),
        out_shape=(
            jax.ShapeDtypeStruct(ph_in.shape, f32),
            jax.ShapeDtypeStruct(pp_in.shape, f32),
        ),
        in_specs=[pl.BlockSpec(memory_space=pltpu.VMEM)] * 3,
        out_specs=(anywhere,) * 2,
        scratch_shapes=[
            pltpu.VMEM(ph_in.shape, f32),
            pltpu.VMEM(pp_in.shape, f32),
            dma((trans, 2)),
        ],
        compiler_params=pltpu.CompilerParams(vmem_limit_bytes=16 * 1024 * 1024),
    )(*[pltpu.with_memory_space_constraint(one, pltpu.VMEM) for one in sums])


def solution(mesh):
    placed = (
        P("blk", None, None, None),
        P("blk", None),
        P("blk", None),
        P("blk", None),
        P(None, "blk", "grp", None),
        P(None, "blk", "grp", None),
    )
    return jax.shard_map(
        on_device,
        mesh=mesh,
        in_specs=placed,
        out_specs=(P(None, "blk", "grp", None), P(None, "blk", "grp", None)),
        check_vma=False,
    )
```

```python
import functools
import math

import jax
import jax.numpy as jnp
from jax import lax
from jax.experimental import pallas as pl
from jax.experimental.pallas import tpu as pltpu
from jax.sharding import PartitionSpec as P

NW = 16
NK = 16
COUPLING = 0.5
VMEM = 67043328
LANES = 128
ROWS = 8
MESH = pl.DeviceIdType.MESH
NT = (((1,), (1,)), ((), ()))


def angle(steps):
    return steps.astype(jnp.float32) * (math.pi / NW)


def whole_gather(blocks, groups, reach):
    return blocks == 8 and groups == 4 and reach == 7


def send(src, dst, send_sem, recv_sem, target):
    return pltpu.make_async_remote_copy(
        src_ref=src,
        dst_ref=dst,
        send_sem=send_sem,
        recv_sem=recv_sem,
        device_id=target,
        device_id_type=MESH,
    )


def bulk(view, sem):
    return pltpu.make_async_copy(view, view, sem)


class Gather:
    TURNS = ('', 'H0 O0 O1 I0', 'H1 h0 F0', 'F1 i0 I1', 'h1', 'f0 f1 i1', '', '')
    SLOTS = 'SOHIFhfi'

    def __init__(self, group, block, order, walkers, masses, spins, held, held_spins, recv, sends):
        self.chip, self.core = group // 2, group % 2
        self.block, self.layer, self.side = block, block // 2, block % 2
        self.masses, self.spins = masses, spins
        self.held, self.held_spins = held, held_spins
        self.recv, self.sends = recv, sends
        self.quarter = order // 4
        self.walkers = walkers
        self.end = jnp.logical_or(self.layer == 0, self.layer == 3)
        other = self.chip * 2 + (1 - self.core)
        self.other = other
        self.partner = (other, block)
        self.across = ((1 - self.chip) * 2 + (1 - self.core), block)
        self.beside = (other, self.layer * 2 + (1 - self.side))
        same, mate = self.side, 1 - self.side
        first, second = self.by_layer(1, 3, 0, 2), self.by_layer(2, 2, 1, 1)
        full = self.by_layer(3, 0, 3, 0)
        self.slots = {
            "S": block,
            "O": self.layer * 2 + mate,
            "H": first * 2 + same,
            "I": second * 2 + same,
            "F": full * 2 + same,
            "h": first * 2 + mate,
            "i": second * 2 + mate,
            "f": full * 2 + mate,
        }

    def by_layer(self, *values):
        return sum(
            value * (self.layer == i).astype(jnp.int32) for i, value in enumerate(values)
        )

    def slot_at(self, k):
        return sum(
            self.slots[kind] * (k == i).astype(jnp.int32) for i, kind in enumerate(self.SLOTS)
        )

    def up(self, layer):
        return (self.other, layer * 2 + self.side)

    def others(self):
        return [(self.other, lax.rem(self.block + step, 8)) for step in range(1, 8)]

    def greet(self):
        self.barrier = pltpu.get_barrier_semaphore()
        targets = self.others() + [self.partner, self.across]
        for target in targets:
            pl.semaphore_signal(self.barrier, inc=1, device_id=target, device_id_type=MESH)

    def enter(self):
        pl.semaphore_wait(self.barrier, 9)

    def rows(self, ref, half, parity):
        first = pl.multiple_of((half * 2 + parity) * self.quarter, self.quarter)
        return ref.at[:, :, pl.ds(first, self.quarter)]

    def own(self, part, target):
        half = 1 - self.chip if part else self.chip
        dst = self.rows(self.held.at[self.block], half, 1 - self.core)
        src = self.rows(self.masses, half, 1 - self.core)
        send(src, dst, self.sends.at[0], self.recv.at[self.block, part], target).start()

    def note(self, target):
        return send(self.spins, self.held_spins.at[self.block], self.sends.at[3],
                    self.sends.at[4], target)

    def begin(self):
        for target in self.others():
            self.note(target).start()
        ends = self.by_layer(1, 0, 0, 2), self.by_layer(3, 0, 0, 0)
        inner = self.by_layer(2, 2, 1, 1)
        near_end, far_end = self.by_layer(0, 0, 3, 0), self.by_layer(0, 3, 0, 0)

        @pl.when(self.end)
        def _():
            self.own(0, self.beside)
            self.own(1, self.beside)
            self.own(0, self.up(inner))
            for layer in ends:
                self.own(0, self.up(layer))
                self.own(1, self.up(layer))

        @pl.when(jnp.logical_not(self.end))
        def _():
            self.own(0, self.up(near_end))
            self.own(0, self.up(far_end))
            self.own(0, self.beside)
            self.own(1, self.beside)
            self.own(0, self.up(inner))

    def parity(self, kind, part):
        moved = kind in "fi" if part == 0 else kind in "HIf"
        if kind == "h":
            moved = part == 0
        return 1 - self.core if moved else self.core

    def event(self, kind, part):
        slot = self.slots[kind]
        half = 1 - self.chip if part else self.chip
        view = self.rows(self.held.at[slot], half, self.parity(kind, part))

        def copy(sem, recv, target):
            return send(view, view, self.sends.at[sem], self.recv.at[slot, recv], target)

        copy(1, part, self.partner).wait_recv()
        if kind == "F" or (kind in "HI" and part == 0):
            copy(1, part, self.beside).start()
        if kind in "HIhi" and part == 0:
            copy(1, 1, self.across).start()
        copy(2, 2, self.partner).start()

    def some(self, count):
        return self.held.at[0:count, :, :, 0 : self.quarter]

    def turn(self, k):
        for i, turn in enumerate(self.TURNS):
            if turn:
                @pl.when(k == i)
                def _():
                    for name in turn.split():
                        self.event(name[0], int(name[1]))

        @pl.when(k == 1)
        def _():
            bulk(self.held_spins.at[0:7], self.sends.at[4]).wait()

        @pl.when(k >= 1)
        def _():
            half = self.held.at[0, :, :, 0 : 2 * self.quarter]
            bulk(half, self.recv.at[self.slot_at(k), 2]).wait()

    def drain(self):
        pl.when(self.end)(lambda: bulk(self.some(7), self.sends.at[0]).wait())
        pl.when(jnp.logical_not(self.end))(lambda: bulk(self.some(5), self.sends.at[0]).wait())
        bulk(self.some(8), self.sends.at[1]).wait()
        bulk(self.held.at[0:7, :, :, 0 : 2 * self.quarter], self.sends.at[2]).wait()
        bulk(self.held_spins.at[0:7], self.sends.at[3]).wait()


class Chain:
    def __init__(self, group, block, groups, blocks, reach, height, masses, spins, held,
                 held_spins, recv, sends):
        self.group, self.block = group, block
        self.blocks, self.reach, self.height = blocks, reach, height
        self.groups, self.chips = groups, groups // 2
        self.chip, self.core = group // 2, group % 2
        self.partner = self.chip * 2 + (1 - self.core)
        self.masses, self.spins = masses, spins
        self.held, self.held_spins = held, held_spins
        self.recv, self.sends = recv, sends

    def slot_at(self, k):
        return k

    def far(self, step):
        return lax.rem(self.chip + step, self.chips) * 2 + self.core

    def rows(self, ref, piece):
        first = pl.multiple_of(piece * self.height, self.height)
        return ref.at[:, :, pl.ds(first, self.height)]

    def greet(self):
        self.barrier = pltpu.get_barrier_semaphore()
        blocks = [
            lax.rem(self.block - offset + self.blocks, self.blocks)
            for offset in range(1, self.reach + 1)
        ]
        targets = [(self.group, block) for block in blocks] + [(self.partner, self.block)]
        targets += [(self.far(step), self.block) for step in range(1, self.chips)]
        for target in targets:
            pl.semaphore_signal(self.barrier, inc=1, device_id=target, device_id_type=MESH)

    def enter(self):
        pl.semaphore_wait(self.barrier, self.reach + self.chips)

    def direct(self, offset):
        target = (self.group, lax.rem(self.block + offset, self.blocks))
        return (
            send(
                self.rows(self.masses, self.group),
                self.rows(self.held.at[offset], self.group),
                self.sends.at[offset, 0], self.recv.at[offset, self.group], target,
            ),
            send(
                self.spins, self.held_spins.at[offset],
                self.sends.at[offset, 1], self.recv.at[offset, self.groups], target,
            ),
        )

    def passed(self, offset, piece, target, sem):
        view = self.rows(self.held.at[offset], piece)
        return send(view, view, self.sends.at[offset, sem], self.recv.at[offset, piece],
                    (target, self.block))

    def to_core(self, offset):
        return self.passed(offset, self.group, self.partner, 2)

    def to_far(self, offset, step):
        return self.passed(offset, self.group, self.far(step), 1 + 2 * step)

    def relay(self, offset, step):
        return self.passed(offset, self.far(step), self.partner, 2 + 2 * step)

    def arrival(self, offset, piece):
        return self.passed(offset, piece, self.partner, 2)

    def begin(self):
        for offset in range(1, self.reach + 1):
            for copy in self.direct(offset):
                copy.start()

    def take(self, k):
        self.arrival(k, self.group).wait_recv()
        for step in range(1, self.chips):
            self.to_far(k, step).start()
        self.to_core(k).start()

    def turn(self, k):
        pl.when(k == 0)(lambda: self.take(1))
        pl.when(jnp.logical_and(k >= 1, k < self.reach))(lambda: self.take(k + 1))

        @pl.when(k >= 1)
        def _():
            for step in range(1, self.chips):
                self.arrival(k, self.far(step)).wait_recv()
                self.relay(k, step).start()
            self.arrival(k, self.partner).wait_recv()
            for step in range(1, self.chips):
                piece = lax.rem(self.chip + step, self.chips) * 2 + (1 - self.core)
                self.arrival(k, piece).wait_recv()
            self.direct(k)[1].wait_recv()

    def drain(self):
        for offset in range(1, self.reach + 1):
            for copy in self.direct(offset):
                copy.wait_send()
            self.to_core(offset).wait_send()
            for step in range(1, self.chips):
                self.to_far(offset, step).wait_send()
                self.relay(offset, step).wait_send()

def kernel(
    blocks, groups, reach, shift_ref, masses_ref, spins_ref, ph_ref, pp_ref,
    sums, ph_keep, pp_keep, held, held_spins, steps, band, unit, skew, props, fixed,
    recv_sem, send_sem, local_sem,
):
    group = lax.axis_index("grp")
    block = lax.axis_index("blk")
    order = held.shape[-1]
    walkers = held.shape[1]
    trans = sums.shape[0]
    height = order // groups
    lanes = sums.shape[-1]
    f32, bf16 = jnp.float32, jnp.bfloat16
    gather = whole_gather(blocks, groups, reach)
    home = block if gather else 0

    local = [
        pltpu.make_async_copy(masses_ref, held.at[home], local_sem.at[0]),
        pltpu.make_async_copy(spins_ref, held_spins.at[home], local_sem.at[1]),
        pltpu.make_async_copy(ph_ref, ph_keep, local_sem.at[2]),
        pltpu.make_async_copy(pp_ref, pp_keep, local_sem.at[3]),
    ]
    if gather:
        plan = Gather(
            group, block, order, walkers, masses_ref, spins_ref, held, held_spins,
            recv_sem, send_sem,
        )
    else:
        plan = Chain(
            group, block, groups, blocks, reach, height, masses_ref, spins_ref, held,
            held_spins, recv_sem, send_sem,
        )
    plan.greet()
    for copy in local:
        copy.start()
    plan.enter()
    plan.begin()

    norm = 1.0 / math.sqrt(NW * NK)
    row = lax.broadcasted_iota(jnp.int32, (NW, order), 0)
    column = lax.broadcasted_iota(jnp.int32, (NW, order), 1)
    slices, sites = column // NK, column % NK

    def circle(numerator):
        turn = angle(numerator % (2 * NW))
        return jnp.cos(turn), jnp.sin(turn)

    site_cos, site_sin = circle(2 * NW * NK - 2 * row * sites)
    odd_cos, odd_sin = circle((2 * row + 1) * slices)
    even_cos, even_sin = circle(2 * row * slices)
    for i in range(NW):
        here = slice(i * NK, (i + 1) * NK)
        c, d = odd_cos[i : i + 1], odd_sin[i : i + 1]
        cos, sin = c * site_cos - d * site_sin, d * site_cos + c * site_sin
        unit[0, here], unit[1, here] = cos, sin
        if i < NW // 2:
            steps[here] = (cos * norm).astype(bf16)
            steps[order // 2 + i * NK : order // 2 + (i + 1) * NK] = (sin * norm).astype(bf16)
        c, d = even_cos[i : i + 1], even_sin[i : i + 1]
        skew[here, 0:order] = ((c * site_cos - d * site_sin) * norm).astype(bf16)
        skew[here, order:] = ((d * site_cos + c * site_sin) * norm).astype(bf16)
    mine = pl.ds(pl.multiple_of(group * height, height), height)
    band[0:height] = (unit[0, mine] * norm).astype(bf16)
    band[height:] = (unit[1, mine] * norm).astype(bf16)
    sums[...] = jnp.zeros(sums.shape, f32)

    def dot(a, b):
        return jnp.dot(a, b, preferred_element_type=f32)

    middle = order // 2
    flip = ROWS - 1 - lax.broadcasted_iota(jnp.int32, (ROWS, lanes), 0)

    def put(s, part, half, lower, upper):
        for i in range(NW // 2):
            tiles = [lower[i * NK + r : i * NK + r + ROWS] for r in range(0, NK, ROWS)]
            for r, tile in enumerate(tiles + tiles[:1]):
                props[s, part, half, i, r * ROWS : (r + 1) * ROWS] = tile
            tiles = [upper[i * NK + r : i * NK + r + ROWS] for r in range(0, NK, ROWS)]
            tiles = [jnp.take_along_axis(tile, flip, 0) for tile in tiles[::-1]]
            for r, tile in enumerate(tiles + tiles[:1]):
                props[s, part, half, NW - 1 - i, r * ROWS : (r + 1) * ROWS] = tile

    def from_row(freq, mom):
        mirrored = (freq >= NW // 2).astype(jnp.int32)
        return pl.ds(lax.rem(mom - mirrored + NK, NK), ROWS)

    def absorb(slot, w):
        signed = (2 * held_spins[slot, w : w + 1, :] - 1).astype(f32)
        turned, back = [], []
        for s in range(2):
            factor = jnp.exp((COUPLING if s == 0 else -COUPLING) * signed)
            scaled = (held[slot, w, s].astype(f32) * factor).astype(bf16)
            left = lax.dot_general(band[...], scaled, NT, preferred_element_type=f32)
            real, imag = left[:height], left[height:]
            cos, sin = unit[0, mine], unit[1, mine]
            back += [
                (cos * real + sin * imag).astype(bf16),
                (sin * real - cos * imag).astype(bf16),
            ]
            first = dot(steps[...], scaled)
            real, imag = first[:middle], first[middle:]
            cos, sin = unit[0, 0:middle], unit[1, 0:middle]
            turned += [
                (real * cos + imag * sin).astype(bf16),
                (imag * cos - real * sin).astype(bf16),
            ]
        moving = dot(jnp.concatenate(turned + back, 0), skew[...])
        for s in range(2):
            for half in range(order // lanes):
                even = slice(half * lanes, (half + 1) * lanes)
                odd = slice(order + half * lanes, order + (half + 1) * lanes)
                real = moving[s * order : s * order + middle]
                imag = moving[s * order + middle : (s + 1) * order]
                put(s, 0, half, real[:, even] + imag[:, odd], real[:, even] - imag[:, odd])
                put(s, 1, half, imag[:, even] - real[:, odd], -imag[:, even] - real[:, odd])
                first = 2 * order + 2 * s * height
                real = moving[first : first + height]
                imag = moving[first + height : first + 2 * height]
                fixed[s, 0, half] = real[:, even] - imag[:, odd]
                fixed[s, 1, half] = -real[:, odd] - imag[:, even]

        @pl.loop(0, trans)
        def _(t):
            freq, mom = shift_ref[t, 0] // NK, shift_ref[t, 0] % NK
            for i in range(height // NK):
                at = group * (height // NK) + i
                up, down = lax.rem(at + freq, NW), lax.rem(at - freq + NW, NW)
                for piece in range(NK // ROWS):
                    rows = i * NK + piece * ROWS
                    place = slice(rows, rows + ROWS)
                    offset = piece * ROWS
                    ahead = from_row(up, mom + offset)
                    behind = from_row(down, NK - mom + offset)
                    own = from_row(at, offset)
                    for half in range(order // lanes):
                        real, imag = sums[t, 0, half, place], sums[t, 1, half, place]
                        for s in range(2):
                            a, b = fixed[s, 0, half, place], fixed[s, 1, half, place]
                            c, d = props[s, 0, half, up, ahead], props[s, 1, half, up, ahead]
                            real = real + (a * c + b * d)
                            imag = imag + (a * d - b * c)
                        sums[t, 0, half, place] = real
                        sums[t, 1, half, place] = imag
                        a, b = props[0, 0, half, at, own], props[0, 1, half, at, own]
                        c, d = props[1, 0, half, down, behind], props[1, 1, half, down, behind]
                        sums[t, 2, half, place] += a * c + b * d
                        sums[t, 3, half, place] += b * c - a * d

    @pl.loop(0, reach + 1)
    def _(k):
        @pl.when(k == 0)
        def _():
            local[0].wait()
            local[1].wait()

        plan.turn(k)
        for w in range(walkers):
            absorb(plan.slot_at(k), w)

    local[2].wait()
    local[3].wait()
    plan.drain()


def leave(groups, sums, ph_keep, pp_keep, ph_out, pp_out, ph_new, pp_new, sem):
    trans, _, _, height, lanes = sums.shape
    group = lax.axis_index("grp")
    row = lax.broadcasted_iota(jnp.int32, (height, lanes), 0)
    lane = lax.broadcasted_iota(jnp.int32, (height, lanes), 1)
    freq = (lane // NK - group * (height // NK) - row // NK + 2 * NW) % NW
    mom = (lane % NK - row % NK + NK) % NK
    source = freq * NK + mom
    index, upper = source % lanes, source >= lanes
    copies = []
    for t in range(trans):
        for keep, new, first in ((ph_keep, ph_new, 0), (pp_keep, pp_new, 2)):
            for part in range(2):
                low, high = [
                    jnp.take_along_axis(sums[t, first + part, half], index, 1) for half in range(2)
                ]
                new[part, t, :, 0:lanes] = keep[part, t, :, 0:lanes] + jnp.where(upper, high, low)
                new[part, t, :, lanes:] = keep[part, t, :, lanes:] + jnp.where(upper, low, high)
        for i, (new, out) in enumerate(((ph_new, ph_out), (pp_new, pp_out))):
            copies.append(pltpu.make_async_copy(new.at[:, t], out.at[:, t], sem.at[t, i]))
            copies[-1].start()
    for copy in copies:
        copy.wait()


def on_device(masses, spins, shift_table, flip_table, ph_in, pp_in):
    groups = lax.axis_size("grp")
    blocks = lax.axis_size("blk")
    reach = min(8, blocks - 1)
    visits = reach + 1
    walkers, _, order, _ = masses.shape
    trans = shift_table.shape[0]
    height = order // groups
    chips = groups // 2
    f32, bf16 = jnp.float32, jnp.bfloat16
    sums_shape = (trans, 4, order // LANES, height, LANES)
    dma = pltpu.SemaphoreType.DMA
    anywhere = pl.BlockSpec(memory_space=pl.ANY)
    if whole_gather(blocks, groups, reach):
        recv_shape, send_shape = (visits, 3), (5,)
    else:
        recv_shape, send_shape = (visits, groups + 1), (visits, 3 + 2 * (chips - 1))
    sums = pl.pallas_call(
        functools.partial(kernel, blocks, groups, reach),
        out_shape=(
            pltpu.VMEM(sums_shape, f32),
            pltpu.VMEM(ph_in.shape, f32),
            pltpu.VMEM(pp_in.shape, f32),
        ),
        in_specs=[pl.BlockSpec(memory_space=pltpu.SMEM)]
        + [pl.BlockSpec(memory_space=pltpu.HBM)] * 4,
        out_specs=(pl.BlockSpec(memory_space=pltpu.VMEM),) * 3,
        scratch_shapes=[
            pltpu.VMEM((visits, walkers, 2, order, order), bf16),
            pltpu.VMEM((visits, walkers, order), jnp.int32),
            pltpu.VMEM((order, order), bf16),
            pltpu.VMEM((2 * height, order), bf16),
            pltpu.VMEM((2, order, order), f32),
            pltpu.VMEM((order, 2 * order), bf16),
            pltpu.VMEM((2, 2, order // LANES, NW, NK + ROWS, LANES), f32),
            pltpu.VMEM((2, 2, order // LANES, height, LANES), f32),
            dma(recv_shape),
            dma(send_shape),
            dma((4,)),
        ],
        compiler_params=pltpu.CompilerParams(
            collective_id=0, has_side_effects=True, vmem_limit_bytes=VMEM - 8 * (ph_in.size + pp_in.size) - 65536
        ),
    )(shift_table, masses, spins, ph_in, pp_in)
    return pl.pallas_call(
        functools.partial(leave, groups),
        out_shape=(
            jax.ShapeDtypeStruct(ph_in.shape, f32),
            jax.ShapeDtypeStruct(pp_in.shape, f32),
        ),
        in_specs=[pl.BlockSpec(memory_space=pltpu.VMEM)] * 3,
        out_specs=(anywhere,) * 2,
        scratch_shapes=[
            pltpu.VMEM(ph_in.shape, f32),
            pltpu.VMEM(pp_in.shape, f32),
            dma((trans, 2)),
        ],
        compiler_params=pltpu.CompilerParams(vmem_limit_bytes=16 * 1024 * 1024),
    )(*[pltpu.with_memory_space_constraint(one, pltpu.VMEM) for one in sums])


def solution(mesh):
    placed = (
        P("blk", None, None, None),
        P("blk", None),
        P("blk", None),
        P("blk", None),
        P(None, "blk", "grp", None),
        P(None, "blk", "grp", None),
    )
    return jax.shard_map(
        on_device,
        mesh=mesh,
        in_specs=placed,
        out_specs=(P(None, "blk", "grp", None), P(None, "blk", "grp", None)),
        check_vma=False,
    )
```

```python
import functools
import math

import jax
import jax.numpy as jnp
from jax import lax
from jax.experimental import pallas as pl
from jax.experimental.pallas import tpu as pltpu
from jax.sharding import PartitionSpec as P

NW = 16
NK = 16
COUPLING = 0.5
VMEM = 67043328
LANES = 128
ROWS = 8
HALF_BITS = 3
BITS = 4
MESH = pl.DeviceIdType.MESH
NT = (((1,), (1,)), ((), ()))


def angle(steps):
    return steps.astype(jnp.float32) * (math.pi / NW)


def whole_gather(blocks, groups, reach):
    return blocks == 8 and groups == 4 and reach == 7


def send(src, dst, send_sem, recv_sem, target):
    return pltpu.make_async_remote_copy(
        src_ref=src,
        dst_ref=dst,
        send_sem=send_sem,
        recv_sem=recv_sem,
        device_id=target,
        device_id_type=MESH,
    )


def bulk(view, sem):
    return pltpu.make_async_copy(view, view, sem)


class Gather:
    TURNS = ('', 'H0 O0 O1 I0', 'H1 h0 F0', 'F1 i0 I1', 'h1', 'f0 f1 i1', '', '')
    SLOTS = 'SOHIFhfi'

    def __init__(self, group, block, order, walkers, masses, spins, held, held_spins, recv, sends):
        self.chip, self.core = group // 2, group % 2
        self.block, self.layer, self.side = block, block // 2, block % 2
        self.masses, self.spins = masses, spins
        self.held, self.held_spins = held, held_spins
        self.recv, self.sends = recv, sends
        self.quarter = order // 4
        self.walkers = walkers
        self.end = jnp.logical_or(self.layer == 0, self.layer == 3)
        other = self.chip * 2 + (1 - self.core)
        self.other = other
        self.partner = (other, block)
        self.across = ((1 - self.chip) * 2 + (1 - self.core), block)
        self.beside = (other, self.layer * 2 + (1 - self.side))
        same, mate = self.side, 1 - self.side
        first, second = self.by_layer(1, 3, 0, 2), self.by_layer(2, 2, 1, 1)
        full = self.by_layer(3, 0, 3, 0)
        self.slots = {
            "S": block,
            "O": self.layer * 2 + mate,
            "H": first * 2 + same,
            "I": second * 2 + same,
            "F": full * 2 + same,
            "h": first * 2 + mate,
            "i": second * 2 + mate,
            "f": full * 2 + mate,
        }

    def by_layer(self, *values):
        return sum(
            value * (self.layer == i).astype(jnp.int32) for i, value in enumerate(values)
        )

    def slot_at(self, k):
        return sum(
            self.slots[kind] * (k == i).astype(jnp.int32) for i, kind in enumerate(self.SLOTS)
        )

    def up(self, layer):
        return (self.other, layer * 2 + self.side)

    def others(self):
        return [(self.other, lax.rem(self.block + step, 8)) for step in range(1, 8)]

    def greet(self):
        self.barrier = pltpu.get_barrier_semaphore()
        targets = self.others() + [self.partner, self.across]
        for target in targets:
            pl.semaphore_signal(self.barrier, inc=1, device_id=target, device_id_type=MESH)

    def enter(self):
        pl.semaphore_wait(self.barrier, 9)

    def rows(self, ref, half, parity):
        first = pl.multiple_of((half * 2 + parity) * self.quarter, self.quarter)
        return ref.at[:, :, pl.ds(first, self.quarter)]

    def own(self, part, target):
        half = 1 - self.chip if part else self.chip
        dst = self.rows(self.held.at[self.block], half, 1 - self.core)
        src = self.rows(self.masses, half, 1 - self.core)
        send(src, dst, self.sends.at[0], self.recv.at[self.block, part], target).start()

    def note(self, target):
        return send(self.spins, self.held_spins.at[self.block], self.sends.at[3],
                    self.sends.at[4], target)

    def begin(self):
        for target in self.others():
            self.note(target).start()
        ends = self.by_layer(1, 0, 0, 2), self.by_layer(3, 0, 0, 0)
        inner = self.by_layer(2, 2, 1, 1)
        near_end, far_end = self.by_layer(0, 0, 3, 0), self.by_layer(0, 3, 0, 0)

        @pl.when(self.end)
        def _():
            self.own(0, self.beside)
            self.own(1, self.beside)
            self.own(0, self.up(inner))
            for layer in ends:
                self.own(0, self.up(layer))
                self.own(1, self.up(layer))

        @pl.when(jnp.logical_not(self.end))
        def _():
            self.own(0, self.up(near_end))
            self.own(0, self.up(far_end))
            self.own(0, self.beside)
            self.own(1, self.beside)
            self.own(0, self.up(inner))

    def parity(self, kind, part):
        moved = kind in "fi" if part == 0 else kind in "HIf"
        if kind == "h":
            moved = part == 0
        return 1 - self.core if moved else self.core

    def event(self, kind, part):
        slot = self.slots[kind]
        half = 1 - self.chip if part else self.chip
        view = self.rows(self.held.at[slot], half, self.parity(kind, part))

        def copy(sem, recv, target):
            return send(view, view, self.sends.at[sem], self.recv.at[slot, recv], target)

        copy(1, part, self.partner).wait_recv()
        if kind == "F" or (kind in "HI" and part == 0):
            copy(1, part, self.beside).start()
        if kind in "HIhi" and part == 0:
            copy(1, 1, self.across).start()
        copy(2, 2, self.partner).start()

    def some(self, count):
        return self.held.at[0:count, :, :, 0 : self.quarter]

    def turn(self, k):
        for i, turn in enumerate(self.TURNS):
            if turn:
                @pl.when(k == i)
                def _():
                    for name in turn.split():
                        self.event(name[0], int(name[1]))

        @pl.when(k == 1)
        def _():
            bulk(self.held_spins.at[0:7], self.sends.at[4]).wait()

        @pl.when(k >= 1)
        def _():
            half = self.held.at[0, :, :, 0 : 2 * self.quarter]
            bulk(half, self.recv.at[self.slot_at(k), 2]).wait()

    def drain(self):
        pl.when(self.end)(lambda: bulk(self.some(7), self.sends.at[0]).wait())
        pl.when(jnp.logical_not(self.end))(lambda: bulk(self.some(5), self.sends.at[0]).wait())
        bulk(self.some(8), self.sends.at[1]).wait()
        bulk(self.held.at[0:7, :, :, 0 : 2 * self.quarter], self.sends.at[2]).wait()
        bulk(self.held_spins.at[0:7], self.sends.at[3]).wait()


class Chain:
    def __init__(self, group, block, groups, blocks, reach, height, masses, spins, held,
                 held_spins, recv, sends):
        self.group, self.block = group, block
        self.blocks, self.reach, self.height = blocks, reach, height
        self.groups, self.chips = groups, groups // 2
        self.chip, self.core = group // 2, group % 2
        self.partner = self.chip * 2 + (1 - self.core)
        self.masses, self.spins = masses, spins
        self.held, self.held_spins = held, held_spins
        self.recv, self.sends = recv, sends

    def slot_at(self, k):
        return k

    def far(self, step):
        return lax.rem(self.chip + step, self.chips) * 2 + self.core

    def rows(self, ref, piece):
        first = pl.multiple_of(piece * self.height, self.height)
        return ref.at[:, :, pl.ds(first, self.height)]

    def greet(self):
        self.barrier = pltpu.get_barrier_semaphore()
        blocks = [
            lax.rem(self.block - offset + self.blocks, self.blocks)
            for offset in range(1, self.reach + 1)
        ]
        targets = [(self.group, block) for block in blocks] + [(self.partner, self.block)]
        targets += [(self.far(step), self.block) for step in range(1, self.chips)]
        for target in targets:
            pl.semaphore_signal(self.barrier, inc=1, device_id=target, device_id_type=MESH)

    def enter(self):
        pl.semaphore_wait(self.barrier, self.reach + self.chips)

    def direct(self, offset):
        target = (self.group, lax.rem(self.block + offset, self.blocks))
        return (
            send(
                self.rows(self.masses, self.group),
                self.rows(self.held.at[offset], self.group),
                self.sends.at[offset, 0], self.recv.at[offset, self.group], target,
            ),
            send(
                self.spins, self.held_spins.at[offset],
                self.sends.at[offset, 1], self.recv.at[offset, self.groups], target,
            ),
        )

    def passed(self, offset, piece, target, sem):
        view = self.rows(self.held.at[offset], piece)
        return send(view, view, self.sends.at[offset, sem], self.recv.at[offset, piece],
                    (target, self.block))

    def to_core(self, offset):
        return self.passed(offset, self.group, self.partner, 2)

    def to_far(self, offset, step):
        return self.passed(offset, self.group, self.far(step), 1 + 2 * step)

    def relay(self, offset, step):
        return self.passed(offset, self.far(step), self.partner, 2 + 2 * step)

    def arrival(self, offset, piece):
        return self.passed(offset, piece, self.partner, 2)

    def begin(self):
        for offset in range(1, self.reach + 1):
            for copy in self.direct(offset):
                copy.start()

    def take(self, k):
        self.arrival(k, self.group).wait_recv()
        for step in range(1, self.chips):
            self.to_far(k, step).start()
        self.to_core(k).start()

    def turn(self, k):
        pl.when(k == 0)(lambda: self.take(1))
        pl.when(jnp.logical_and(k >= 1, k < self.reach))(lambda: self.take(k + 1))

        @pl.when(k >= 1)
        def _():
            for step in range(1, self.chips):
                self.arrival(k, self.far(step)).wait_recv()
                self.relay(k, step).start()
            self.arrival(k, self.partner).wait_recv()
            for step in range(1, self.chips):
                piece = lax.rem(self.chip + step, self.chips) * 2 + (1 - self.core)
                self.arrival(k, piece).wait_recv()
            self.direct(k)[1].wait_recv()

    def drain(self):
        for offset in range(1, self.reach + 1):
            for copy in self.direct(offset):
                copy.wait_send()
            self.to_core(offset).wait_send()
            for step in range(1, self.chips):
                self.to_far(offset, step).wait_send()
                self.relay(offset, step).wait_send()

def kernel(
    blocks, groups, reach, table_ref, masses_ref, spins_ref, ph_ref, pp_ref,
    sums, ph_keep, pp_keep, held, held_spins, steps, band, unit, skew, props, fixed,
    shift_ref, recv_sem, send_sem, local_sem,
):
    group = lax.axis_index("grp")
    block = lax.axis_index("blk")
    order = held.shape[-1]
    walkers = held.shape[1]
    trans = sums.shape[0]
    height = order // groups
    lanes = sums.shape[-1]
    f32, bf16 = jnp.float32, jnp.bfloat16
    gather = whole_gather(blocks, groups, reach)
    home = block if gather else 0

    local = [
        pltpu.make_async_copy(masses_ref, held.at[home], local_sem.at[0]),
        pltpu.make_async_copy(spins_ref, held_spins.at[home], local_sem.at[1]),
        pltpu.make_async_copy(ph_ref, ph_keep, local_sem.at[2]),
        pltpu.make_async_copy(pp_ref, pp_keep, local_sem.at[3]),
        pltpu.make_async_copy(table_ref, shift_ref, local_sem.at[4]),
    ]
    if gather:
        plan = Gather(
            group, block, order, walkers, masses_ref, spins_ref, held, held_spins,
            recv_sem, send_sem,
        )
    else:
        plan = Chain(
            group, block, groups, blocks, reach, height, masses_ref, spins_ref, held,
            held_spins, recv_sem, send_sem,
        )
    plan.greet()
    for copy in local:
        copy.start()
    plan.enter()
    plan.begin()

    norm = 1.0 / math.sqrt(NW * NK)
    row = lax.broadcasted_iota(jnp.int32, (NW, order), 0)
    column = lax.broadcasted_iota(jnp.int32, (NW, order), 1)
    slices, sites = column // NK, column % NK

    def circle(numerator):
        turn = angle(numerator % (2 * NW))
        return jnp.cos(turn), jnp.sin(turn)

    site_cos, site_sin = circle(2 * NW * NK - 2 * row * sites)
    odd_cos, odd_sin = circle((2 * row + 1) * slices)
    even_cos, even_sin = circle(2 * row * slices)
    for i in range(NW):
        here = slice(i * NK, (i + 1) * NK)
        c, d = odd_cos[i : i + 1], odd_sin[i : i + 1]
        cos, sin = c * site_cos - d * site_sin, d * site_cos + c * site_sin
        unit[0, here], unit[1, here] = cos, sin
        if i < NW // 2:
            steps[here] = (cos * norm).astype(bf16)
            steps[order // 2 + i * NK : order // 2 + (i + 1) * NK] = (sin * norm).astype(bf16)
        c, d = even_cos[i : i + 1], even_sin[i : i + 1]
        skew[here, 0:order] = ((c * site_cos - d * site_sin) * norm).astype(bf16)
        skew[here, order:] = ((d * site_cos + c * site_sin) * norm).astype(bf16)
    mine = pl.ds(pl.multiple_of(group * height, height), height)
    band[0:height] = (unit[0, mine] * norm).astype(bf16)
    band[height:] = (unit[1, mine] * norm).astype(bf16)
    sums[...] = jnp.zeros(sums.shape, f32)

    def dot(a, b):
        return jnp.dot(a, b, preferred_element_type=f32)

    middle = order // 2
    flip = ROWS - 1 - lax.broadcasted_iota(jnp.int32, (ROWS, lanes), 0)

    def put(s, part, half, lower, upper):
        for i in range(NW // 2):
            tiles = [lower[i * NK + r : i * NK + r + ROWS] for r in range(0, NK, ROWS)]
            for r, tile in enumerate(tiles + tiles[:1]):
                props[s, part, half, i, r * ROWS : (r + 1) * ROWS] = tile
            tiles = [upper[i * NK + r : i * NK + r + ROWS] for r in range(0, NK, ROWS)]
            tiles = [jnp.take_along_axis(tile, flip, 0) for tile in tiles[::-1]]
            for r, tile in enumerate(tiles + tiles[:1]):
                props[s, part, half, NW - 1 - i, r * ROWS : (r + 1) * ROWS] = tile

    def from_row(freq, mom):
        mirrored = lax.shift_right_logical(freq, HALF_BITS)
        return pl.ds((mom - mirrored + NK) & (NK - 1), ROWS)

    def absorb(slot, w):
        signed = (2 * held_spins[slot, w : w + 1, :] - 1).astype(f32)
        turned, back = [], []
        for s in range(2):
            factor = jnp.exp((COUPLING if s == 0 else -COUPLING) * signed)
            scaled = (held[slot, w, s].astype(f32) * factor).astype(bf16)
            left = lax.dot_general(band[...], scaled, NT, preferred_element_type=f32)
            real, imag = left[:height], left[height:]
            cos, sin = unit[0, mine], unit[1, mine]
            back += [
                (cos * real + sin * imag).astype(bf16),
                (sin * real - cos * imag).astype(bf16),
            ]
            first = dot(steps[...], scaled)
            real, imag = first[:middle], first[middle:]
            cos, sin = unit[0, 0:middle], unit[1, 0:middle]
            turned += [
                (real * cos + imag * sin).astype(bf16),
                (imag * cos - real * sin).astype(bf16),
            ]
        moving = dot(jnp.concatenate(turned + back, 0), skew[...])
        for s in range(2):
            for half in range(order // lanes):
                even = slice(half * lanes, (half + 1) * lanes)
                odd = slice(order + half * lanes, order + (half + 1) * lanes)
                real = moving[s * order : s * order + middle]
                imag = moving[s * order + middle : (s + 1) * order]
                put(s, 0, half, real[:, even] + imag[:, odd], real[:, even] - imag[:, odd])
                put(s, 1, half, imag[:, even] - real[:, odd], -imag[:, even] - real[:, odd])
                first = 2 * order + 2 * s * height
                real = moving[first : first + height]
                imag = moving[first + height : first + 2 * height]
                fixed[s, 0, half] = real[:, even] - imag[:, odd]
                fixed[s, 1, half] = -real[:, odd] - imag[:, even]

        @pl.loop(0, trans)
        def _(t):
            start = shift_ref[t, 0]
            freq, mom = lax.shift_right_logical(start, BITS), start & (NK - 1)
            for i in range(height // NK):
                at = group * (height // NK) + i
                up, down = (at + freq) & (NW - 1), (at - freq + NW) & (NW - 1)
                for piece in range(NK // ROWS):
                    rows = i * NK + piece * ROWS
                    place = slice(rows, rows + ROWS)
                    offset = piece * ROWS
                    ahead = from_row(up, mom + offset)
                    behind = from_row(down, NK - mom + offset)
                    own = from_row(at, offset)
                    for half in range(order // lanes):
                        real, imag = sums[t, 0, half, place], sums[t, 1, half, place]
                        for s in range(2):
                            a, b = fixed[s, 0, half, place], fixed[s, 1, half, place]
                            c, d = props[s, 0, half, up, ahead], props[s, 1, half, up, ahead]
                            real = real + (a * c + b * d)
                            imag = imag + (a * d - b * c)
                        sums[t, 0, half, place] = real
                        sums[t, 1, half, place] = imag
                        a, b = props[0, 0, half, at, own], props[0, 1, half, at, own]
                        c, d = props[1, 0, half, down, behind], props[1, 1, half, down, behind]
                        sums[t, 2, half, place] += a * c + b * d
                        sums[t, 3, half, place] += b * c - a * d

    @pl.loop(0, reach + 1)
    def _(k):
        @pl.when(k == 0)
        def _():
            local[0].wait()
            local[1].wait()
            local[4].wait()

        plan.turn(k)
        for w in range(walkers):
            absorb(plan.slot_at(k), w)

    local[2].wait()
    local[3].wait()
    plan.drain()


def leave(groups, sums, ph_keep, pp_keep, ph_out, pp_out, ph_new, pp_new, sem):
    trans, _, _, height, lanes = sums.shape
    group = lax.axis_index("grp")
    row = lax.broadcasted_iota(jnp.int32, (height, lanes), 0)
    lane = lax.broadcasted_iota(jnp.int32, (height, lanes), 1)
    freq = (lane // NK - group * (height // NK) - row // NK + 2 * NW) % NW
    mom = (lane % NK - row % NK + NK) % NK
    source = freq * NK + mom
    index, upper = source % lanes, source >= lanes
    copies = []
    for t in range(trans):
        for keep, new, first in ((ph_keep, ph_new, 0), (pp_keep, pp_new, 2)):
            for part in range(2):
                low, high = [
                    jnp.take_along_axis(sums[t, first + part, half], index, 1) for half in range(2)
                ]
                new[part, t, :, 0:lanes] = keep[part, t, :, 0:lanes] + jnp.where(upper, high, low)
                new[part, t, :, lanes:] = keep[part, t, :, lanes:] + jnp.where(upper, low, high)
        for i, (new, out) in enumerate(((ph_new, ph_out), (pp_new, pp_out))):
            copies.append(pltpu.make_async_copy(new.at[:, t], out.at[:, t], sem.at[t, i]))
            copies[-1].start()
    for copy in copies:
        copy.wait()


def on_device(masses, spins, shift_table, flip_table, ph_in, pp_in):
    groups = lax.axis_size("grp")
    blocks = lax.axis_size("blk")
    reach = min(8, blocks - 1)
    visits = reach + 1
    walkers, _, order, _ = masses.shape
    trans = shift_table.shape[0]
    height = order // groups
    chips = groups // 2
    f32, bf16 = jnp.float32, jnp.bfloat16
    sums_shape = (trans, 4, order // LANES, height, LANES)
    dma = pltpu.SemaphoreType.DMA
    anywhere = pl.BlockSpec(memory_space=pl.ANY)
    if whole_gather(blocks, groups, reach):
        recv_shape, send_shape = (visits, 3), (5,)
    else:
        recv_shape, send_shape = (visits, groups + 1), (visits, 3 + 2 * (chips - 1))
    sums = pl.pallas_call(
        functools.partial(kernel, blocks, groups, reach),
        out_shape=(
            pltpu.VMEM(sums_shape, f32),
            pltpu.VMEM(ph_in.shape, f32),
            pltpu.VMEM(pp_in.shape, f32),
        ),
        in_specs=[pl.BlockSpec(memory_space=pltpu.HBM)] * 5,
        out_specs=(pl.BlockSpec(memory_space=pltpu.VMEM),) * 3,
        scratch_shapes=[
            pltpu.VMEM((visits, walkers, 2, order, order), bf16),
            pltpu.VMEM((visits, walkers, order), jnp.int32),
            pltpu.VMEM((order, order), bf16),
            pltpu.VMEM((2 * height, order), bf16),
            pltpu.VMEM((2, order, order), f32),
            pltpu.VMEM((order, 2 * order), bf16),
            pltpu.VMEM((2, 2, order // LANES, NW, NK + ROWS, LANES), f32),
            pltpu.VMEM((2, 2, order // LANES, height, LANES), f32),
            pltpu.SMEM(shift_table.shape, jnp.int32),
            dma(recv_shape),
            dma(send_shape),
            dma((5,)),
        ],
        compiler_params=pltpu.CompilerParams(
            collective_id=0, has_side_effects=True, vmem_limit_bytes=VMEM - 8 * (ph_in.size + pp_in.size) - 65536
        ),
    )(shift_table, masses, spins, ph_in, pp_in)
    return pl.pallas_call(
        functools.partial(leave, groups),
        out_shape=(
            jax.ShapeDtypeStruct(ph_in.shape, f32),
            jax.ShapeDtypeStruct(pp_in.shape, f32),
        ),
        in_specs=[pl.BlockSpec(memory_space=pltpu.VMEM)] * 3,
        out_specs=(anywhere,) * 2,
        scratch_shapes=[
            pltpu.VMEM(ph_in.shape, f32),
            pltpu.VMEM(pp_in.shape, f32),
            dma((trans, 2)),
        ],
        compiler_params=pltpu.CompilerParams(vmem_limit_bytes=16 * 1024 * 1024),
    )(*[pltpu.with_memory_space_constraint(one, pltpu.VMEM) for one in sums])


def solution(mesh):
    placed = (
        P("blk", None, None, None),
        P("blk", None),
        P("blk", None),
        P("blk", None),
        P(None, "blk", "grp", None),
        P(None, "blk", "grp", None),
    )
    return jax.shard_map(
        on_device,
        mesh=mesh,
        in_specs=placed,
        out_specs=(P(None, "blk", "grp", None), P(None, "blk", "grp", None)),
        check_vma=False,
    )
```

```python
import functools
import math

import jax
import jax.numpy as jnp
from jax import lax
from jax.experimental import pallas as pl
from jax.experimental.pallas import tpu as pltpu
from jax.sharding import PartitionSpec as P

NW = 16
NK = 16
COUPLING = 0.5
VMEM = 67043328
LANES = 128
ROWS = 8
HALF_BITS = 3
BITS = 4
MESH = pl.DeviceIdType.MESH
NT = (((1,), (1,)), ((), ()))


def angle(steps):
    return steps.astype(jnp.float32) * (math.pi / NW)


def whole_gather(blocks, groups, reach):
    return blocks == 8 and groups == 4 and reach == 7


def send(src, dst, send_sem, recv_sem, target):
    return pltpu.make_async_remote_copy(
        src_ref=src,
        dst_ref=dst,
        send_sem=send_sem,
        recv_sem=recv_sem,
        device_id=target,
        device_id_type=MESH,
    )


def bulk(view, sem):
    return pltpu.make_async_copy(view, view, sem)


class Gather:
    TURNS = ('', 'H0 O0 I0 O1', 'H1 h0 F0', 'F1 i0 I1', 'h1 f0', 'f1 i1', '', '')
    SLOTS = 'SOHIFhfi'

    def __init__(self, group, block, order, walkers, masses, spins, held, held_spins, recv, sends):
        self.chip, self.core = group // 2, group % 2
        self.block, self.layer, self.side = block, block // 2, block % 2
        self.masses, self.spins = masses, spins
        self.held, self.held_spins = held, held_spins
        self.recv, self.sends = recv, sends
        self.quarter = order // 4
        self.walkers = walkers
        self.end = jnp.logical_or(self.layer == 0, self.layer == 3)
        other = self.chip * 2 + (1 - self.core)
        self.other = other
        self.partner = (other, block)
        self.across = ((1 - self.chip) * 2 + (1 - self.core), block)
        self.beside = (other, self.layer * 2 + (1 - self.side))
        same, mate = self.side, 1 - self.side
        first, second = self.by_layer(1, 3, 0, 2), self.by_layer(2, 2, 1, 1)
        full = self.by_layer(3, 0, 3, 0)
        self.slots = {
            "S": block,
            "O": self.layer * 2 + mate,
            "H": first * 2 + same,
            "I": second * 2 + same,
            "F": full * 2 + same,
            "h": first * 2 + mate,
            "i": second * 2 + mate,
            "f": full * 2 + mate,
        }

    def by_layer(self, *values):
        return sum(
            value * (self.layer == i).astype(jnp.int32) for i, value in enumerate(values)
        )

    def slot_at(self, k):
        return sum(
            self.slots[kind] * (k == i).astype(jnp.int32) for i, kind in enumerate(self.SLOTS)
        )

    def up(self, layer):
        return (self.other, layer * 2 + self.side)

    def others(self):
        return [(self.other, lax.rem(self.block + step, 8)) for step in range(1, 8)]

    def greet(self):
        self.barrier = pltpu.get_barrier_semaphore()
        targets = self.others() + [self.partner, self.across]
        for target in targets:
            pl.semaphore_signal(self.barrier, inc=1, device_id=target, device_id_type=MESH)

    def enter(self):
        pl.semaphore_wait(self.barrier, 9)

    def rows(self, ref, half, parity):
        first = pl.multiple_of((half * 2 + parity) * self.quarter, self.quarter)
        return ref.at[:, :, pl.ds(first, self.quarter)]

    def own(self, part, target):
        half = 1 - self.chip if part else self.chip
        dst = self.rows(self.held.at[self.block], half, 1 - self.core)
        src = self.rows(self.masses, half, 1 - self.core)
        send(src, dst, self.sends.at[0], self.recv.at[self.block, part], target).start()

    def note(self, target):
        return send(self.spins, self.held_spins.at[self.block], self.sends.at[3],
                    self.sends.at[4], target)

    def begin(self):
        for target in self.others():
            self.note(target).start()
        ends = self.by_layer(1, 0, 0, 2), self.by_layer(3, 0, 0, 0)
        inner = self.by_layer(2, 2, 1, 1)
        near_end, far_end = self.by_layer(0, 0, 3, 0), self.by_layer(0, 3, 0, 0)

        @pl.when(self.end)
        def _():
            self.own(0, self.beside)
            self.own(1, self.beside)
            self.own(0, self.up(inner))
            for layer in ends:
                self.own(0, self.up(layer))
                self.own(1, self.up(layer))

        @pl.when(jnp.logical_not(self.end))
        def _():
            self.own(0, self.up(near_end))
            self.own(0, self.up(far_end))
            self.own(0, self.beside)
            self.own(1, self.beside)
            self.own(0, self.up(inner))

    def parity(self, kind, part):
        moved = kind in "fi" if part == 0 else kind in "HIf"
        if kind == "h":
            moved = part == 0
        return 1 - self.core if moved else self.core

    def event(self, kind, part):
        slot = self.slots[kind]
        half = 1 - self.chip if part else self.chip
        view = self.rows(self.held.at[slot], half, self.parity(kind, part))

        def copy(sem, recv, target):
            return send(view, view, self.sends.at[sem], self.recv.at[slot, recv], target)

        copy(1, part, self.partner).wait_recv()
        if kind == "F" or (kind in "HI" and part == 0):
            copy(1, part, self.beside).start()
        if kind in "HIhi" and part == 0:
            copy(1, 1, self.across).start()
        copy(2, 2, self.partner).start()

    def some(self, count):
        return self.held.at[0:count, :, :, 0 : self.quarter]

    def turn(self, k):
        for i, turn in enumerate(self.TURNS):
            if turn:
                @pl.when(k == i)
                def _():
                    for name in turn.split():
                        self.event(name[0], int(name[1]))

        @pl.when(k == 1)
        def _():
            bulk(self.held_spins.at[0:7], self.sends.at[4]).wait()

        @pl.when(k >= 1)
        def _():
            half = self.held.at[0, :, :, 0 : 2 * self.quarter]
            bulk(half, self.recv.at[self.slot_at(k), 2]).wait()

    def drain(self):
        pl.when(self.end)(lambda: bulk(self.some(7), self.sends.at[0]).wait())
        pl.when(jnp.logical_not(self.end))(lambda: bulk(self.some(5), self.sends.at[0]).wait())
        bulk(self.some(8), self.sends.at[1]).wait()
        bulk(self.held.at[0:7, :, :, 0 : 2 * self.quarter], self.sends.at[2]).wait()
        bulk(self.held_spins.at[0:7], self.sends.at[3]).wait()


class Chain:
    def __init__(self, group, block, groups, blocks, reach, height, masses, spins, held,
                 held_spins, recv, sends):
        self.group, self.block = group, block
        self.blocks, self.reach, self.height = blocks, reach, height
        self.groups, self.chips = groups, groups // 2
        self.chip, self.core = group // 2, group % 2
        self.partner = self.chip * 2 + (1 - self.core)
        self.masses, self.spins = masses, spins
        self.held, self.held_spins = held, held_spins
        self.recv, self.sends = recv, sends

    def slot_at(self, k):
        return k

    def far(self, step):
        return lax.rem(self.chip + step, self.chips) * 2 + self.core

    def rows(self, ref, piece):
        first = pl.multiple_of(piece * self.height, self.height)
        return ref.at[:, :, pl.ds(first, self.height)]

    def greet(self):
        self.barrier = pltpu.get_barrier_semaphore()
        blocks = [
            lax.rem(self.block - offset + self.blocks, self.blocks)
            for offset in range(1, self.reach + 1)
        ]
        targets = [(self.group, block) for block in blocks] + [(self.partner, self.block)]
        targets += [(self.far(step), self.block) for step in range(1, self.chips)]
        for target in targets:
            pl.semaphore_signal(self.barrier, inc=1, device_id=target, device_id_type=MESH)

    def enter(self):
        pl.semaphore_wait(self.barrier, self.reach + self.chips)

    def direct(self, offset):
        target = (self.group, lax.rem(self.block + offset, self.blocks))
        return (
            send(
                self.rows(self.masses, self.group),
                self.rows(self.held.at[offset], self.group),
                self.sends.at[offset, 0], self.recv.at[offset, self.group], target,
            ),
            send(
                self.spins, self.held_spins.at[offset],
                self.sends.at[offset, 1], self.recv.at[offset, self.groups], target,
            ),
        )

    def passed(self, offset, piece, target, sem):
        view = self.rows(self.held.at[offset], piece)
        return send(view, view, self.sends.at[offset, sem], self.recv.at[offset, piece],
                    (target, self.block))

    def to_core(self, offset):
        return self.passed(offset, self.group, self.partner, 2)

    def to_far(self, offset, step):
        return self.passed(offset, self.group, self.far(step), 1 + 2 * step)

    def relay(self, offset, step):
        return self.passed(offset, self.far(step), self.partner, 2 + 2 * step)

    def arrival(self, offset, piece):
        return self.passed(offset, piece, self.partner, 2)

    def begin(self):
        for offset in range(1, self.reach + 1):
            for copy in self.direct(offset):
                copy.start()

    def take(self, k):
        self.arrival(k, self.group).wait_recv()
        for step in range(1, self.chips):
            self.to_far(k, step).start()
        self.to_core(k).start()

    def turn(self, k):
        pl.when(k == 0)(lambda: self.take(1))
        pl.when(jnp.logical_and(k >= 1, k < self.reach))(lambda: self.take(k + 1))

        @pl.when(k >= 1)
        def _():
            for step in range(1, self.chips):
                self.arrival(k, self.far(step)).wait_recv()
                self.relay(k, step).start()
            self.arrival(k, self.partner).wait_recv()
            for step in range(1, self.chips):
                piece = lax.rem(self.chip + step, self.chips) * 2 + (1 - self.core)
                self.arrival(k, piece).wait_recv()
            self.direct(k)[1].wait_recv()

    def drain(self):
        for offset in range(1, self.reach + 1):
            for copy in self.direct(offset):
                copy.wait_send()
            self.to_core(offset).wait_send()
            for step in range(1, self.chips):
                self.to_far(offset, step).wait_send()
                self.relay(offset, step).wait_send()

def kernel(
    blocks, groups, reach, table_ref, masses_ref, spins_ref, ph_ref, pp_ref,
    sums, ph_keep, pp_keep, held, held_spins, steps, band, unit, skew, props, fixed,
    shift_ref, recv_sem, send_sem, local_sem,
):
    group = lax.axis_index("grp")
    block = lax.axis_index("blk")
    order = held.shape[-1]
    walkers = held.shape[1]
    trans = sums.shape[0]
    height = order // groups
    lanes = sums.shape[-1]
    f32, bf16 = jnp.float32, jnp.bfloat16
    gather = whole_gather(blocks, groups, reach)
    home = block if gather else 0

    local = [
        pltpu.make_async_copy(masses_ref, held.at[home], local_sem.at[0]),
        pltpu.make_async_copy(spins_ref, held_spins.at[home], local_sem.at[1]),
        pltpu.make_async_copy(ph_ref, ph_keep, local_sem.at[2]),
        pltpu.make_async_copy(pp_ref, pp_keep, local_sem.at[3]),
        pltpu.make_async_copy(table_ref, shift_ref, local_sem.at[4]),
    ]
    if gather:
        plan = Gather(
            group, block, order, walkers, masses_ref, spins_ref, held, held_spins,
            recv_sem, send_sem,
        )
    else:
        plan = Chain(
            group, block, groups, blocks, reach, height, masses_ref, spins_ref, held,
            held_spins, recv_sem, send_sem,
        )
    plan.greet()
    for copy in local:
        copy.start()
    plan.enter()
    plan.begin()

    norm = 1.0 / math.sqrt(NW * NK)
    row = lax.broadcasted_iota(jnp.int32, (NW, order), 0)
    column = lax.broadcasted_iota(jnp.int32, (NW, order), 1)
    slices, sites = column // NK, column % NK

    def circle(numerator):
        turn = angle(numerator % (2 * NW))
        return jnp.cos(turn), jnp.sin(turn)

    site_cos, site_sin = circle(2 * NW * NK - 2 * row * sites)
    odd_cos, odd_sin = circle((2 * row + 1) * slices)
    even_cos, even_sin = circle(2 * row * slices)
    for i in range(NW):
        here = slice(i * NK, (i + 1) * NK)
        c, d = odd_cos[i : i + 1], odd_sin[i : i + 1]
        cos, sin = c * site_cos - d * site_sin, d * site_cos + c * site_sin
        unit[0, here], unit[1, here] = cos, sin
        if i < NW // 2:
            steps[2 * i * NK : (2 * i + 1) * NK] = (cos * norm).astype(bf16)
            steps[(2 * i + 1) * NK : (2 * i + 2) * NK] = (sin * norm).astype(bf16)
        c, d = even_cos[i : i + 1], even_sin[i : i + 1]
        cos, sin = c * site_cos - d * site_sin, d * site_cos + c * site_sin
        for half in range(order // lanes):
            part = slice(half * lanes, (half + 1) * lanes)
            skew[half, here, 0:lanes] = (cos[:, part] * norm).astype(bf16)
            skew[half, here, lanes:] = (sin[:, part] * norm).astype(bf16)
    for i in range(height // NK):
        near = pl.ds(pl.multiple_of(group * height + i * NK, NK), NK)
        band[2 * i * NK : (2 * i + 1) * NK] = (unit[0, near] * norm).astype(bf16)
        band[(2 * i + 1) * NK : (2 * i + 2) * NK] = (unit[1, near] * norm).astype(bf16)
    sums[...] = jnp.zeros(sums.shape, f32)

    def dot(a, b):
        return jnp.dot(a, b, preferred_element_type=f32)

    flip = ROWS - 1 - lax.broadcasted_iota(jnp.int32, (ROWS, lanes), 0)

    def put(s, part, half, i, lower, upper):
        tiles = [lower[r : r + ROWS] for r in range(0, NK, ROWS)]
        for r, tile in enumerate(tiles + tiles[:1]):
            props[s, part, half, i, r * ROWS : (r + 1) * ROWS] = tile
        tiles = [upper[r : r + ROWS] for r in range(0, NK, ROWS)]
        tiles = [jnp.take_along_axis(tile, flip, 0) for tile in tiles[::-1]]
        for r, tile in enumerate(tiles + tiles[:1]):
            props[s, part, half, NW - 1 - i, r * ROWS : (r + 1) * ROWS] = tile

    def from_row(freq, mom):
        mirrored = lax.shift_right_logical(freq, HALF_BITS)
        return pl.ds((mom - mirrored + NK) & (NK - 1), ROWS)

    def absorb(slot, w):
        signed = (2 * held_spins[slot, w : w + 1, :] - 1).astype(f32)
        turned = []
        for s in range(2):
            factor = jnp.exp((COUPLING if s == 0 else -COUPLING) * signed)
            scaled = (held[slot, w, s].astype(f32) * factor).astype(bf16)
            first = dot(steps[...], scaled)
            for i in range(NW // 2):
                real, imag = first[2 * i * NK : (2 * i + 1) * NK], first[(2 * i + 1) * NK : (2 * i + 2) * NK]
                cos, sin = unit[0, i * NK : (i + 1) * NK], unit[1, i * NK : (i + 1) * NK]
                turned += [
                    (real * cos + imag * sin).astype(bf16),
                    (imag * cos - real * sin).astype(bf16),
                ]
            left = lax.dot_general(band[...], scaled, NT, preferred_element_type=f32)
            for i in range(height // NK):
                real, imag = left[2 * i * NK : (2 * i + 1) * NK], left[(2 * i + 1) * NK : (2 * i + 2) * NK]
                near = pl.ds(pl.multiple_of(group * height + i * NK, NK), NK)
                cos, sin = unit[0, near], unit[1, near]
                turned += [
                    (cos * real + sin * imag).astype(bf16),
                    (sin * real - cos * imag).astype(bf16),
                ]
        turned = jnp.concatenate(turned, 0)
        for half in range(order // lanes):
            moving = dot(turned, skew[half])
            first = 0
            for s in range(2):
                for i in range(NW // 2):
                    real, imag = moving[first : first + NK], moving[first + NK : first + 2 * NK]
                    first += 2 * NK
                    c, d, e, f = real[:, :lanes], real[:, lanes:], imag[:, :lanes], imag[:, lanes:]
                    put(s, 0, half, i, c + f, c - f)
                    put(s, 1, half, i, e - d, -e - d)
                for i in range(height // NK):
                    real, imag = moving[first : first + NK], moving[first + NK : first + 2 * NK]
                    first += 2 * NK
                    c, d, e, f = real[:, :lanes], real[:, lanes:], imag[:, :lanes], imag[:, lanes:]
                    fixed[s, 0, half, i * NK : (i + 1) * NK] = c - f
                    fixed[s, 1, half, i * NK : (i + 1) * NK] = -d - e

        @pl.loop(0, trans)
        def _(t):
            start = shift_ref[t, 0]
            freq, mom = lax.shift_right_logical(start, BITS), start & (NK - 1)
            for i in range(height // NK):
                at = group * (height // NK) + i
                up, down = (at + freq) & (NW - 1), (at - freq + NW) & (NW - 1)
                for piece in range(NK // ROWS):
                    rows = i * NK + piece * ROWS
                    place = slice(rows, rows + ROWS)
                    offset = piece * ROWS
                    ahead = from_row(up, mom + offset)
                    behind = from_row(down, NK - mom + offset)
                    own = from_row(at, offset)
                    for half in range(order // lanes):
                        real, imag = sums[t, 0, half, place], sums[t, 1, half, place]
                        for s in range(2):
                            a, b = fixed[s, 0, half, place], fixed[s, 1, half, place]
                            c, d = props[s, 0, half, up, ahead], props[s, 1, half, up, ahead]
                            real = real + (a * c + b * d)
                            imag = imag + (a * d - b * c)
                        sums[t, 0, half, place] = real
                        sums[t, 1, half, place] = imag
                        a, b = props[0, 0, half, at, own], props[0, 1, half, at, own]
                        c, d = props[1, 0, half, down, behind], props[1, 1, half, down, behind]
                        sums[t, 2, half, place] += a * c + b * d
                        sums[t, 3, half, place] += b * c - a * d

    @pl.loop(0, reach + 1)
    def _(k):
        @pl.when(k == 0)
        def _():
            local[0].wait()
            local[1].wait()
            local[4].wait()

        plan.turn(k)
        for w in range(walkers):
            absorb(plan.slot_at(k), w)

    local[2].wait()
    local[3].wait()
    plan.drain()


def leave(groups, sums, ph_keep, pp_keep, ph_out, pp_out, ph_new, pp_new, sem):
    trans, _, _, height, lanes = sums.shape
    group = lax.axis_index("grp")
    row = lax.broadcasted_iota(jnp.int32, (height, lanes), 0)
    lane = lax.broadcasted_iota(jnp.int32, (height, lanes), 1)
    freq = (lane // NK - group * (height // NK) - row // NK + 2 * NW) % NW
    mom = (lane % NK - row % NK + NK) % NK
    source = freq * NK + mom
    index, upper = source % lanes, source >= lanes
    copies = []
    for t in range(trans):
        for keep, new, first in ((ph_keep, ph_new, 0), (pp_keep, pp_new, 2)):
            for part in range(2):
                low, high = [
                    jnp.take_along_axis(sums[t, first + part, half], index, 1) for half in range(2)
                ]
                new[part, t, :, 0:lanes] = keep[part, t, :, 0:lanes] + jnp.where(upper, high, low)
                new[part, t, :, lanes:] = keep[part, t, :, lanes:] + jnp.where(upper, low, high)
        for i, (new, out) in enumerate(((ph_new, ph_out), (pp_new, pp_out))):
            copies.append(pltpu.make_async_copy(new.at[:, t], out.at[:, t], sem.at[t, i]))
            copies[-1].start()
    for copy in copies:
        copy.wait()


def on_device(masses, spins, shift_table, flip_table, ph_in, pp_in):
    groups = lax.axis_size("grp")
    blocks = lax.axis_size("blk")
    reach = min(8, blocks - 1)
    visits = reach + 1
    walkers, _, order, _ = masses.shape
    trans = shift_table.shape[0]
    height = order // groups
    chips = groups // 2
    f32, bf16 = jnp.float32, jnp.bfloat16
    sums_shape = (trans, 4, order // LANES, height, LANES)
    dma = pltpu.SemaphoreType.DMA
    anywhere = pl.BlockSpec(memory_space=pl.ANY)
    if whole_gather(blocks, groups, reach):
        recv_shape, send_shape = (visits, 3), (5,)
    else:
        recv_shape, send_shape = (visits, groups + 1), (visits, 3 + 2 * (chips - 1))
    sums = pl.pallas_call(
        functools.partial(kernel, blocks, groups, reach),
        out_shape=(
            pltpu.VMEM(sums_shape, f32),
            pltpu.VMEM(ph_in.shape, f32),
            pltpu.VMEM(pp_in.shape, f32),
        ),
        in_specs=[pl.BlockSpec(memory_space=pltpu.HBM)] * 5,
        out_specs=(pl.BlockSpec(memory_space=pltpu.VMEM),) * 3,
        scratch_shapes=[
            pltpu.VMEM((visits, walkers, 2, order, order), bf16),
            pltpu.VMEM((visits, walkers, order), jnp.int32),
            pltpu.VMEM((order, order), bf16),
            pltpu.VMEM((2 * height, order), bf16),
            pltpu.VMEM((2, order, order), f32),
            pltpu.VMEM((order // LANES, order, 2 * LANES), bf16),
            pltpu.VMEM((2, 2, order // LANES, NW, NK + ROWS, LANES), f32),
            pltpu.VMEM((2, 2, order // LANES, height, LANES), f32),
            pltpu.SMEM(shift_table.shape, jnp.int32),
            dma(recv_shape),
            dma(send_shape),
            dma((5,)),
        ],
        compiler_params=pltpu.CompilerParams(
            collective_id=0, has_side_effects=True, vmem_limit_bytes=VMEM - 8 * (ph_in.size + pp_in.size) - 65536
        ),
    )(shift_table, masses, spins, ph_in, pp_in)
    return pl.pallas_call(
        functools.partial(leave, groups),
        out_shape=(
            jax.ShapeDtypeStruct(ph_in.shape, f32),
            jax.ShapeDtypeStruct(pp_in.shape, f32),
        ),
        in_specs=[pl.BlockSpec(memory_space=pltpu.VMEM)] * 3,
        out_specs=(anywhere,) * 2,
        scratch_shapes=[
            pltpu.VMEM(ph_in.shape, f32),
            pltpu.VMEM(pp_in.shape, f32),
            dma((trans, 2)),
        ],
        compiler_params=pltpu.CompilerParams(vmem_limit_bytes=16 * 1024 * 1024),
    )(*[pltpu.with_memory_space_constraint(one, pltpu.VMEM) for one in sums])


def solution(mesh):
    placed = (
        P("blk", None, None, None),
        P("blk", None),
        P("blk", None),
        P("blk", None),
        P(None, "blk", "grp", None),
        P(None, "blk", "grp", None),
    )
    return jax.shard_map(
        on_device,
        mesh=mesh,
        in_specs=placed,
        out_specs=(P(None, "blk", "grp", None), P(None, "blk", "grp", None)),
        check_vma=False,
    )
```

```python
import functools
import math

import jax
import jax.numpy as jnp
from jax import lax
from jax.experimental import pallas as pl
from jax.experimental.pallas import tpu as pltpu
from jax.sharding import PartitionSpec as P

NW = 16
NK = 16
COUPLING = 0.5
VMEM = 67043328
LANES = 128
ROWS = 8
HALF_BITS = 3
BITS = 4
MESH = pl.DeviceIdType.MESH
NT = (((1,), (1,)), ((), ()))


def angle(steps):
    return steps.astype(jnp.float32) * (math.pi / NW)


def whole_gather(blocks, groups, reach):
    return blocks == 8 and groups == 4 and reach == 7


def send(src, dst, send_sem, recv_sem, target):
    return pltpu.make_async_remote_copy(
        src_ref=src,
        dst_ref=dst,
        send_sem=send_sem,
        recv_sem=recv_sem,
        device_id=target,
        device_id_type=MESH,
    )


def bulk(view, sem):
    return pltpu.make_async_copy(view, view, sem)


class Gather:
    TURNS = ('', 'H0 O0 I0 O1', 'H1 h0 F0 i0', 'F1 I1', 'h1 f0', 'f1 i1', '', '')
    SLOTS = 'SOHIFhfi'

    def __init__(self, group, block, order, walkers, masses, spins, held, held_spins, recv, sends):
        self.chip, self.core = group // 2, group % 2
        self.block, self.layer, self.side = block, block // 2, block % 2
        self.masses, self.spins = masses, spins
        self.held, self.held_spins = held, held_spins
        self.recv, self.sends = recv, sends
        self.quarter = order // 4
        self.walkers = walkers
        self.end = jnp.logical_or(self.layer == 0, self.layer == 3)
        other = self.chip * 2 + (1 - self.core)
        self.other = other
        self.partner = (other, block)
        self.across = ((1 - self.chip) * 2 + (1 - self.core), block)
        self.beside = (other, self.layer * 2 + (1 - self.side))
        same, mate = self.side, 1 - self.side
        first, second = self.by_layer(1, 3, 0, 2), self.by_layer(2, 2, 1, 1)
        full = self.by_layer(3, 0, 3, 0)
        self.slots = {
            "S": block,
            "O": self.layer * 2 + mate,
            "H": first * 2 + same,
            "I": second * 2 + same,
            "F": full * 2 + same,
            "h": first * 2 + mate,
            "i": second * 2 + mate,
            "f": full * 2 + mate,
        }

    def by_layer(self, *values):
        return sum(
            value * (self.layer == i).astype(jnp.int32) for i, value in enumerate(values)
        )

    def slot_at(self, k):
        return sum(
            self.slots[kind] * (k == i).astype(jnp.int32) for i, kind in enumerate(self.SLOTS)
        )

    def up(self, layer):
        return (self.other, layer * 2 + self.side)

    def others(self):
        return [(self.other, lax.rem(self.block + step, 8)) for step in range(1, 8)]

    def greet(self):
        self.barrier = pltpu.get_barrier_semaphore()
        targets = self.others() + [self.partner, self.across]
        for target in targets:
            pl.semaphore_signal(self.barrier, inc=1, device_id=target, device_id_type=MESH)

    def enter(self):
        pl.semaphore_wait(self.barrier, 9)

    def rows(self, ref, half, parity):
        first = pl.multiple_of((half * 2 + parity) * self.quarter, self.quarter)
        return ref.at[:, :, pl.ds(first, self.quarter)]

    def own(self, part, target):
        half = 1 - self.chip if part else self.chip
        dst = self.rows(self.held.at[self.block], half, 1 - self.core)
        src = self.rows(self.masses, half, 1 - self.core)
        send(src, dst, self.sends.at[0], self.recv.at[self.block, part], target).start()

    def note(self, target):
        return send(self.spins, self.held_spins.at[self.block], self.sends.at[3],
                    self.sends.at[4], target)

    def begin(self):
        for target in self.others():
            self.note(target).start()
        ends = self.by_layer(1, 0, 0, 2), self.by_layer(3, 0, 0, 0)
        inner = self.by_layer(2, 2, 1, 1)
        near_end, far_end = self.by_layer(0, 0, 3, 0), self.by_layer(0, 3, 0, 0)

        @pl.when(self.end)
        def _():
            self.own(0, self.beside)
            self.own(1, self.beside)
            self.own(0, self.up(inner))
            for layer in ends:
                self.own(0, self.up(layer))
                self.own(1, self.up(layer))

        @pl.when(jnp.logical_not(self.end))
        def _():
            self.own(0, self.up(near_end))
            self.own(0, self.up(far_end))
            self.own(0, self.beside)
            self.own(1, self.beside)
            self.own(0, self.up(inner))

    def parity(self, kind, part):
        moved = kind in "fi" if part == 0 else kind in "HIf"
        if kind == "h":
            moved = part == 0
        return 1 - self.core if moved else self.core

    def event(self, kind, part):
        slot = self.slots[kind]
        half = 1 - self.chip if part else self.chip
        view = self.rows(self.held.at[slot], half, self.parity(kind, part))

        def copy(sem, recv, target):
            return send(view, view, self.sends.at[sem], self.recv.at[slot, recv], target)

        copy(1, part, self.partner).wait_recv()
        if kind == "F" or (kind in "HI" and part == 0):
            copy(1, part, self.beside).start()
        if kind in "HIhi" and part == 0:
            copy(1, 1, self.across).start()
        copy(2, 2, self.partner).start()

    def some(self, count):
        return self.held.at[0:count, :, :, 0 : self.quarter]

    def turn(self, k):
        for i, turn in enumerate(self.TURNS):
            if turn:
                @pl.when(k == i)
                def _():
                    for name in turn.split():
                        self.event(name[0], int(name[1]))

        @pl.when(k == 1)
        def _():
            bulk(self.held_spins.at[0:7], self.sends.at[4]).wait()

        @pl.when(k >= 1)
        def _():
            half = self.held.at[0, :, :, 0 : 2 * self.quarter]
            bulk(half, self.recv.at[self.slot_at(k), 2]).wait()

    def drain(self):
        pl.when(self.end)(lambda: bulk(self.some(7), self.sends.at[0]).wait())
        pl.when(jnp.logical_not(self.end))(lambda: bulk(self.some(5), self.sends.at[0]).wait())
        bulk(self.some(8), self.sends.at[1]).wait()
        bulk(self.held.at[0:7, :, :, 0 : 2 * self.quarter], self.sends.at[2]).wait()
        bulk(self.held_spins.at[0:7], self.sends.at[3]).wait()


class Chain:
    def __init__(self, group, block, groups, blocks, reach, height, masses, spins, held,
                 held_spins, recv, sends):
        self.group, self.block = group, block
        self.blocks, self.reach, self.height = blocks, reach, height
        self.groups, self.chips = groups, groups // 2
        self.chip, self.core = group // 2, group % 2
        self.partner = self.chip * 2 + (1 - self.core)
        self.masses, self.spins = masses, spins
        self.held, self.held_spins = held, held_spins
        self.recv, self.sends = recv, sends

    def slot_at(self, k):
        return k

    def far(self, step):
        return lax.rem(self.chip + step, self.chips) * 2 + self.core

    def rows(self, ref, piece):
        first = pl.multiple_of(piece * self.height, self.height)
        return ref.at[:, :, pl.ds(first, self.height)]

    def greet(self):
        self.barrier = pltpu.get_barrier_semaphore()
        blocks = [
            lax.rem(self.block - offset + self.blocks, self.blocks)
            for offset in range(1, self.reach + 1)
        ]
        targets = [(self.group, block) for block in blocks] + [(self.partner, self.block)]
        targets += [(self.far(step), self.block) for step in range(1, self.chips)]
        for target in targets:
            pl.semaphore_signal(self.barrier, inc=1, device_id=target, device_id_type=MESH)

    def enter(self):
        pl.semaphore_wait(self.barrier, self.reach + self.chips)

    def direct(self, offset):
        target = (self.group, lax.rem(self.block + offset, self.blocks))
        return (
            send(
                self.rows(self.masses, self.group),
                self.rows(self.held.at[offset], self.group),
                self.sends.at[offset, 0], self.recv.at[offset, self.group], target,
            ),
            send(
                self.spins, self.held_spins.at[offset],
                self.sends.at[offset, 1], self.recv.at[offset, self.groups], target,
            ),
        )

    def passed(self, offset, piece, target, sem):
        view = self.rows(self.held.at[offset], piece)
        return send(view, view, self.sends.at[offset, sem], self.recv.at[offset, piece],
                    (target, self.block))

    def to_core(self, offset):
        return self.passed(offset, self.group, self.partner, 2)

    def to_far(self, offset, step):
        return self.passed(offset, self.group, self.far(step), 1 + 2 * step)

    def relay(self, offset, step):
        return self.passed(offset, self.far(step), self.partner, 2 + 2 * step)

    def arrival(self, offset, piece):
        return self.passed(offset, piece, self.partner, 2)

    def begin(self):
        for offset in range(1, self.reach + 1):
            for copy in self.direct(offset):
                copy.start()

    def take(self, k):
        self.arrival(k, self.group).wait_recv()
        for step in range(1, self.chips):
            self.to_far(k, step).start()
        self.to_core(k).start()

    def turn(self, k):
        pl.when(k == 0)(lambda: self.take(1))
        pl.when(jnp.logical_and(k >= 1, k < self.reach))(lambda: self.take(k + 1))

        @pl.when(k >= 1)
        def _():
            for step in range(1, self.chips):
                self.arrival(k, self.far(step)).wait_recv()
                self.relay(k, step).start()
            self.arrival(k, self.partner).wait_recv()
            for step in range(1, self.chips):
                piece = lax.rem(self.chip + step, self.chips) * 2 + (1 - self.core)
                self.arrival(k, piece).wait_recv()
            self.direct(k)[1].wait_recv()

    def drain(self):
        for offset in range(1, self.reach + 1):
            for copy in self.direct(offset):
                copy.wait_send()
            self.to_core(offset).wait_send()
            for step in range(1, self.chips):
                self.to_far(offset, step).wait_send()
                self.relay(offset, step).wait_send()

def kernel(
    blocks, groups, reach, table_ref, masses_ref, spins_ref, ph_ref, pp_ref,
    sums, ph_keep, pp_keep, held, held_spins, steps, band, unit, skew, props, fixed,
    shift_ref, recv_sem, send_sem, local_sem,
):
    group = lax.axis_index("grp")
    block = lax.axis_index("blk")
    order = held.shape[-1]
    walkers = held.shape[1]
    trans = sums.shape[0]
    height = order // groups
    lanes = sums.shape[-1]
    f32, bf16 = jnp.float32, jnp.bfloat16
    gather = whole_gather(blocks, groups, reach)
    home = block if gather else 0

    local = [
        pltpu.make_async_copy(masses_ref, held.at[home], local_sem.at[0]),
        pltpu.make_async_copy(spins_ref, held_spins.at[home], local_sem.at[1]),
        pltpu.make_async_copy(ph_ref, ph_keep, local_sem.at[2]),
        pltpu.make_async_copy(pp_ref, pp_keep, local_sem.at[3]),
        pltpu.make_async_copy(table_ref, shift_ref, local_sem.at[4]),
    ]
    if gather:
        plan = Gather(
            group, block, order, walkers, masses_ref, spins_ref, held, held_spins,
            recv_sem, send_sem,
        )
    else:
        plan = Chain(
            group, block, groups, blocks, reach, height, masses_ref, spins_ref, held,
            held_spins, recv_sem, send_sem,
        )
    plan.greet()
    for copy in local:
        copy.start()
    plan.enter()
    plan.begin()

    norm = 1.0 / math.sqrt(NW * NK)
    row = lax.broadcasted_iota(jnp.int32, (NW, order), 0)
    column = lax.broadcasted_iota(jnp.int32, (NW, order), 1)
    slices, sites = column // NK, column % NK

    def circle(numerator):
        turn = angle(numerator % (2 * NW))
        return jnp.cos(turn), jnp.sin(turn)

    site_cos, site_sin = circle(2 * NW * NK - 2 * row * sites)
    odd_cos, odd_sin = circle((2 * row + 1) * slices)
    even_cos, even_sin = circle(2 * row * slices)
    for i in range(NW):
        here = slice(i * NK, (i + 1) * NK)
        c, d = odd_cos[i : i + 1], odd_sin[i : i + 1]
        cos, sin = c * site_cos - d * site_sin, d * site_cos + c * site_sin
        unit[0, here], unit[1, here] = cos, sin
        if i < NW // 2:
            steps[2 * i * NK : (2 * i + 1) * NK] = (cos * norm).astype(bf16)
            steps[(2 * i + 1) * NK : (2 * i + 2) * NK] = (sin * norm).astype(bf16)
        c, d = even_cos[i : i + 1], even_sin[i : i + 1]
        cos, sin = c * site_cos - d * site_sin, d * site_cos + c * site_sin
        for half in range(order // lanes):
            part = slice(half * lanes, (half + 1) * lanes)
            skew[half, here, 0:lanes] = (cos[:, part] * norm).astype(bf16)
            skew[half, here, lanes:] = (sin[:, part] * norm).astype(bf16)
    for i in range(height // NK):
        near = pl.ds(pl.multiple_of(group * height + i * NK, NK), NK)
        band[2 * i * NK : (2 * i + 1) * NK] = (unit[0, near] * norm).astype(bf16)
        band[(2 * i + 1) * NK : (2 * i + 2) * NK] = (unit[1, near] * norm).astype(bf16)
    sums[...] = jnp.zeros(sums.shape, f32)

    def dot(a, b):
        return jnp.dot(a, b, preferred_element_type=f32)

    flip = ROWS - 1 - lax.broadcasted_iota(jnp.int32, (ROWS, lanes), 0)

    def put(s, part, half, i, lower, upper):
        tiles = [lower[r : r + ROWS] for r in range(0, NK, ROWS)]
        for r, tile in enumerate(tiles + tiles[:1]):
            props[s, part, half, i, r * ROWS : (r + 1) * ROWS] = tile
        tiles = [upper[r : r + ROWS] for r in range(0, NK, ROWS)]
        tiles = [jnp.take_along_axis(tile, flip, 0) for tile in tiles[::-1]]
        for r, tile in enumerate(tiles + tiles[:1]):
            props[s, part, half, NW - 1 - i, r * ROWS : (r + 1) * ROWS] = tile

    def from_row(freq, mom):
        mirrored = lax.shift_right_logical(freq, HALF_BITS)
        return pl.ds((mom - mirrored + NK) & (NK - 1), ROWS)

    def absorb(slot, w):
        signed = (2 * held_spins[slot, w : w + 1, :] - 1).astype(f32)
        turned = []
        for s in range(2):
            factor = jnp.exp((COUPLING if s == 0 else -COUPLING) * signed)
            scaled = (held[slot, w, s].astype(f32) * factor).astype(bf16)
            first = dot(steps[...], scaled)
            for i in range(NW // 2):
                real, imag = first[2 * i * NK : (2 * i + 1) * NK], first[(2 * i + 1) * NK : (2 * i + 2) * NK]
                cos, sin = unit[0, i * NK : (i + 1) * NK], unit[1, i * NK : (i + 1) * NK]
                turned += [
                    (real * cos + imag * sin).astype(bf16),
                    (imag * cos - real * sin).astype(bf16),
                ]
            left = lax.dot_general(band[...], scaled, NT, preferred_element_type=f32)
            for i in range(height // NK):
                real, imag = left[2 * i * NK : (2 * i + 1) * NK], left[(2 * i + 1) * NK : (2 * i + 2) * NK]
                near = pl.ds(pl.multiple_of(group * height + i * NK, NK), NK)
                cos, sin = unit[0, near], unit[1, near]
                turned += [
                    (cos * real + sin * imag).astype(bf16),
                    (sin * real - cos * imag).astype(bf16),
                ]
        turned = jnp.concatenate(turned, 0)
        for half in range(order // lanes):
            moving = dot(turned, skew[half])
            first = 0
            for s in range(2):
                for i in range(NW // 2):
                    real, imag = moving[first : first + NK], moving[first + NK : first + 2 * NK]
                    first += 2 * NK
                    c, d, e, f = real[:, :lanes], real[:, lanes:], imag[:, :lanes], imag[:, lanes:]
                    put(s, 0, half, i, c + f, c - f)
                    put(s, 1, half, i, e - d, -e - d)
                for i in range(height // NK):
                    real, imag = moving[first : first + NK], moving[first + NK : first + 2 * NK]
                    first += 2 * NK
                    c, d, e, f = real[:, :lanes], real[:, lanes:], imag[:, :lanes], imag[:, lanes:]
                    fixed[s, 0, half, i * NK : (i + 1) * NK] = c - f
                    fixed[s, 1, half, i * NK : (i + 1) * NK] = -d - e

        @pl.loop(0, trans)
        def _(t):
            start = shift_ref[t, 0]
            freq, mom = lax.shift_right_logical(start, BITS), start & (NK - 1)
            for i in range(height // NK):
                at = group * (height // NK) + i
                up, down = (at + freq) & (NW - 1), (at - freq + NW) & (NW - 1)
                for piece in range(NK // ROWS):
                    rows = i * NK + piece * ROWS
                    place = slice(rows, rows + ROWS)
                    offset = piece * ROWS
                    ahead = from_row(up, mom + offset)
                    behind = from_row(down, NK - mom + offset)
                    own = from_row(at, offset)
                    for half in range(order // lanes):
                        real, imag = sums[t, 0, half, place], sums[t, 1, half, place]
                        for s in range(2):
                            a, b = fixed[s, 0, half, place], fixed[s, 1, half, place]
                            c, d = props[s, 0, half, up, ahead], props[s, 1, half, up, ahead]
                            real = real + (a * c + b * d)
                            imag = imag + (a * d - b * c)
                        sums[t, 0, half, place] = real
                        sums[t, 1, half, place] = imag
                        a, b = props[0, 0, half, at, own], props[0, 1, half, at, own]
                        c, d = props[1, 0, half, down, behind], props[1, 1, half, down, behind]
                        sums[t, 2, half, place] += a * c + b * d
                        sums[t, 3, half, place] += b * c - a * d

    @pl.loop(0, reach + 1)
    def _(k):
        @pl.when(k == 0)
        def _():
            local[0].wait()
            local[1].wait()
            local[4].wait()

        plan.turn(k)
        for w in range(walkers):
            absorb(plan.slot_at(k), w)

    local[2].wait()
    local[3].wait()
    plan.drain()


def leave(groups, sums, ph_keep, pp_keep, ph_out, pp_out, ph_new, pp_new, sem):
    trans, _, _, height, lanes = sums.shape
    group = lax.axis_index("grp")
    row = lax.broadcasted_iota(jnp.int32, (height, lanes), 0)
    lane = lax.broadcasted_iota(jnp.int32, (height, lanes), 1)
    freq = (lane // NK - group * (height // NK) - row // NK + 2 * NW) % NW
    mom = (lane % NK - row % NK + NK) % NK
    source = freq * NK + mom
    index, upper = source % lanes, source >= lanes
    for t in range(trans):
        for i, (keep, new, out) in enumerate(((ph_keep, ph_new, ph_out), (pp_keep, pp_new, pp_out))):
            for part in range(2):
                low, high = [
                    jnp.take_along_axis(sums[t, 2 * i + part, half], index, 1)
                    for half in range(2)
                ]
                new[part, t, :, 0:lanes] = keep[part, t, :, 0:lanes] + jnp.where(upper, high, low)
                new[part, t, :, lanes:] = keep[part, t, :, lanes:] + jnp.where(upper, low, high)
                pltpu.make_async_copy(new.at[part, t], out.at[part, t], sem.at[i]).start()
    for i, (new, out) in enumerate(((ph_new, ph_out), (pp_new, pp_out))):
        pltpu.make_async_copy(new, out, sem.at[i]).wait()


def on_device(masses, spins, shift_table, flip_table, ph_in, pp_in):
    groups = lax.axis_size("grp")
    blocks = lax.axis_size("blk")
    reach = min(8, blocks - 1)
    visits = reach + 1
    walkers, _, order, _ = masses.shape
    trans = shift_table.shape[0]
    height = order // groups
    chips = groups // 2
    f32, bf16 = jnp.float32, jnp.bfloat16
    sums_shape = (trans, 4, order // LANES, height, LANES)
    dma = pltpu.SemaphoreType.DMA
    anywhere = pl.BlockSpec(memory_space=pl.ANY)
    if whole_gather(blocks, groups, reach):
        recv_shape, send_shape = (visits, 3), (5,)
    else:
        recv_shape, send_shape = (visits, groups + 1), (visits, 3 + 2 * (chips - 1))
    sums = pl.pallas_call(
        functools.partial(kernel, blocks, groups, reach),
        out_shape=(
            pltpu.VMEM(sums_shape, f32),
            pltpu.VMEM(ph_in.shape, f32),
            pltpu.VMEM(pp_in.shape, f32),
        ),
        in_specs=[pl.BlockSpec(memory_space=pltpu.HBM)] * 5,
        out_specs=(pl.BlockSpec(memory_space=pltpu.VMEM),) * 3,
        scratch_shapes=[
            pltpu.VMEM((visits, walkers, 2, order, order), bf16),
            pltpu.VMEM((visits, walkers, order), jnp.int32),
            pltpu.VMEM((order, order), bf16),
            pltpu.VMEM((2 * height, order), bf16),
            pltpu.VMEM((2, order, order), f32),
            pltpu.VMEM((order // LANES, order, 2 * LANES), bf16),
            pltpu.VMEM((2, 2, order // LANES, NW, NK + ROWS, LANES), f32),
            pltpu.VMEM((2, 2, order // LANES, height, LANES), f32),
            pltpu.SMEM(shift_table.shape, jnp.int32),
            dma(recv_shape),
            dma(send_shape),
            dma((5,)),
        ],
        compiler_params=pltpu.CompilerParams(
            collective_id=0, has_side_effects=True, vmem_limit_bytes=VMEM - 8 * (ph_in.size + pp_in.size) - 65536
        ),
    )(shift_table, masses, spins, ph_in, pp_in)
    return pl.pallas_call(
        functools.partial(leave, groups),
        out_shape=(
            jax.ShapeDtypeStruct(ph_in.shape, f32),
            jax.ShapeDtypeStruct(pp_in.shape, f32),
        ),
        in_specs=[pl.BlockSpec(memory_space=pltpu.VMEM)] * 3,
        out_specs=(anywhere,) * 2,
        scratch_shapes=[
            pltpu.VMEM(ph_in.shape, f32),
            pltpu.VMEM(pp_in.shape, f32),
            dma((2,)),
        ],
        compiler_params=pltpu.CompilerParams(vmem_limit_bytes=16 * 1024 * 1024),
    )(*[pltpu.with_memory_space_constraint(one, pltpu.VMEM) for one in sums])


def solution(mesh):
    placed = (
        P("blk", None, None, None),
        P("blk", None),
        P("blk", None),
        P("blk", None),
        P(None, "blk", "grp", None),
        P(None, "blk", "grp", None),
    )
    return jax.shard_map(
        on_device,
        mesh=mesh,
        in_specs=placed,
        out_specs=(P(None, "blk", "grp", None), P(None, "blk", "grp", None)),
        check_vma=False,
    )
```

```python
import functools
import math

import jax
import jax.numpy as jnp
from jax import lax
from jax.experimental import pallas as pl
from jax.experimental.pallas import tpu as pltpu
from jax.sharding import PartitionSpec as P

NW = 16
NK = 16
COUPLING = 0.5
VMEM = 67043328
LANES = 128
ROWS = 8
HALF_BITS = 3
BITS = 4
MESH = pl.DeviceIdType.MESH
NT = (((1,), (1,)), ((), ()))


def angle(steps):
    return steps.astype(jnp.float32) * (math.pi / NW)


def whole_gather(blocks, groups, reach):
    return blocks == 8 and groups == 4 and reach == 7


def send(src, dst, send_sem, recv_sem, target):
    return pltpu.make_async_remote_copy(
        src_ref=src,
        dst_ref=dst,
        send_sem=send_sem,
        recv_sem=recv_sem,
        device_id=target,
        device_id_type=MESH,
    )


def bulk(view, sem):
    return pltpu.make_async_copy(view, view, sem)


class Gather:
    TURNS = ('', 'H0 O0 I0 O1', 'H1 h0 F0 i0', 'F1 I1', 'h1 f0', 'f1 i1', '', '')
    SLOTS = 'SOHIFhfi'

    def __init__(self, group, block, order, walkers, masses, spins, held, held_spins, recv, sends):
        self.chip, self.core = group // 2, group % 2
        self.block, self.layer, self.side = block, block // 2, block % 2
        self.masses, self.spins = masses, spins
        self.held, self.held_spins = held, held_spins
        self.recv, self.sends = recv, sends
        self.quarter = order // 4
        self.walkers = walkers
        self.end = jnp.logical_or(self.layer == 0, self.layer == 3)
        other = self.chip * 2 + (1 - self.core)
        self.other = other
        self.partner = (other, block)
        self.across = ((1 - self.chip) * 2 + (1 - self.core), block)
        self.beside = (other, self.layer * 2 + (1 - self.side))
        same, mate = self.side, 1 - self.side
        first, second = self.by_layer(1, 3, 0, 2), self.by_layer(2, 2, 1, 1)
        full = self.by_layer(3, 0, 3, 0)
        self.slots = {
            "S": block,
            "O": self.layer * 2 + mate,
            "H": first * 2 + same,
            "I": second * 2 + same,
            "F": full * 2 + same,
            "h": first * 2 + mate,
            "i": second * 2 + mate,
            "f": full * 2 + mate,
        }

    def by_layer(self, *values):
        return sum(
            value * (self.layer == i).astype(jnp.int32) for i, value in enumerate(values)
        )

    def slot_at(self, k):
        return sum(
            self.slots[kind] * (k == i).astype(jnp.int32) for i, kind in enumerate(self.SLOTS)
        )

    def up(self, layer):
        return (self.other, layer * 2 + self.side)

    def others(self):
        return [(self.other, lax.rem(self.block + step, 8)) for step in range(1, 8)]

    def greet(self):
        self.barrier = pltpu.get_barrier_semaphore()
        targets = self.others() + [self.partner, self.across]
        for target in targets:
            pl.semaphore_signal(self.barrier, inc=1, device_id=target, device_id_type=MESH)

    def enter(self):
        pl.semaphore_wait(self.barrier, 9)

    def rows(self, ref, half, parity):
        first = pl.multiple_of((half * 2 + parity) * self.quarter, self.quarter)
        return ref.at[:, :, pl.ds(first, self.quarter)]

    def own(self, part, target):
        half = 1 - self.chip if part else self.chip
        dst = self.rows(self.held.at[self.block], half, 1 - self.core)
        src = self.rows(self.masses, half, 1 - self.core)
        send(src, dst, self.sends.at[0], self.recv.at[self.block, part], target).start()

    def note(self, target):
        return send(self.spins, self.held_spins.at[self.block], self.sends.at[2],
                    self.sends.at[3], target)

    def begin(self):
        for target in self.others():
            self.note(target).start()
        ends = self.by_layer(1, 0, 0, 2), self.by_layer(3, 0, 0, 0)
        inner = self.by_layer(2, 2, 1, 1)
        near_end, far_end = self.by_layer(0, 0, 3, 0), self.by_layer(0, 3, 0, 0)

        @pl.when(self.end)
        def _():
            self.own(0, self.beside)
            self.own(1, self.beside)
            self.own(0, self.up(inner))
            for layer in ends:
                self.own(0, self.up(layer))
                self.own(1, self.up(layer))

        @pl.when(jnp.logical_not(self.end))
        def _():
            self.own(0, self.up(near_end))
            self.own(0, self.up(far_end))
            self.own(0, self.beside)
            self.own(1, self.beside)
            self.own(0, self.up(inner))

    def parity(self, kind, part):
        moved = kind in "fi" if part == 0 else kind in "HIf"
        if kind == "h":
            moved = part == 0
        return 1 - self.core if moved else self.core

    def event(self, kind, part):
        slot = self.slots[kind]
        half = 1 - self.chip if part else self.chip
        view = self.rows(self.held.at[slot], half, self.parity(kind, part))

        def copy(sem, recv, target):
            return send(view, view, self.sends.at[sem], self.recv.at[slot, recv], target)

        copy(1, part, self.partner).wait_recv()
        if kind == "F" or (kind in "HI" and part == 0):
            copy(1, part, self.beside).start()
        if kind in "HIhi" and part == 0:
            copy(1, 1, self.across).start()
        copy(1, 2, self.partner).start()

    def some(self, count):
        return self.held.at[0:count, :, :, 0 : self.quarter]

    def turn(self, k):
        for i, turn in enumerate(self.TURNS):
            if turn:
                @pl.when(k == i)
                def _():
                    for name in turn.split():
                        self.event(name[0], int(name[1]))

        @pl.when(k == 1)
        def _():
            bulk(self.held_spins.at[0:7], self.sends.at[3]).wait()

        @pl.when(k >= 1)
        def _():
            half = self.held.at[0, :, :, 0 : 2 * self.quarter]
            bulk(half, self.recv.at[self.slot_at(k), 2]).wait()

    def drain(self):
        pl.when(self.end)(lambda: bulk(self.some(7), self.sends.at[0]).wait())
        pl.when(jnp.logical_not(self.end))(lambda: bulk(self.some(5), self.sends.at[0]).wait())
        bulk(self.held.at[:, :, :, 0 : 11 * self.quarter // 4], self.sends.at[1]).wait()
        bulk(self.held_spins.at[0:7], self.sends.at[2]).wait()


class Chain:
    def __init__(self, group, block, groups, blocks, reach, height, masses, spins, held,
                 held_spins, recv, sends):
        self.group, self.block = group, block
        self.blocks, self.reach, self.height = blocks, reach, height
        self.groups, self.chips = groups, groups // 2
        self.chip, self.core = group // 2, group % 2
        self.partner = self.chip * 2 + (1 - self.core)
        self.masses, self.spins = masses, spins
        self.held, self.held_spins = held, held_spins
        self.recv, self.sends = recv, sends

    def slot_at(self, k):
        return k

    def far(self, step):
        return lax.rem(self.chip + step, self.chips) * 2 + self.core

    def rows(self, ref, piece):
        first = pl.multiple_of(piece * self.height, self.height)
        return ref.at[:, :, pl.ds(first, self.height)]

    def greet(self):
        self.barrier = pltpu.get_barrier_semaphore()
        blocks = [
            lax.rem(self.block - offset + self.blocks, self.blocks)
            for offset in range(1, self.reach + 1)
        ]
        targets = [(self.group, block) for block in blocks] + [(self.partner, self.block)]
        targets += [(self.far(step), self.block) for step in range(1, self.chips)]
        for target in targets:
            pl.semaphore_signal(self.barrier, inc=1, device_id=target, device_id_type=MESH)

    def enter(self):
        pl.semaphore_wait(self.barrier, self.reach + self.chips)

    def direct(self, offset):
        target = (self.group, lax.rem(self.block + offset, self.blocks))
        return (
            send(
                self.rows(self.masses, self.group),
                self.rows(self.held.at[offset], self.group),
                self.sends.at[offset, 0], self.recv.at[offset, self.group], target,
            ),
            send(
                self.spins, self.held_spins.at[offset],
                self.sends.at[offset, 1], self.recv.at[offset, self.groups], target,
            ),
        )

    def passed(self, offset, piece, target, sem):
        view = self.rows(self.held.at[offset], piece)
        return send(view, view, self.sends.at[offset, sem], self.recv.at[offset, piece],
                    (target, self.block))

    def to_core(self, offset):
        return self.passed(offset, self.group, self.partner, 2)

    def to_far(self, offset, step):
        return self.passed(offset, self.group, self.far(step), 1 + 2 * step)

    def relay(self, offset, step):
        return self.passed(offset, self.far(step), self.partner, 2 + 2 * step)

    def arrival(self, offset, piece):
        return self.passed(offset, piece, self.partner, 2)

    def begin(self):
        for offset in range(1, self.reach + 1):
            for copy in self.direct(offset):
                copy.start()

    def take(self, k):
        self.arrival(k, self.group).wait_recv()
        for step in range(1, self.chips):
            self.to_far(k, step).start()
        self.to_core(k).start()

    def turn(self, k):
        pl.when(k == 0)(lambda: self.take(1))
        pl.when(jnp.logical_and(k >= 1, k < self.reach))(lambda: self.take(k + 1))

        @pl.when(k >= 1)
        def _():
            for step in range(1, self.chips):
                self.arrival(k, self.far(step)).wait_recv()
                self.relay(k, step).start()
            self.arrival(k, self.partner).wait_recv()
            for step in range(1, self.chips):
                piece = lax.rem(self.chip + step, self.chips) * 2 + (1 - self.core)
                self.arrival(k, piece).wait_recv()
            self.direct(k)[1].wait_recv()

    def drain(self):
        for offset in range(1, self.reach + 1):
            for copy in self.direct(offset):
                copy.wait_send()
            self.to_core(offset).wait_send()
            for step in range(1, self.chips):
                self.to_far(offset, step).wait_send()
                self.relay(offset, step).wait_send()

def kernel(
    blocks, groups, reach, table_ref, masses_ref, spins_ref, ph_ref, pp_ref,
    sums, ph_keep, pp_keep, held, held_spins, steps, band, unit, skew, props, fixed,
    shift_ref, recv_sem, send_sem, local_sem,
):
    group = lax.axis_index("grp")
    block = lax.axis_index("blk")
    order = held.shape[-1]
    walkers = held.shape[1]
    trans = sums.shape[0]
    height = order // groups
    lanes = sums.shape[-1]
    f32, bf16 = jnp.float32, jnp.bfloat16
    gather = whole_gather(blocks, groups, reach)
    home = block if gather else 0

    local = [
        pltpu.make_async_copy(masses_ref, held.at[home], local_sem.at[0]),
        pltpu.make_async_copy(spins_ref, held_spins.at[home], local_sem.at[1]),
        pltpu.make_async_copy(ph_ref, ph_keep, local_sem.at[2]),
        pltpu.make_async_copy(pp_ref, pp_keep, local_sem.at[3]),
        pltpu.make_async_copy(table_ref, shift_ref, local_sem.at[4]),
    ]
    if gather:
        plan = Gather(
            group, block, order, walkers, masses_ref, spins_ref, held, held_spins,
            recv_sem, send_sem,
        )
    else:
        plan = Chain(
            group, block, groups, blocks, reach, height, masses_ref, spins_ref, held,
            held_spins, recv_sem, send_sem,
        )
    plan.greet()
    for copy in local:
        copy.start()
    plan.enter()
    plan.begin()

    norm = 1.0 / math.sqrt(NW * NK)
    row = lax.broadcasted_iota(jnp.int32, (NW, order), 0)
    column = lax.broadcasted_iota(jnp.int32, (NW, order), 1)
    slices, sites = column // NK, column % NK

    def circle(numerator):
        turn = angle(numerator % (2 * NW))
        return jnp.cos(turn), jnp.sin(turn)

    site_cos, site_sin = circle(2 * NW * NK - 2 * row * sites)
    odd_cos, odd_sin = circle((2 * row + 1) * slices)
    even_cos, even_sin = circle(2 * row * slices)
    for i in range(NW):
        here = slice(i * NK, (i + 1) * NK)
        c, d = odd_cos[i : i + 1], odd_sin[i : i + 1]
        cos, sin = c * site_cos - d * site_sin, d * site_cos + c * site_sin
        unit[0, here], unit[1, here] = cos, sin
        if i < NW // 2:
            steps[2 * i * NK : (2 * i + 1) * NK] = (cos * norm).astype(bf16)
            steps[(2 * i + 1) * NK : (2 * i + 2) * NK] = (sin * norm).astype(bf16)
        c, d = even_cos[i : i + 1], even_sin[i : i + 1]
        cos, sin = c * site_cos - d * site_sin, d * site_cos + c * site_sin
        for half in range(order // lanes):
            part = slice(half * lanes, (half + 1) * lanes)
            skew[half, here, 0:lanes] = (cos[:, part] * norm).astype(bf16)
            skew[half, here, lanes:] = (sin[:, part] * norm).astype(bf16)
    for i in range(height // NK):
        near = pl.ds(pl.multiple_of(group * height + i * NK, NK), NK)
        band[2 * i * NK : (2 * i + 1) * NK] = (unit[0, near] * norm).astype(bf16)
        band[(2 * i + 1) * NK : (2 * i + 2) * NK] = (unit[1, near] * norm).astype(bf16)
    sums[...] = jnp.zeros(sums.shape, f32)

    def dot(a, b):
        return jnp.dot(a, b, preferred_element_type=f32)

    flip = ROWS - 1 - lax.broadcasted_iota(jnp.int32, (ROWS, lanes), 0)

    def put(s, part, half, i, lower, upper):
        tiles = [lower[r : r + ROWS] for r in range(0, NK, ROWS)]
        for r, tile in enumerate(tiles + tiles[:1]):
            props[s, part, half, i, r * ROWS : (r + 1) * ROWS] = tile
        tiles = [upper[r : r + ROWS] for r in range(0, NK, ROWS)]
        tiles = [jnp.take_along_axis(tile, flip, 0) for tile in tiles[::-1]]
        for r, tile in enumerate(tiles + tiles[:1]):
            props[s, part, half, NW - 1 - i, r * ROWS : (r + 1) * ROWS] = tile

    def from_row(freq, mom):
        mirrored = lax.shift_right_logical(freq, HALF_BITS)
        return pl.ds((mom - mirrored + NK) & (NK - 1), ROWS)

    def absorb(slot, w):
        signed = (2 * held_spins[slot, w : w + 1, :] - 1).astype(f32)
        turned = []
        for s in range(2):
            factor = jnp.exp((COUPLING if s == 0 else -COUPLING) * signed)
            scaled = (held[slot, w, s].astype(f32) * factor).astype(bf16)
            first = dot(steps[...], scaled)
            for i in range(NW // 2):
                real, imag = first[2 * i * NK : (2 * i + 1) * NK], first[(2 * i + 1) * NK : (2 * i + 2) * NK]
                cos, sin = unit[0, i * NK : (i + 1) * NK], unit[1, i * NK : (i + 1) * NK]
                turned += [
                    (real * cos + imag * sin).astype(bf16),
                    (imag * cos - real * sin).astype(bf16),
                ]
            left = lax.dot_general(band[...], scaled, NT, preferred_element_type=f32)
            for i in range(height // NK):
                real, imag = left[2 * i * NK : (2 * i + 1) * NK], left[(2 * i + 1) * NK : (2 * i + 2) * NK]
                near = pl.ds(pl.multiple_of(group * height + i * NK, NK), NK)
                cos, sin = unit[0, near], unit[1, near]
                turned += [
                    (cos * real + sin * imag).astype(bf16),
                    (sin * real - cos * imag).astype(bf16),
                ]
        turned = jnp.concatenate(turned, 0)
        for half in range(order // lanes):
            moving = dot(turned, skew[half])
            first = 0
            for s in range(2):
                for i in range(NW // 2):
                    real, imag = moving[first : first + NK], moving[first + NK : first + 2 * NK]
                    first += 2 * NK
                    c, d, e, f = real[:, :lanes], real[:, lanes:], imag[:, :lanes], imag[:, lanes:]
                    put(s, 0, half, i, c + f, c - f)
                    put(s, 1, half, i, e - d, -e - d)
                for i in range(height // NK):
                    real, imag = moving[first : first + NK], moving[first + NK : first + 2 * NK]
                    first += 2 * NK
                    c, d, e, f = real[:, :lanes], real[:, lanes:], imag[:, :lanes], imag[:, lanes:]
                    fixed[s, 0, half, i * NK : (i + 1) * NK] = c - f
                    fixed[s, 1, half, i * NK : (i + 1) * NK] = -d - e

        @pl.loop(0, trans, unroll=2)
        def _(t):
            start = shift_ref[t, 0]
            freq, mom = lax.shift_right_logical(start, BITS), start & (NK - 1)
            for i in range(height // NK):
                at = group * (height // NK) + i
                up, down = (at + freq) & (NW - 1), (at - freq + NW) & (NW - 1)
                for piece in range(NK // ROWS):
                    rows = i * NK + piece * ROWS
                    place = slice(rows, rows + ROWS)
                    offset = piece * ROWS
                    ahead = from_row(up, mom + offset)
                    behind = from_row(down, NK - mom + offset)
                    own = from_row(at, offset)
                    for half in range(order // lanes):
                        real, imag = sums[t, 0, half, place], sums[t, 1, half, place]
                        for s in range(2):
                            a, b = fixed[s, 0, half, place], fixed[s, 1, half, place]
                            c, d = props[s, 0, half, up, ahead], props[s, 1, half, up, ahead]
                            real = real + (a * c + b * d)
                            imag = imag + (a * d - b * c)
                        sums[t, 0, half, place] = real
                        sums[t, 1, half, place] = imag
                        a, b = props[0, 0, half, at, own], props[0, 1, half, at, own]
                        c, d = props[1, 0, half, down, behind], props[1, 1, half, down, behind]
                        sums[t, 2, half, place] += a * c + b * d
                        sums[t, 3, half, place] += b * c - a * d

    @pl.loop(0, reach + 1)
    def _(k):
        @pl.when(k == 0)
        def _():
            local[0].wait()
            local[1].wait()
            local[4].wait()

        plan.turn(k)
        for w in range(walkers):
            absorb(plan.slot_at(k), w)

    local[2].wait()
    local[3].wait()
    plan.drain()


def leave(groups, sums, ph_keep, pp_keep, ph_out, pp_out, ph_new, pp_new, sem):
    trans, _, _, height, lanes = sums.shape
    group = lax.axis_index("grp")
    row = lax.broadcasted_iota(jnp.int32, (height, lanes), 0)
    lane = lax.broadcasted_iota(jnp.int32, (height, lanes), 1)
    freq = (lane // NK - group * (height // NK) - row // NK + 2 * NW) % NW
    mom = (lane % NK - row % NK + NK) % NK
    source = freq * NK + mom
    index, upper = source % lanes, source >= lanes
    for t in range(trans):
        for i, (keep, new, out) in enumerate(((ph_keep, ph_new, ph_out), (pp_keep, pp_new, pp_out))):
            for part in range(2):
                low, high = [
                    jnp.take_along_axis(sums[t, 2 * i + part, half], index, 1)
                    for half in range(2)
                ]
                new[part, t, :, 0:lanes] = keep[part, t, :, 0:lanes] + jnp.where(upper, high, low)
                new[part, t, :, lanes:] = keep[part, t, :, lanes:] + jnp.where(upper, low, high)
                pltpu.make_async_copy(new.at[part, t], out.at[part, t], sem.at[i]).start()
    for i, (new, out) in enumerate(((ph_new, ph_out), (pp_new, pp_out))):
        pltpu.make_async_copy(new, out, sem.at[i]).wait()


def on_device(masses, spins, shift_table, flip_table, ph_in, pp_in):
    groups = lax.axis_size("grp")
    blocks = lax.axis_size("blk")
    reach = min(8, blocks - 1)
    visits = reach + 1
    walkers, _, order, _ = masses.shape
    trans = shift_table.shape[0]
    height = order // groups
    chips = groups // 2
    f32, bf16 = jnp.float32, jnp.bfloat16
    sums_shape = (trans, 4, order // LANES, height, LANES)
    dma = pltpu.SemaphoreType.DMA
    anywhere = pl.BlockSpec(memory_space=pl.ANY)
    if whole_gather(blocks, groups, reach):
        recv_shape, send_shape = (visits, 3), (4,)
    else:
        recv_shape, send_shape = (visits, groups + 1), (visits, 3 + 2 * (chips - 1))
    sums = pl.pallas_call(
        functools.partial(kernel, blocks, groups, reach),
        out_shape=(
            pltpu.VMEM(sums_shape, f32),
            pltpu.VMEM(ph_in.shape, f32),
            pltpu.VMEM(pp_in.shape, f32),
        ),
        in_specs=[pl.BlockSpec(memory_space=pltpu.HBM)] * 5,
        out_specs=(pl.BlockSpec(memory_space=pltpu.VMEM),) * 3,
        scratch_shapes=[
            pltpu.VMEM((visits, walkers, 2, order, order), bf16),
            pltpu.VMEM((visits, walkers, order), jnp.int32),
            pltpu.VMEM((order, order), bf16),
            pltpu.VMEM((2 * height, order), bf16),
            pltpu.VMEM((2, order, order), f32),
            pltpu.VMEM((order // LANES, order, 2 * LANES), bf16),
            pltpu.VMEM((2, 2, order // LANES, NW, NK + ROWS, LANES), f32),
            pltpu.VMEM((2, 2, order // LANES, height, LANES), f32),
            pltpu.SMEM(shift_table.shape, jnp.int32),
            dma(recv_shape),
            dma(send_shape),
            dma((5,)),
        ],
        compiler_params=pltpu.CompilerParams(
            collective_id=0, has_side_effects=True, vmem_limit_bytes=VMEM - 8 * (ph_in.size + pp_in.size) - 65536
        ),
    )(shift_table, masses, spins, ph_in, pp_in)
    return pl.pallas_call(
        functools.partial(leave, groups),
        out_shape=(
            jax.ShapeDtypeStruct(ph_in.shape, f32),
            jax.ShapeDtypeStruct(pp_in.shape, f32),
        ),
        in_specs=[pl.BlockSpec(memory_space=pltpu.VMEM)] * 3,
        out_specs=(anywhere,) * 2,
        scratch_shapes=[
            pltpu.VMEM(ph_in.shape, f32),
            pltpu.VMEM(pp_in.shape, f32),
            dma((2,)),
        ],
        compiler_params=pltpu.CompilerParams(vmem_limit_bytes=16 * 1024 * 1024),
    )(*[pltpu.with_memory_space_constraint(one, pltpu.VMEM) for one in sums])


def solution(mesh):
    placed = (
        P("blk", None, None, None),
        P("blk", None),
        P("blk", None),
        P("blk", None),
        P(None, "blk", "grp", None),
        P(None, "blk", "grp", None),
    )
    return jax.shard_map(
        on_device,
        mesh=mesh,
        in_specs=placed,
        out_specs=(P(None, "blk", "grp", None), P(None, "blk", "grp", None)),
        check_vma=False,
    )
```

```python
import functools
import math

import jax
import jax.numpy as jnp
from jax import lax
from jax.experimental import pallas as pl
from jax.experimental.pallas import tpu as pltpu
from jax.sharding import PartitionSpec as P

NW = 16
NK = 16
COUPLING = 0.5
VMEM = 67043328
LANES = 128
ROWS = 8
HALF_BITS = 3
BITS = 4
MESH = pl.DeviceIdType.MESH
NT = (((1,), (1,)), ((), ()))


def angle(steps):
    return steps.astype(jnp.float32) * (math.pi / NW)


def whole_gather(blocks, groups, reach):
    return blocks == 8 and groups == 4 and reach == 7


def send(src, dst, send_sem, recv_sem, target):
    return pltpu.make_async_remote_copy(
        src_ref=src,
        dst_ref=dst,
        send_sem=send_sem,
        recv_sem=recv_sem,
        device_id=target,
        device_id_type=MESH,
    )


def bulk(view, sem):
    return pltpu.make_async_copy(view, view, sem)


class Gather:
    TURNS = ('', 'H0 O0 I0 O1', 'H1 h0 F0 i0', 'F1 I1', 'h1 f0', 'f1 i1', '', '')
    SLOTS = 'SOHIFhfi'

    def __init__(self, group, block, order, walkers, masses, spins, held, held_spins, recv, sends):
        self.chip, self.core = group // 2, group % 2
        self.block, self.layer, self.side = block, block // 2, block % 2
        self.masses, self.spins = masses, spins
        self.held, self.held_spins = held, held_spins
        self.recv, self.sends = recv, sends
        self.quarter = order // 4
        self.walkers = walkers
        self.end = jnp.logical_or(self.layer == 0, self.layer == 3)
        other = self.chip * 2 + (1 - self.core)
        self.other = other
        self.partner = (other, block)
        self.across = ((1 - self.chip) * 2 + (1 - self.core), block)
        self.beside = (other, self.layer * 2 + (1 - self.side))
        same, mate = self.side, 1 - self.side
        first, second = self.by_layer(1, 3, 0, 2), self.by_layer(2, 2, 1, 1)
        full = self.by_layer(3, 0, 3, 0)
        self.slots = {
            "S": block,
            "O": self.layer * 2 + mate,
            "H": first * 2 + same,
            "I": second * 2 + same,
            "F": full * 2 + same,
            "h": first * 2 + mate,
            "i": second * 2 + mate,
            "f": full * 2 + mate,
        }

    def by_layer(self, *values):
        return sum(
            value * (self.layer == i).astype(jnp.int32) for i, value in enumerate(values)
        )

    def slot_at(self, k):
        return sum(
            self.slots[kind] * (k == i).astype(jnp.int32) for i, kind in enumerate(self.SLOTS)
        )

    def up(self, layer):
        return (self.other, layer * 2 + self.side)

    def others(self):
        return [(self.other, lax.rem(self.block + step, 8)) for step in range(1, 8)]

    def greet(self):
        self.barrier = pltpu.get_barrier_semaphore()
        targets = [self.across] + self.others()[::-1] + [self.partner]
        for target in targets:
            pl.semaphore_signal(self.barrier, inc=1, device_id=target, device_id_type=MESH)

    def enter(self):
        pl.semaphore_wait(self.barrier, 9)

    def rows(self, ref, half, parity):
        first = pl.multiple_of((half * 2 + parity) * self.quarter, self.quarter)
        return ref.at[:, :, pl.ds(first, self.quarter)]

    def own(self, part, target):
        half = 1 - self.chip if part else self.chip
        dst = self.rows(self.held.at[self.block], half, 1 - self.core)
        src = self.rows(self.masses, half, 1 - self.core)
        send(src, dst, self.sends.at[0], self.recv.at[self.block, part], target).start()

    def note(self, target):
        return send(self.spins, self.held_spins.at[self.block], self.sends.at[3],
                    self.sends.at[4], target)

    def begin(self):
        for target in self.others():
            self.note(target).start()
        ends = self.by_layer(1, 0, 0, 2), self.by_layer(3, 0, 0, 0)
        inner = self.by_layer(2, 2, 1, 1)
        near_end, far_end = self.by_layer(0, 0, 3, 0), self.by_layer(0, 3, 0, 0)

        @pl.when(self.end)
        def _():
            self.own(0, self.beside)
            self.own(1, self.beside)
            self.own(0, self.up(inner))
            for layer in ends:
                self.own(0, self.up(layer))
                self.own(1, self.up(layer))

        @pl.when(jnp.logical_not(self.end))
        def _():
            self.own(0, self.up(near_end))
            self.own(0, self.up(far_end))
            self.own(0, self.beside)
            self.own(1, self.beside)
            self.own(0, self.up(inner))

    def parity(self, kind, part):
        moved = kind in "fi" if part == 0 else kind in "HIf"
        if kind == "h":
            moved = part == 0
        return 1 - self.core if moved else self.core

    def event(self, kind, part):
        slot = self.slots[kind]
        half = 1 - self.chip if part else self.chip
        view = self.rows(self.held.at[slot], half, self.parity(kind, part))

        def copy(sem, recv, target):
            return send(view, view, self.sends.at[sem], self.recv.at[slot, recv], target)

        copy(1, part, self.partner).wait_recv()
        if kind == "F" or (kind in "HI" and part == 0):
            copy(1, part, self.beside).start()
        if kind in "HIhi" and part == 0:
            copy(1, 1, self.across).start()
        copy(2, 2, self.partner).start()

    def some(self, count):
        return self.held.at[0:count, :, :, 0 : self.quarter]

    def turn(self, k):
        for i, turn in enumerate(self.TURNS):
            if turn:
                @pl.when(k == i)
                def _():
                    for name in turn.split():
                        self.event(name[0], int(name[1]))

        @pl.when(k == 1)
        def _():
            bulk(self.held_spins.at[0:7], self.sends.at[4]).wait()

        @pl.when(k >= 1)
        def _():
            half = self.held.at[0, :, :, 0 : 2 * self.quarter]
            bulk(half, self.recv.at[self.slot_at(k), 2]).wait()

    def drain(self):
        pl.when(self.end)(lambda: bulk(self.some(7), self.sends.at[0]).wait())
        pl.when(jnp.logical_not(self.end))(lambda: bulk(self.some(5), self.sends.at[0]).wait())
        bulk(self.some(8), self.sends.at[1]).wait()
        bulk(self.held.at[0:7, :, :, 0 : 2 * self.quarter], self.sends.at[2]).wait()
        bulk(self.held_spins.at[0:7], self.sends.at[3]).wait()


class Chain:
    def __init__(self, group, block, groups, blocks, reach, height, masses, spins, held,
                 held_spins, recv, sends):
        self.group, self.block = group, block
        self.blocks, self.reach, self.height = blocks, reach, height
        self.groups, self.chips = groups, groups // 2
        self.chip, self.core = group // 2, group % 2
        self.partner = self.chip * 2 + (1 - self.core)
        self.masses, self.spins = masses, spins
        self.held, self.held_spins = held, held_spins
        self.recv, self.sends = recv, sends

    def slot_at(self, k):
        return k

    def far(self, step):
        return lax.rem(self.chip + step, self.chips) * 2 + self.core

    def rows(self, ref, piece):
        first = pl.multiple_of(piece * self.height, self.height)
        return ref.at[:, :, pl.ds(first, self.height)]

    def greet(self):
        self.barrier = pltpu.get_barrier_semaphore()
        blocks = [
            lax.rem(self.block - offset + self.blocks, self.blocks)
            for offset in range(1, self.reach + 1)
        ]
        targets = [(self.group, block) for block in blocks] + [(self.partner, self.block)]
        targets += [(self.far(step), self.block) for step in range(1, self.chips)]
        for target in targets:
            pl.semaphore_signal(self.barrier, inc=1, device_id=target, device_id_type=MESH)

    def enter(self):
        pl.semaphore_wait(self.barrier, self.reach + self.chips)

    def direct(self, offset):
        target = (self.group, lax.rem(self.block + offset, self.blocks))
        return (
            send(
                self.rows(self.masses, self.group),
                self.rows(self.held.at[offset], self.group),
                self.sends.at[offset, 0], self.recv.at[offset, self.group], target,
            ),
            send(
                self.spins, self.held_spins.at[offset],
                self.sends.at[offset, 1], self.recv.at[offset, self.groups], target,
            ),
        )

    def passed(self, offset, piece, target, sem):
        view = self.rows(self.held.at[offset], piece)
        return send(view, view, self.sends.at[offset, sem], self.recv.at[offset, piece],
                    (target, self.block))

    def to_core(self, offset):
        return self.passed(offset, self.group, self.partner, 2)

    def to_far(self, offset, step):
        return self.passed(offset, self.group, self.far(step), 1 + 2 * step)

    def relay(self, offset, step):
        return self.passed(offset, self.far(step), self.partner, 2 + 2 * step)

    def arrival(self, offset, piece):
        return self.passed(offset, piece, self.partner, 2)

    def begin(self):
        for offset in range(1, self.reach + 1):
            for copy in self.direct(offset):
                copy.start()

    def take(self, k):
        self.arrival(k, self.group).wait_recv()
        for step in range(1, self.chips):
            self.to_far(k, step).start()
        self.to_core(k).start()

    def turn(self, k):
        pl.when(k == 0)(lambda: self.take(1))
        pl.when(jnp.logical_and(k >= 1, k < self.reach))(lambda: self.take(k + 1))

        @pl.when(k >= 1)
        def _():
            for step in range(1, self.chips):
                self.arrival(k, self.far(step)).wait_recv()
                self.relay(k, step).start()
            self.arrival(k, self.partner).wait_recv()
            for step in range(1, self.chips):
                piece = lax.rem(self.chip + step, self.chips) * 2 + (1 - self.core)
                self.arrival(k, piece).wait_recv()
            self.direct(k)[1].wait_recv()

    def drain(self):
        for offset in range(1, self.reach + 1):
            for copy in self.direct(offset):
                copy.wait_send()
            self.to_core(offset).wait_send()
            for step in range(1, self.chips):
                self.to_far(offset, step).wait_send()
                self.relay(offset, step).wait_send()

def kernel(
    blocks, groups, reach, table_ref, masses_ref, spins_ref, ph_ref, pp_ref,
    sums, ph_keep, pp_keep, held, held_spins, steps, band, unit, skew, props, fixed,
    shift_ref, recv_sem, send_sem, local_sem,
):
    group = lax.axis_index("grp")
    block = lax.axis_index("blk")
    order = held.shape[-1]
    walkers = held.shape[1]
    trans = sums.shape[0]
    height = order // groups
    lanes = sums.shape[-1]
    f32, bf16 = jnp.float32, jnp.bfloat16
    gather = whole_gather(blocks, groups, reach)
    home = block if gather else 0

    local = [
        pltpu.make_async_copy(masses_ref, held.at[home], local_sem.at[0]),
        pltpu.make_async_copy(spins_ref, held_spins.at[home], local_sem.at[1]),
        pltpu.make_async_copy(ph_ref, ph_keep, local_sem.at[2]),
        pltpu.make_async_copy(pp_ref, pp_keep, local_sem.at[3]),
        pltpu.make_async_copy(table_ref, shift_ref, local_sem.at[4]),
    ]
    if gather:
        plan = Gather(
            group, block, order, walkers, masses_ref, spins_ref, held, held_spins,
            recv_sem, send_sem,
        )
    else:
        plan = Chain(
            group, block, groups, blocks, reach, height, masses_ref, spins_ref, held,
            held_spins, recv_sem, send_sem,
        )
    plan.greet()
    for copy in local:
        copy.start()
    plan.enter()
    plan.begin()

    norm = 1.0 / math.sqrt(NW * NK)
    row = lax.broadcasted_iota(jnp.int32, (NW, order), 0)
    column = lax.broadcasted_iota(jnp.int32, (NW, order), 1)
    slices, sites = column // NK, column % NK

    def circle(numerator):
        turn = angle(numerator % (2 * NW))
        return jnp.cos(turn), jnp.sin(turn)

    site_cos, site_sin = circle(2 * NW * NK - 2 * row * sites)
    odd_cos, odd_sin = circle((2 * row + 1) * slices)
    even_cos, even_sin = circle(2 * row * slices)
    for i in range(NW):
        here = slice(i * NK, (i + 1) * NK)
        c, d = odd_cos[i : i + 1], odd_sin[i : i + 1]
        cos, sin = c * site_cos - d * site_sin, d * site_cos + c * site_sin
        unit[0, here], unit[1, here] = cos, sin
        if i < NW // 2:
            steps[2 * i * NK : (2 * i + 1) * NK] = (cos * norm).astype(bf16)
            steps[(2 * i + 1) * NK : (2 * i + 2) * NK] = (sin * norm).astype(bf16)
        c, d = even_cos[i : i + 1], even_sin[i : i + 1]
        cos, sin = c * site_cos - d * site_sin, d * site_cos + c * site_sin
        for half in range(order // lanes):
            part = slice(half * lanes, (half + 1) * lanes)
            skew[half, here, 0:lanes] = (cos[:, part] * norm).astype(bf16)
            skew[half, here, lanes:] = (sin[:, part] * norm).astype(bf16)
    for i in range(height // NK):
        near = pl.ds(pl.multiple_of(group * height + i * NK, NK), NK)
        band[2 * i * NK : (2 * i + 1) * NK] = (unit[0, near] * norm).astype(bf16)
        band[(2 * i + 1) * NK : (2 * i + 2) * NK] = (unit[1, near] * norm).astype(bf16)
    sums[...] = jnp.zeros(sums.shape, f32)

    def dot(a, b):
        return jnp.dot(a, b, preferred_element_type=f32)

    flip = ROWS - 1 - lax.broadcasted_iota(jnp.int32, (ROWS, lanes), 0)

    def put(s, part, half, i, lower, upper):
        tiles = [lower[r : r + ROWS] for r in range(0, NK, ROWS)]
        for r, tile in enumerate(tiles + tiles[:1]):
            props[s, part, half, i, r * ROWS : (r + 1) * ROWS] = tile
        tiles = [upper[r : r + ROWS] for r in range(0, NK, ROWS)]
        tiles = [jnp.take_along_axis(tile, flip, 0) for tile in tiles[::-1]]
        for r, tile in enumerate(tiles + tiles[:1]):
            props[s, part, half, NW - 1 - i, r * ROWS : (r + 1) * ROWS] = tile

    def from_row(freq, mom):
        mirrored = lax.shift_right_logical(freq, HALF_BITS)
        return pl.ds((mom - mirrored + NK) & (NK - 1), ROWS)

    def absorb(slot, w):
        signed = (2 * held_spins[slot, w : w + 1, :] - 1).astype(f32)
        turned = []
        for s in range(2):
            factor = jnp.exp((COUPLING if s == 0 else -COUPLING) * signed)
            scaled = (held[slot, w, s].astype(f32) * factor).astype(bf16)
            first = dot(steps[...], scaled)
            for i in range(NW // 2):
                real, imag = first[2 * i * NK : (2 * i + 1) * NK], first[(2 * i + 1) * NK : (2 * i + 2) * NK]
                cos, sin = unit[0, i * NK : (i + 1) * NK], unit[1, i * NK : (i + 1) * NK]
                turned += [
                    (real * cos + imag * sin).astype(bf16),
                    (imag * cos - real * sin).astype(bf16),
                ]
            left = lax.dot_general(band[...], scaled, NT, preferred_element_type=f32)
            for i in range(height // NK):
                real, imag = left[2 * i * NK : (2 * i + 1) * NK], left[(2 * i + 1) * NK : (2 * i + 2) * NK]
                near = pl.ds(pl.multiple_of(group * height + i * NK, NK), NK)
                cos, sin = unit[0, near], unit[1, near]
                turned += [
                    (cos * real + sin * imag).astype(bf16),
                    (sin * real - cos * imag).astype(bf16),
                ]
        turned = jnp.concatenate(turned, 0)
        for half in range(order // lanes):
            moving = dot(turned, skew[half])
            first = 0
            for s in range(2):
                for i in range(NW // 2):
                    real, imag = moving[first : first + NK], moving[first + NK : first + 2 * NK]
                    first += 2 * NK
                    c, d, e, f = real[:, :lanes], real[:, lanes:], imag[:, :lanes], imag[:, lanes:]
                    put(s, 0, half, i, c + f, c - f)
                    put(s, 1, half, i, e - d, -e - d)
                for i in range(height // NK):
                    real, imag = moving[first : first + NK], moving[first + NK : first + 2 * NK]
                    first += 2 * NK
                    c, d, e, f = real[:, :lanes], real[:, lanes:], imag[:, :lanes], imag[:, lanes:]
                    fixed[s, 0, half, i * NK : (i + 1) * NK] = c - f
                    fixed[s, 1, half, i * NK : (i + 1) * NK] = -d - e

        @pl.loop(0, trans)
        def _(t):
            start = shift_ref[t, 0]
            freq, mom = lax.shift_right_logical(start, BITS), start & (NK - 1)
            for i in range(height // NK):
                at = group * (height // NK) + i
                up, down = (at + freq) & (NW - 1), (at - freq + NW) & (NW - 1)
                for piece in range(NK // ROWS):
                    rows = i * NK + piece * ROWS
                    place = slice(rows, rows + ROWS)
                    offset = piece * ROWS
                    ahead = from_row(up, mom + offset)
                    behind = from_row(down, NK - mom + offset)
                    own = from_row(at, offset)
                    for half in range(order // lanes):
                        real, imag = sums[t, 0, half, place], sums[t, 1, half, place]
                        for s in range(2):
                            a, b = fixed[s, 0, half, place], fixed[s, 1, half, place]
                            c, d = props[s, 0, half, up, ahead], props[s, 1, half, up, ahead]
                            real = real + (a * c + b * d)
                            imag = imag + (a * d - b * c)
                        sums[t, 0, half, place] = real
                        sums[t, 1, half, place] = imag
                        a, b = props[0, 0, half, at, own], props[0, 1, half, at, own]
                        c, d = props[1, 0, half, down, behind], props[1, 1, half, down, behind]
                        sums[t, 2, half, place] += a * c + b * d
                        sums[t, 3, half, place] += b * c - a * d

    @pl.loop(0, reach + 1)
    def _(k):
        @pl.when(k == 0)
        def _():
            local[0].wait()
            local[1].wait()
            local[4].wait()

        plan.turn(k)
        for w in range(walkers):
            absorb(plan.slot_at(k), w)

    local[2].wait()
    local[3].wait()
    plan.drain()


def leave(groups, sums, ph_keep, pp_keep, ph_out, pp_out, ph_new, pp_new, sem):
    trans, _, _, height, lanes = sums.shape
    group = lax.axis_index("grp")
    row = lax.broadcasted_iota(jnp.int32, (height, lanes), 0)
    lane = lax.broadcasted_iota(jnp.int32, (height, lanes), 1)
    freq = (lane // NK - group * (height // NK) - row // NK + 2 * NW) % NW
    mom = (lane % NK - row % NK + NK) % NK
    source = freq * NK + mom
    index, upper = source % lanes, source >= lanes
    for t in range(trans):
        for i, (keep, new, out) in enumerate(((ph_keep, ph_new, ph_out), (pp_keep, pp_new, pp_out))):
            for part in range(2):
                low, high = [
                    jnp.take_along_axis(sums[t, 2 * i + part, half], index, 1)
                    for half in range(2)
                ]
                new[part, t, :, 0:lanes] = keep[part, t, :, 0:lanes] + jnp.where(upper, high, low)
                new[part, t, :, lanes:] = keep[part, t, :, lanes:] + jnp.where(upper, low, high)
                pltpu.make_async_copy(new.at[part, t], out.at[part, t], sem.at[i]).start()
    for i, (new, out) in enumerate(((ph_new, ph_out), (pp_new, pp_out))):
        pltpu.make_async_copy(new, out, sem.at[i]).wait()


def on_device(masses, spins, shift_table, flip_table, ph_in, pp_in):
    groups = lax.axis_size("grp")
    blocks = lax.axis_size("blk")
    reach = min(8, blocks - 1)
    visits = reach + 1
    walkers, _, order, _ = masses.shape
    trans = shift_table.shape[0]
    height = order // groups
    chips = groups // 2
    f32, bf16 = jnp.float32, jnp.bfloat16
    sums_shape = (trans, 4, order // LANES, height, LANES)
    dma = pltpu.SemaphoreType.DMA
    anywhere = pl.BlockSpec(memory_space=pl.ANY)
    if whole_gather(blocks, groups, reach):
        recv_shape, send_shape = (visits, 3), (5,)
    else:
        recv_shape, send_shape = (visits, groups + 1), (visits, 3 + 2 * (chips - 1))
    sums = pl.pallas_call(
        functools.partial(kernel, blocks, groups, reach),
        out_shape=(
            pltpu.VMEM(sums_shape, f32),
            pltpu.VMEM(ph_in.shape, f32),
            pltpu.VMEM(pp_in.shape, f32),
        ),
        in_specs=[pl.BlockSpec(memory_space=pltpu.HBM)] * 5,
        out_specs=(pl.BlockSpec(memory_space=pltpu.VMEM),) * 3,
        scratch_shapes=[
            pltpu.VMEM((visits, walkers, 2, order, order), bf16),
            pltpu.VMEM((visits, walkers, order), jnp.int32),
            pltpu.VMEM((order, order), bf16),
            pltpu.VMEM((2 * height, order), bf16),
            pltpu.VMEM((2, order, order), f32),
            pltpu.VMEM((order // LANES, order, 2 * LANES), bf16),
            pltpu.VMEM((2, 2, order // LANES, NW, NK + ROWS, LANES), f32),
            pltpu.VMEM((2, 2, order // LANES, height, LANES), f32),
            pltpu.SMEM(shift_table.shape, jnp.int32),
            dma(recv_shape),
            dma(send_shape),
            dma((5,)),
        ],
        compiler_params=pltpu.CompilerParams(
            collective_id=0, has_side_effects=True, vmem_limit_bytes=VMEM - 8 * (ph_in.size + pp_in.size) - 65536
        ),
    )(shift_table, masses, spins, ph_in, pp_in)
    return pl.pallas_call(
        functools.partial(leave, groups),
        out_shape=(
            jax.ShapeDtypeStruct(ph_in.shape, f32),
            jax.ShapeDtypeStruct(pp_in.shape, f32),
        ),
        in_specs=[pl.BlockSpec(memory_space=pltpu.VMEM)] * 3,
        out_specs=(anywhere,) * 2,
        scratch_shapes=[
            pltpu.VMEM(ph_in.shape, f32),
            pltpu.VMEM(pp_in.shape, f32),
            dma((2,)),
        ],
        compiler_params=pltpu.CompilerParams(vmem_limit_bytes=16 * 1024 * 1024),
    )(*[pltpu.with_memory_space_constraint(one, pltpu.VMEM) for one in sums])


def solution(mesh):
    placed = (
        P("blk", None, None, None),
        P("blk", None),
        P("blk", None),
        P("blk", None),
        P(None, "blk", "grp", None),
        P(None, "blk", "grp", None),
    )
    return jax.shard_map(
        on_device,
        mesh=mesh,
        in_specs=placed,
        out_specs=(P(None, "blk", "grp", None), P(None, "blk", "grp", None)),
        check_vma=False,
    )
```
